32 devices in a mesh: narrow: 2 (over x), wide: 16 (over z, y, core).
Axes of the slice: x: 2, y: 2, z: 4, core: 2. Of those that a mesh axis runs over, the one named last changes fastest.
Arguments:
- inputs: bfloat16 [24576, 768], P('wide', 'narrow'), may hold values from -6 to 6
- block_segment: int32 [48], P('wide'), may hold values from 0 to 2, as said below
- query_weight: bfloat16 [768, 768], P('wide', 'narrow'), may hold values from -0.21875 to 0.21875
- key_weight: bfloat16 [768, 768], P('wide', 'narrow'), may hold values from -0.21875 to 0.21875
- value_weight: bfloat16 [768, 768], P('wide', 'narrow'), may hold values from -0.21875 to 0.21875
- output_weight: bfloat16 [768, 768], P('narrow', 'wide'), may hold values from -1.25 to 1.25
- inner_weight: bfloat16 [768, 3072], P('wide', 'narrow'), may hold values from -0.21875 to 0.21875
- outer_weight: bfloat16 [3072, 768], P('narrow', 'wide'), may hold values from -0.109375 to 0.109375
- first_gain: float32 [768], P('narrow'), may hold values from 0.5 to 1.5
- first_bias: float32 [768], P('narrow'), may hold values from -3 to 3
- second_gain: float32 [768], P('narrow'), may hold values from 0.5 to 1.5
- second_bias: float32 [768], P('narrow'), may hold values from -3 to 3
- output_cotangent: bfloat16 [24576, 768], P('wide', 'narrow'), may hold values from -6 to 6
Outputs:
- layer_output: bfloat16 [24576, 768], P('wide', 'narrow')
- input_gradient: bfloat16 [24576, 768], P('wide', 'narrow')
- query_gradient: float32 [768, 768], P('wide', 'narrow')
- key_gradient: float32 [768, 768], P('wide', 'narrow')
- value_gradient: float32 [768, 768], P('wide', 'narrow')
- output_gradient: float32 [768, 768], P('narrow', 'wide')
- inner_gradient: float32 [768, 3072], P('wide', 'narrow')
- outer_gradient: float32 [3072, 768], P('narrow', 'wide')
- first_gain_gradient: float32 [768], P(('narrow', 'wide'))
- first_bias_gradient: float32 [768], P(('narrow', 'wide'))
- second_gain_gradient: float32 [768], P(('narrow', 'wide'))
- second_bias_gradient: float32 [768], P(('narrow', 'wide'))
The draws below stay inside these ranges and needn't reach their ends.
Inputs may be any that keep to these rules, and one draw needn't show every extreme that they name: `block_segment`: entry b belongs to block b; every 3 consecutive entries form a group that lies on one index of wide; within a group the entries start at 0 and rise by 0 or 1 from block to block, so sequences hold 1 to 3 whole blocks.
All inputs are finite; a program needn't handle non-finite values.
Results may differ from the reference program's by a relative error of at most 0.017.
Values may be sent and summed in bfloat16 or wider, within the bound.
A program may use at most 256 MiB of HBM per device.

```python
import jax
import jax.numpy as jnp
from jax import lax

D = 768
HEADS = 12
HEAD_DIM = 64
FF = 3072
BLOCK = 512
SPAN = 3
TOKENS = 24576


def draw_block_segment(key, part):
    groups = TOKENS // (SPAN * BLOCK)
    table = jnp.array([[0, 0, 0], [0, 0, 1], [0, 1, 1], [0, 1, 2]], dtype=jnp.int32)
    kinds = jax.random.randint(jax.random.fold_in(key, 11), (groups,), 0, 4)
    order = jax.random.permutation(jax.random.fold_in(key, 12), groups)
    kinds = kinds.at[order[:4]].set(jnp.arange(4, dtype=jnp.int32))
    return table[kinds].reshape(-1)


def shard_levels(own_key, shape, shards, low, high):
    def one(position, blocks):
        draws = jax.random.uniform(jax.random.fold_in(jax.random.fold_in(own_key, 6), position), (blocks,), jnp.float32, low / len(shards), high / len(shards))
        return jnp.repeat(jnp.exp(draws), shape[position] // blocks).reshape((-1,) + (1,) * (len(shape) - position - 1))

    loudness = one(*shards[0])
    for cut in shards[1:]:
        loudness = loudness * one(*cut)
    return loudness


def bell_draw(own_key, shape, width, most, cuts=(), held_as=jnp.bfloat16):
    values = width * jax.random.normal(own_key, shape, jnp.float32)
    if cuts:
        values = values * shard_levels(own_key, shape, cuts, -0.22, 0.18)
    return jnp.clip(values, -most, most).astype(held_as)


def setup_inputs(seed: int = 0) -> dict:
    arg_keys = jax.random.split(jax.random.key(seed), 14)
    return {
        "inputs": bell_draw(arg_keys[0], (TOKENS, D), 1.0, 6.0, ((0, 16), (1, 2))),
        "block_segment": draw_block_segment(jax.random.fold_in(arg_keys[13], 71), 0),
        "query_weight": bell_draw(arg_keys[2], (D, D), D ** -0.5, 0.21875, ((0, 16), (1, 2))),
        "key_weight": bell_draw(arg_keys[3], (D, D), D ** -0.5, 0.21875, ((0, 16), (1, 2))),
        "value_weight": bell_draw(arg_keys[4], (D, D), D ** -0.5, 0.21875, ((0, 16), (1, 2))),
        "output_weight": bell_draw(arg_keys[5], (D, D), (D // 32) ** -0.5, 1.25, ((0, 2), (1, 16))),
        "inner_weight": bell_draw(arg_keys[6], (D, FF), D ** -0.5, 0.21875, ((0, 16), (1, 2))),
        "outer_weight": bell_draw(arg_keys[7], (FF, D), FF ** -0.5, 0.109375, ((0, 2), (1, 16))),
        "first_gain": jnp.clip(1.0 + 0.1 * jax.random.normal(arg_keys[8], (D,), jnp.float32), 0.5, 1.5),
        "first_bias": bell_draw(arg_keys[9], (D,), 0.5, 3.0, ((0, 2),), jnp.float32),
        "second_gain": jnp.clip(1.0 + 0.1 * jax.random.normal(arg_keys[10], (D,), jnp.float32), 0.5, 1.5),
        "second_bias": bell_draw(arg_keys[11], (D,), 0.5, 3.0, ((0, 2),), jnp.float32),
        "output_cotangent": bell_draw(arg_keys[12], (TOKENS, D), 1.0, 6.0, ((0, 16), (1, 2))),
    }


EPSILON = 1e-06
NEGATIVE = -1e+30
THETA = 10000.0
ROOT_HALF = 0.7071067811865476

@jax.custom_vjp
def low(v):
    return lax.optimization_barrier(v.astype(jnp.bfloat16)).astype(jnp.float32)

@jax.custom_vjp
def low_back(v):
    return v

def low_keep(v):
    return (low(v), None)

def low_pass(kept, grad):
    return (grad,)

def back_keep(v):
    return (v, None)

def back_low(kept, grad):
    return (low(grad),)
low.defvjp(low_keep, low_pass)
low_back.defvjp(back_keep, back_low)

def mult(left, right):
    return jnp.dot(left, right, preferred_element_type=jnp.float32, precision=lax.Precision.HIGHEST)

def norm(values, gain, bias):
    mean = lax.optimization_barrier(jnp.mean(values, axis=-1, keepdims=True))
    centred = values - mean
    variance = lax.optimization_barrier(jnp.mean(centred * centred, axis=-1, keepdims=True))
    return centred * lax.rsqrt(variance + EPSILON) * gain + bias

def gelu(values):
    return 0.5 * values * (1.0 + lax.erf(values * ROOT_HALF))

def rotate(values, cosine, sine):
    half = values.shape[-1] // 2
    first = values[..., :half]
    second = values[..., half:]
    return jnp.concatenate([first * cosine - second * sine, second * cosine + first * sine], axis=-1)

def tables(segment):
    earlier = lax.optimization_barrier(jnp.sum((segment[None, :] < segment[:, None]).astype(jnp.int32), axis=1))
    offsets = (jnp.arange(SPAN, dtype=jnp.int32) - earlier) * BLOCK
    positions = (offsets[:, None] + jnp.arange(BLOCK, dtype=jnp.int32)[None, :]).reshape(-1).astype(jnp.float32)
    half = HEAD_DIM // 2
    rates = THETA ** (-jnp.arange(half, dtype=jnp.float32) / half)
    angle = positions[:, None] * rates[None, :]
    labels = jnp.repeat(segment, BLOCK)
    same = labels[:, None] == labels[None, :]
    return (jnp.cos(angle)[:, None, :], jnp.sin(angle)[:, None, :], same)

def layer(rows, weights, cosine, sine, same):
    query_weight, key_weight, value_weight, output_weight, inner_weight, outer_weight, first_gain, first_bias, second_gain, second_bias = weights
    length = rows.shape[0]
    shape = (length, HEADS, HEAD_DIM)
    queries = low(rotate(low_back(mult(rows, query_weight)).reshape(shape), cosine, sine))
    keys = low(rotate(low_back(mult(rows, key_weight)).reshape(shape), cosine, sine))
    values = low(low_back(mult(rows, value_weight))).reshape(shape)
    scores = jnp.einsum('qhd,khd->hqk', queries, keys, precision=lax.Precision.HIGHEST)
    scores = low_back(scores * HEAD_DIM ** (-0.5))
    scores = jnp.where(same[None], scores, NEGATIVE)
    top = lax.optimization_barrier(jnp.max(scores, axis=-1, keepdims=True))
    raised = jnp.exp(scores - top)
    weights_soft = low(raised / lax.optimization_barrier(jnp.sum(raised, axis=-1, keepdims=True)))
    context = jnp.einsum('hqk,khd->qhd', weights_soft, values, precision=lax.Precision.HIGHEST).reshape(length, D)
    context = low(low_back(context))
    attended = low_back(mult(context, output_weight))
    first = norm(rows + attended, first_gain, first_bias)
    inner = low_back(mult(low(first), inner_weight))
    activated = low(gelu(inner))
    mixed = low_back(mult(activated, outer_weight))
    return norm(first + mixed, second_gain, second_bias)

def reference(inputs, block_segment, query_weight, key_weight, value_weight, output_weight, inner_weight, outer_weight, first_gain, first_bias, second_gain, second_bias, output_cotangent):
    groups = TOKENS // (SPAN * BLOCK)
    length = SPAN * BLOCK
    params = tuple((item.astype(jnp.float32) for item in (query_weight, key_weight, value_weight, output_weight, inner_weight, outer_weight, first_gain, first_bias, second_gain, second_bias)))
    rows_all = inputs.astype(jnp.float32).reshape(groups, length, D)
    cotangents = output_cotangent.astype(jnp.float32).reshape(groups, length, D)
    segments = block_segment.reshape(groups, SPAN)

    def step(carry, items):
        rows, cotangent, segment = items
        cosine, sine, same = tables(segment)

        def forward(rows_in, weights):
            return layer(rows_in, weights, cosine, sine, same)
        result, pullback = jax.vjp(forward, rows, params)
        grad_rows, grad_params = pullback(cotangent)
        carry = jax.tree.map(lambda left, right: left + right, carry, grad_params)
        return (carry, (result.astype(jnp.bfloat16), grad_rows.astype(jnp.bfloat16)))
    zeros = tuple((jnp.zeros(item.shape, jnp.float32) for item in params))
    grads, (results, grad_inputs) = lax.scan(step, zeros, (rows_all, cotangents, segments))
    return (results.reshape(TOKENS, D), grad_inputs.reshape(TOKENS, D), grads[0], grads[1], grads[2], grads[3], grads[4], grads[5], grads[6], grads[7], grads[8], grads[9])
```

```python
import functools

import jax
import jax.numpy as jnp
import numpy as np
from jax import lax
from jax.experimental import pallas as pl
from jax.experimental.pallas import tpu as pltpu
from jax.sharding import PartitionSpec as P

HEAD_DIM = 64
BLOCK = 512
SPAN = 3


EPSILON = 1e-06
NEGATIVE = -1e30
THETA = 10000.0
ROOT_HALF = 0.7071067811865476
INVERSE_ROOT = 0.3989422804014327


def product(left, right):
    return jnp.dot(left, right, preferred_element_type=jnp.float32)


def left_transposed(left, right):
    return lax.dot_general(
        left, right, (((0,), (0,)), ((), ())), preferred_element_type=jnp.float32
    )


def right_transposed(left, right):
    return lax.dot_general(
        left, right, (((1,), (1,)), ((), ())), preferred_element_type=jnp.float32
    )


def whole_features(values):
    return lax.all_gather(values, "narrow", axis=1, tiled=True)


def feature_sums(values):
    return lax.psum_scatter(
        values.astype(jnp.bfloat16), "narrow", scatter_dimension=1, tiled=True
    ).astype(jnp.float32)


def moments(first_sum, second_sum):
    return lax.psum((first_sum, second_sum), "narrow")


def gelu_value(values):
    return 0.5 * values * (1.0 + lax.erf(values * ROOT_HALF))


def gelu_slope(values):
    return (
        0.5 * (1.0 + lax.erf(values * ROOT_HALF))
        + values * jnp.exp(-0.5 * values * values) * INVERSE_ROOT
    )


def rotate(values, cosine, sine):
    half = values.shape[-1] // 2
    first = values[..., :half]
    second = values[..., half:]
    return jnp.concatenate(
        [first * cosine - second * sine, second * cosine + first * sine], axis=-1
    )


def rotate_back(values, cosine, sine):
    half = values.shape[-1] // 2
    first = values[..., :half]
    second = values[..., half:]
    return jnp.concatenate(
        [first * cosine + second * sine, second * cosine - first * sine], axis=-1
    )


def tables(block_segment):
    segment = block_segment.reshape(-1, SPAN)
    earlier = jnp.sum((segment[:, None, :] < segment[:, :, None]).astype(jnp.int32), axis=2)
    offsets = (jnp.arange(SPAN, dtype=jnp.int32)[None, :] - earlier) * BLOCK
    positions = (
        (offsets[:, :, None] + jnp.arange(BLOCK, dtype=jnp.int32)[None, None, :])
        .reshape(-1)
        .astype(jnp.float32)
    )
    half = HEAD_DIM // 2
    rates = THETA ** (-jnp.arange(half, dtype=jnp.float32) / half)
    angle = positions[:, None] * rates[None, :]
    labels = jnp.repeat(segment, BLOCK, axis=1)
    return (jnp.cos(angle)[:, None, :], jnp.sin(angle)[:, None, :], labels)


def normalize(summed, gain, bias, width):
    total, squares = moments(jnp.sum(summed, axis=1), jnp.sum(summed * summed, axis=1))
    mean = total / width
    reciprocal = lax.rsqrt(squares / width - mean * mean + EPSILON)
    normed = (summed - mean[:, None]) * reciprocal[:, None]
    return (normed * gain + bias, normed, reciprocal)


def normalize_back(grad, normed, reciprocal, gain, width):
    scaled = grad * gain
    total, cross = moments(jnp.sum(scaled, axis=1), jnp.sum(scaled * normed, axis=1))
    return reciprocal[:, None] * (scaled - total[:, None] / width - normed * cross[:, None] / width)


def block_scores(block_queries, group_keys, block_labels, group_labels, factor):
    scores = (
        jnp.einsum("qhd,khd->hqk", block_queries, group_keys, preferred_element_type=jnp.float32)
        * factor
    )
    same = block_labels[:, None] == group_labels[None, :]
    return jnp.where(same[None], scores, NEGATIVE)


def attention_forward(queries, keys, values, labels, factor):
    groups, length = labels.shape
    shape = (groups, length) + queries.shape[1:]

    def one_group(items):
        group_queries, group_keys, group_values, group_labels = items
        contexts = []
        totals = []
        for index in range(length // BLOCK):
            low_end = index * BLOCK
            high_end = low_end + BLOCK
            scores = block_scores(
                group_queries[low_end:high_end],
                group_keys,
                group_labels[low_end:high_end],
                group_labels,
                factor,
            )
            top = jnp.max(scores, axis=2, keepdims=True)
            raised = jnp.exp(scores - top)
            summed = jnp.sum(raised, axis=2, keepdims=True)
            soft = (raised / summed).astype(jnp.bfloat16)
            contexts.append(
                jnp.einsum("hqk,khd->qhd", soft, group_values, preferred_element_type=jnp.float32)
            )
            totals.append((top + jnp.log(summed))[..., 0])
        return (jnp.concatenate(contexts, axis=0), jnp.concatenate(totals, axis=1))

    contexts, totals = lax.map(
        one_group, (queries.reshape(shape), keys.reshape(shape), values.reshape(shape), labels)
    )
    return (contexts.reshape(queries.shape), totals)


def attention_backward(queries, keys, values, totals, grad_context, labels, factor):
    groups, length = labels.shape
    shape = (groups, length) + queries.shape[1:]

    def one_group(items):
        group_queries, group_keys, group_values, group_totals, group_grads, group_labels = items
        keys_grad = jnp.zeros(group_keys.shape, jnp.float32)
        values_grad = jnp.zeros(group_values.shape, jnp.float32)
        pieces = []
        for index in range(length // BLOCK):
            low_end = index * BLOCK
            high_end = low_end + BLOCK
            block_queries = group_queries[low_end:high_end]
            block_grads = group_grads[low_end:high_end]
            scores = block_scores(
                block_queries, group_keys, group_labels[low_end:high_end], group_labels, factor
            )
            soft = jnp.exp(scores - group_totals[:, low_end:high_end, None])
            inner = jnp.einsum(
                "qhd,khd->hqk", block_grads, group_values, preferred_element_type=jnp.float32
            )
            centre = jnp.sum(soft * inner, axis=2, keepdims=True)
            scores_grad = (soft * (inner - centre)).astype(jnp.bfloat16)
            pieces.append(
                jnp.einsum(
                    "hqk,khd->qhd", scores_grad, group_keys, preferred_element_type=jnp.float32
                )
                * factor
            )
            keys_grad = (
                keys_grad
                + jnp.einsum(
                    "hqk,qhd->khd", scores_grad, block_queries, preferred_element_type=jnp.float32
                )
                * factor
            )
            values_grad = values_grad + jnp.einsum(
                "hqk,qhd->khd",
                soft.astype(jnp.bfloat16),
                block_grads,
                preferred_element_type=jnp.float32,
            )
        return (jnp.concatenate(pieces, axis=0), keys_grad, values_grad)

    queries_grad, keys_grad, values_grad = lax.map(
        one_group,
        (
            queries.reshape(shape),
            keys.reshape(shape),
            values.reshape(shape),
            totals,
            grad_context.reshape(shape),
            labels,
        ),
    )
    return (
        queries_grad.reshape(queries.shape),
        keys_grad.reshape(queries.shape),
        values_grad.reshape(queries.shape),
    )


def shards(
    inputs,
    block_segment,
    query_weight,
    key_weight,
    value_weight,
    output_weight,
    inner_weight,
    outer_weight,
    first_gain,
    first_bias,
    second_gain,
    second_bias,
    output_cotangent,
):
    width = first_gain.shape[0] * lax.axis_size("narrow")
    tokens = inputs.shape[0]
    factor = HEAD_DIM ** (-0.5)
    cosine, sine, labels = tables(block_segment)
    full_inputs = whole_features(inputs)
    query_full, key_full, value_full, inner_full = (
        lax.all_gather(query_weight, "wide", axis=0, tiled=True),
        lax.all_gather(key_weight, "wide", axis=0, tiled=True),
        lax.all_gather(value_weight, "wide", axis=0, tiled=True),
        lax.all_gather(inner_weight, "wide", axis=0, tiled=True),
    )
    output_full, outer_full = (
        lax.all_gather(output_weight, "wide", axis=1, tiled=True),
        lax.all_gather(outer_weight, "wide", axis=1, tiled=True),
    )
    head_shape = (tokens, query_weight.shape[1] // HEAD_DIM, HEAD_DIM)
    queries = rotate(product(full_inputs, query_full).reshape(head_shape), cosine, sine).astype(
        jnp.bfloat16
    )
    keys = rotate(product(full_inputs, key_full).reshape(head_shape), cosine, sine).astype(
        jnp.bfloat16
    )
    values = product(full_inputs, value_full).astype(jnp.bfloat16).reshape(head_shape)
    context, totals = attention_forward(queries, keys, values, labels, factor)
    context_low = context.reshape(tokens, -1).astype(jnp.bfloat16)
    attended = feature_sums(product(context_low, output_full))
    first, first_normed, first_scale = normalize(
        inputs.astype(jnp.float32) + attended, first_gain, first_bias, width
    )
    first_low = first.astype(jnp.bfloat16)
    feed_rows = whole_features(first_low)
    inner = product(feed_rows, inner_full)
    activated = gelu_value(inner).astype(jnp.bfloat16)
    mixed = feature_sums(product(activated, outer_full))
    second, second_normed, second_scale = normalize(first + mixed, second_gain, second_bias, width)
    layer_output = second.astype(jnp.bfloat16)
    cotangent = output_cotangent.astype(jnp.float32)
    second_gain_grad = jnp.sum(cotangent * second_normed, axis=0)
    second_bias_grad = jnp.sum(cotangent, axis=0)
    grad_second = normalize_back(cotangent, second_normed, second_scale, second_gain, width)
    grad_mixed = grad_second.astype(jnp.bfloat16)
    grad_rows = whole_features(grad_mixed)
    grad_activated = right_transposed(grad_rows, outer_full)
    outer_grad = left_transposed(activated, grad_rows)
    grad_inner = (grad_activated * gelu_slope(inner)).astype(jnp.bfloat16)
    inner_grad = left_transposed(feed_rows, grad_inner)
    grad_first = grad_second + feature_sums(right_transposed(grad_inner, inner_full))
    first_gain_grad = jnp.sum(grad_first * first_normed, axis=0)
    first_bias_grad = jnp.sum(grad_first, axis=0)
    grad_first_sum = normalize_back(grad_first, first_normed, first_scale, first_gain, width)
    attended_rows = whole_features(grad_first_sum.astype(jnp.bfloat16))
    output_grad = left_transposed(context_low, attended_rows)
    grad_context = right_transposed(attended_rows, output_full).astype(jnp.bfloat16)
    queries_grad, keys_grad, values_grad = attention_backward(
        queries, keys, values, totals, grad_context.reshape(head_shape), labels, factor
    )
    queries_grad = rotate_back(queries_grad, cosine, sine).reshape(tokens, -1).astype(jnp.bfloat16)
    keys_grad = rotate_back(keys_grad, cosine, sine).reshape(tokens, -1).astype(jnp.bfloat16)
    values_grad = values_grad.reshape(tokens, -1).astype(jnp.bfloat16)
    query_grad = left_transposed(full_inputs, queries_grad)
    key_grad = left_transposed(full_inputs, keys_grad)
    value_grad = left_transposed(full_inputs, values_grad)
    spread = (
        right_transposed(queries_grad, query_full)
        + right_transposed(keys_grad, key_full)
        + right_transposed(values_grad, value_full)
    )
    input_gradient = (grad_first_sum + feature_sums(spread)).astype(jnp.bfloat16)
    (
        query_total,
        key_total,
        value_total,
        inner_total,
        first_gain_total,
        first_bias_total,
        second_gain_total,
        second_bias_total,
    ) = (
        lax.psum_scatter(query_grad, "wide", scatter_dimension=0, tiled=True),
        lax.psum_scatter(key_grad, "wide", scatter_dimension=0, tiled=True),
        lax.psum_scatter(value_grad, "wide", scatter_dimension=0, tiled=True),
        lax.psum_scatter(inner_grad, "wide", scatter_dimension=0, tiled=True),
        lax.psum_scatter(first_gain_grad, "wide", scatter_dimension=0, tiled=True),
        lax.psum_scatter(first_bias_grad, "wide", scatter_dimension=0, tiled=True),
        lax.psum_scatter(second_gain_grad, "wide", scatter_dimension=0, tiled=True),
        lax.psum_scatter(second_bias_grad, "wide", scatter_dimension=0, tiled=True),
    )
    output_total, outer_total = (
        lax.psum_scatter(output_grad, "wide", scatter_dimension=1, tiled=True),
        lax.psum_scatter(outer_grad, "wide", scatter_dimension=1, tiled=True),
    )
    return (
        layer_output,
        input_gradient,
        query_total,
        key_total,
        value_total,
        output_total,
        inner_total,
        outer_total,
        first_gain_total,
        first_bias_total,
        second_gain_total,
        second_bias_total,
    )


LOW = jnp.bfloat16
WIDE = jnp.float32
MESH = pl.DeviceIdType.MESH
MEGA = 1 << 20
ANY = pl.BlockSpec(memory_space=pl.ANY)


def contract(left, right, left_dim, right_dim):
    return lax.dot_general(
        left, right, (((left_dim,), (right_dim,)), ((), ())), preferred_element_type=WIDE
    )


def place():
    x = lax.axis_index("narrow")
    w = lax.axis_index("wide")
    c = lax.rem(w, 2)
    y = lax.rem(lax.div(w, 2), 2)
    q = lax.div(w, 4)
    return x, w, c, y, q


class Links:
    def __init__(self, depth):
        self.depth = depth
        self.x, self.w, self.c, self.y, self.q = place()
        self.across = (1 - self.x, self.w)
        self.beside = (self.x, self.w + 2 - 4 * self.y)
        self.sibling = (self.x, self.w + 1 - 2 * self.c)
        self.corner = (1 - self.x, self.w + 1 - 2 * self.c)

    def far(self, step):
        return (self.x, lax.rem(self.w + 4 * step, 4 * self.depth))

    def row(self, step):
        return lax.rem(self.q + self.depth - step, self.depth)

    def meet(self):
        barrier = pltpu.get_barrier_semaphore()
        others = [self.across, self.beside, self.sibling, self.corner]
        others += [self.far(step) for step in range(1, self.depth)]
        for other in others:
            pl.semaphore_signal(barrier, 1, device_id=other, device_id_type=MESH)
        pl.semaphore_wait(barrier, len(others))


def remote(source, target, send, recv, device):
    return pltpu.make_async_remote_copy(
        src_ref=source,
        dst_ref=target,
        send_sem=send,
        recv_sem=recv,
        device_id=device,
        device_id_type=MESH,
    )


def gather_marks(depth):
    return 5 * depth + 2


class Gather:
    def __init__(self, links, own, full, cut, whole, send, recv, index, local):
        self.links, self.own, self.full, self.cut = links, own, full, cut
        self.whole, self.local = whole, local
        self.send = lambda k: send.at[index, k]
        self.recv = lambda k: recv.at[index, k]
        self.sent = []
        self.width = own.shape[-1]

    def slot(self, h, q, y):
        return self.full.at[h, q, y, self.links.c]

    def go(self, source, mark, device):
        copy = remote(source, source, self.send(mark), self.recv(mark), device)
        copy.start()
        self.sent.append(copy)

    def arrived(self, target, mark):
        remote(target, target, self.send(mark), self.recv(mark), self.links.sibling).wait_recv()

    def begin(self):
        n, d = self.links, self.links.depth
        mine = self.slot(n.x, n.q, n.y)
        for step in range(1, d):
            copy = remote(self.own, mine, self.send(step - 1), self.recv(step - 1), n.far(step))
            copy.start()
            self.sent.append(copy)
        for mark, device in ((d, n.across), (2 * d, n.beside)):
            copy = remote(self.own, mine, self.send(mark), self.recv(mark), device)
            copy.start()
            self.sent.append(copy)
        self.keep = pltpu.make_async_copy(self.own, mine, self.local)
        self.keep.start()

    def second(self, step):
        n, d = self.links, self.links.depth
        got = self.slot(n.x, n.row(step), n.y)
        self.arrived(got, step - 1)
        self.go(got, d + step, n.across)
        self.go(got, 2 * d + step, n.beside)

    def third(self, step):
        n, d = self.links, self.links.depth
        got = self.slot(1 - n.x, n.row(step), n.y)
        self.arrived(got, d + step)
        part = got.at[:, pl.ds(self.cut, self.width - self.cut)]
        self.go(part, 3 * d + step, n.beside)
        got = self.slot(n.x, n.row(step), 1 - n.y)
        self.arrived(got, 2 * d + step)
        part = got.at[:, pl.ds(0, self.cut)]
        self.go(part, 4 * d + step, n.across)

    def fourth(self):
        n, d = self.links, self.links.depth
        for step in range(d):
            got = self.slot(1 - n.x, n.row(step), 1 - n.y)
            self.arrived(got.at[:, pl.ds(self.cut, self.width - self.cut)], 3 * d + step)
            self.arrived(got.at[:, pl.ds(0, self.cut)], 4 * d + step)
        self.keep.wait()
        if self.whole:
            for h in range(2):
                self.go(self.full.at[h, :, :, n.c], 5 * d + h, n.sibling)
        else:
            self.go(self.full.at[1 - n.c, :, :, n.c], 5 * d, n.sibling)

    def finish(self):
        n, d = self.links, self.links.depth
        if self.whole:
            for h in range(2):
                self.arrived(self.full.at[h, :, :, 1 - n.c], 5 * d + h)
        else:
            self.arrived(self.full.at[n.c, :, :, 1 - n.c], 5 * d)

    def close(self):
        for copy in self.sent:
            copy.wait_send()


def gather_kernel(depth, cuts, meta_in, cot_in, in_ref, q_own, m_own, o_own,
                  meta, cot, rows, q_full, m_full, o_full, send, recv, local, extra_send, extra_recv):
    n = Links(depth)
    n.meet()
    half = in_ref.shape[0] // 2
    home = n.x == n.c
    gathers = [
        Gather(n, own, full, cut, whole, send, recv, k, local.at[k])
        for k, (own, full, cut, whole) in enumerate(
            zip((q_own, m_own, o_own), (q_full, m_full, o_full), cuts, (False, True, True))
        )
    ]
    es = lambda k: extra_send.at[k]
    er = lambda k: extra_recv.at[k]

    @pl.when(jnp.logical_not(home))
    def _():
        remote(in_ref, rows.at[n.x], es(0), er(0), n.across).start()

    gathers[0].begin()

    @pl.when(home)
    def _():
        keep = pltpu.make_async_copy(in_ref, rows.at[n.x], local.at[3])
        keep.start()
        first = remote(in_ref, rows.at[n.x], es(1), er(1), n.sibling)
        first.start()
        note = remote(meta_in, meta, es(3), er(3), n.sibling)
        note.start()
        own = pltpu.make_async_copy(meta_in, meta, local.at[4])
        own.start()
        mine = pltpu.make_async_copy(cot_in.at[pl.ds(n.c * half, half)], cot.at[n.x], local.at[5])
        mine.start()
        theirs = remote(
            cot_in.at[pl.ds((1 - n.c) * half, half)], cot.at[n.x], es(4), er(4), n.sibling
        )
        theirs.start()
        remote(in_ref, rows.at[1 - n.x], es(0), er(0), n.across).wait_recv()
        second = remote(rows.at[1 - n.x], rows.at[1 - n.x], es(2), er(2), n.sibling)
        second.start()
        keep.wait()
        own.wait()
        mine.wait()
        first.wait_send()
        note.wait_send()
        theirs.wait_send()
        second.wait_send()

    @pl.when(jnp.logical_not(home))
    def _():
        remote(in_ref, rows.at[n.x], es(0), er(0), n.across).wait_send()
        one = remote(
            cot_in.at[pl.ds((1 - n.c) * half, half)], cot.at[n.x], es(6), er(6), n.corner
        )
        two = remote(cot_in.at[pl.ds(n.c * half, half)], cot.at[n.x], es(5), er(5), n.across)
        one.start()
        two.start()
        remote(in_ref, rows.at[n.x], es(1), er(1), n.sibling).wait_recv()
        remote(in_ref, rows.at[1 - n.x], es(2), er(2), n.sibling).wait_recv()
        remote(meta_in, meta, es(3), er(3), n.sibling).wait_recv()
        remote(cot_in.at[pl.ds(0, half)], cot.at[n.x], es(4), er(4), n.sibling).wait_recv()
        one.wait_send()
        two.wait_send()

    for k in (0, 1, 2):
        if k:
            gathers[k].begin()
        for step in range(1, depth):
            gathers[k].second(step)
        for step in range(depth):
            gathers[k].third(step)
        gathers[k].fourth()

    @pl.when(home)
    def _():
        remote(cot_in.at[pl.ds(0, half)], cot.at[1 - n.x], es(5), er(5), n.across).wait_recv()

    @pl.when(jnp.logical_not(home))
    def _():
        remote(cot_in.at[pl.ds(0, half)], cot.at[1 - n.x], es(6), er(6), n.corner).wait_recv()

    for k in (0, 1, 2):
        gathers[k].finish()
        gathers[k].close()


def gather_call(depth, cuts, meta, cot, rows, q_own, m_own, o_own):
    r = q_own.shape[0]
    shapes = [jax.ShapeDtypeStruct((2, depth, 2, 2) + own.shape, LOW) for own in (q_own, m_own, o_own)]
    return pl.pallas_call(
        functools.partial(gather_kernel, depth, cuts),
        out_shape=[
            jax.ShapeDtypeStruct(meta.shape, meta.dtype),
            jax.ShapeDtypeStruct((2, cot.shape[0] // 2, cot.shape[1]), LOW),
            jax.ShapeDtypeStruct((2,) + rows.shape, LOW),
        ]
        + shapes,
        in_specs=[ANY] * 6,
        out_specs=[ANY] * 6,
        scratch_shapes=[
            pltpu.SemaphoreType.DMA((3, gather_marks(depth))),
            pltpu.SemaphoreType.DMA((3, gather_marks(depth))),
            pltpu.SemaphoreType.DMA((6,)),
            pltpu.SemaphoreType.DMA((7,)),
            pltpu.SemaphoreType.DMA((7,)),
        ],
        compiler_params=pltpu.CompilerParams(collective_id=0, has_side_effects=True),
        name="gather",
    )(meta, cot, rows, q_own, m_own, o_own)


def plus(left, right):
    return (left.astype(WIDE) + right.astype(WIDE)).astype(LOW)


def scatter_marks(depth):
    return depth + 5


class Scatter:
    def __init__(self, links, part, cut, whole, bufs, out, send, recv, index, local):
        self.links, self.part, self.cut, self.whole, self.out = links, part, cut, whole, out
        self.held, self.other, self.x1, self.y1, self.x2, self.y2, self.z = bufs
        self.send = lambda k: send.at[index, k]
        self.recv = lambda k: recv.at[index, k]
        self.local = local
        self.sent = []
        self.rest = part.shape[-1] - cut

    def go(self, source, target, mark, device):
        copy = remote(source, target, self.send(mark), self.recv(mark), device)
        copy.start()
        self.sent.append(copy)

    def arrived(self, target, mark):
        remote(target, target, self.send(mark), self.recv(mark), self.links.sibling).wait_recv()

    def begin(self):
        n = self.links
        if self.whole:
            self.go(self.part.at[:, :, :, 1 - n.c], self.other, 0, n.sibling)
            self.keep = pltpu.make_async_copy(self.part.at[:, :, :, n.c], self.held, self.local)
        else:
            self.go(self.part.at[:, :, 1 - n.c], self.held.at[n.c], 0, n.sibling)
            self.keep = pltpu.make_async_copy(
                self.part.at[:, :, n.c], self.held.at[n.c], self.local
            )
        self.keep.start()

    def join(self, h, y):
        for q in range(self.links.depth):
            self.held[h, q, y] = plus(self.held[h, q, y], self.other[h, q, y])

    def first(self):
        n = self.links
        self.keep.wait()
        if self.whole:
            self.arrived(self.other, 0)
            self.join(1 - n.x, 1 - n.y)
        else:
            self.arrived(self.held.at[1 - n.c], 0)
        corner = self.held.at[1 - n.x, :, 1 - n.y]
        self.go(corner.at[:, :, pl.ds(0, self.cut)], self.x1, 1, n.across)
        self.go(corner.at[:, :, pl.ds(self.cut, self.rest)], self.y1, 2, n.beside)
        if self.whole:
            self.join(n.x, 1 - n.y)
            self.join(1 - n.x, n.y)
            self.join(n.x, n.y)

    def second(self):
        n = self.links
        low, high = pl.ds(0, self.cut), pl.ds(self.cut, self.rest)
        self.arrived(self.x1, 1)
        for q in range(n.depth):
            self.held[n.x, q, 1 - n.y, :, low] = plus(
                self.held[n.x, q, 1 - n.y, :, low], self.x1[q]
            )
        self.go(self.held.at[n.x, :, 1 - n.y], self.y2, 3, n.beside)
        self.arrived(self.y1, 2)
        for q in range(n.depth):
            self.held[1 - n.x, q, n.y, :, high] = plus(
                self.held[1 - n.x, q, n.y, :, high], self.y1[q]
            )
        self.go(self.held.at[1 - n.x, :, n.y], self.x2, 4, n.across)

    def third(self):
        n = self.links
        self.arrived(self.y2, 3)
        self.arrived(self.x2, 4)
        for step in range(1, n.depth):
            q = lax.rem(n.q + step, n.depth)
            self.held[n.x, q, n.y] = plus(
                plus(self.held[n.x, q, n.y], self.x2[q]), self.y2[q]
            )
            self.go(self.held.at[n.x, q, n.y], self.z.at[step - 1], 4 + step, n.far(step))

    def fourth(self):
        n = self.links
        total = (
            self.held[n.x, n.q, n.y].astype(WIDE)
            + self.x2[n.q].astype(WIDE)
            + self.y2[n.q].astype(WIDE)
        )
        for step in range(1, n.depth):
            self.arrived(self.z.at[step - 1], 4 + step)
            total = total + self.z[step - 1].astype(WIDE)
        self.out[...] = total

    def close(self):
        for copy in self.sent:
            copy.wait_send()


def scatter_scratch(depth, r, columns, cut):
    return [
        pltpu.VMEM((2, depth, 2, r, columns), LOW),
        pltpu.VMEM((2, depth, 2, r, columns), LOW),
        pltpu.VMEM((depth, r, cut), LOW),
        pltpu.VMEM((depth, r, columns - cut), LOW),
        pltpu.VMEM((depth, r, columns), LOW),
        pltpu.VMEM((depth, r, columns), LOW),
        pltpu.VMEM((depth - 1, r, columns), LOW),
    ]


class HandOver:
    def __init__(self, links, source, target, send, recv, base, local):
        self.links, self.source, self.target, self.local = links, source, target, local
        self.send = lambda k: send.at[base + k]
        self.recv = lambda k: recv.at[base + k]
        self.half = source.shape[1]

    def rows(self, c):
        return self.target.at[pl.ds(c * self.half, self.half)]

    def copies(self):
        n = self.links
        near, far = self.source.at[n.x], self.source.at[1 - n.x]
        mine = self.rows(n.c)
        return (
            pltpu.make_async_copy(near, mine, self.local),
            remote(far, mine, self.send(0), self.recv(0), n.across),
            remote(near, mine, self.send(1), self.recv(1), n.sibling),
            remote(far, mine, self.send(2), self.recv(2), n.corner),
        )

    def begin(self):
        n = self.links
        keep, across, sibling, corner = self.copies()

        @pl.when(n.x == n.c)
        def _():
            keep.start()
            across.start()

        @pl.when(n.x != n.c)
        def _():
            sibling.start()
            corner.start()

    def finish(self):
        n = self.links
        keep, across, sibling, corner = self.copies()
        mine, theirs = self.rows(n.c), self.rows(1 - n.c)

        @pl.when(n.x == n.c)
        def _():
            keep.wait()
            across.wait_send()
            remote(theirs, theirs, self.send(1), self.recv(1), n.sibling).wait_recv()

        @pl.when(n.x != n.c)
        def _():
            sibling.wait_send()
            corner.wait_send()
            remote(mine, mine, self.send(0), self.recv(0), n.across).wait_recv()
            remote(theirs, theirs, self.send(2), self.recv(2), n.corner).wait_recv()


def scatter_kernel(depth, cuts, lo_in, dx_in, o_part, m_part, q_part,
                   lo_out, dx_out, o_out, m_out, q_out, *scratch):
    bufs = [scratch[7 * k : 7 * k + 7] for k in range(3)]
    dx_own, dx_other, send, recv, local, extra_send, extra_recv = scratch[21:]
    n = Links(depth)
    n.meet()
    spread_out = remote(
        dx_in.at[1 - n.c], dx_other, extra_send.at[6], extra_recv.at[6], n.sibling
    )
    spread_out.start()
    spread_own = pltpu.make_async_copy(dx_in.at[n.c], dx_own, local.at[3])
    spread_own.start()
    scatters = [
        Scatter(n, part, cut, whole, buf, out, send, recv, k, local.at[k])
        for k, (part, out, cut, whole, buf) in enumerate(
            zip(
                (o_part, m_part, q_part), (o_out, m_out, q_out), cuts, (True, True, False), bufs
            )
        )
    ]
    for item in scatters:
        item.begin()
    spread_own.wait()
    spread_out.wait_recv()
    for h in range(2):
        dx_own[h] = plus(dx_own[h], dx_other[h])
    lo_over = HandOver(n, lo_in, lo_out, extra_send, extra_recv, 0, local.at[4])
    dx_over = HandOver(n, dx_own, dx_out, extra_send, extra_recv, 3, local.at[5])
    dx_over.begin()
    lo_over.begin()
    for item in scatters:
        item.first()
    for item in scatters:
        item.second()
    for item in scatters:
        item.third()
    for item in scatters:
        item.fourth()
    for item in scatters:
        item.close()
    spread_out.wait_send()
    lo_over.finish()
    dx_over.finish()


def scatter_call(depth, cuts, lo, dx, o_part, m_part, q_part):
    r = o_part.shape[-2]
    half, part = lo.shape[1:]
    widths = [item.shape[-1] for item in (o_part, m_part, q_part)]
    scratch = []
    for columns, cut in zip(widths, cuts):
        scratch += scatter_scratch(depth, r, columns, cut)
    vmem = pl.BlockSpec(memory_space=pltpu.VMEM)
    return pl.pallas_call(
        functools.partial(scatter_kernel, depth, cuts),
        out_shape=[jax.ShapeDtypeStruct((2 * half, part), LOW)] * 2
        + [jax.ShapeDtypeStruct((r, columns), WIDE) for columns in widths],
        in_specs=[ANY] * 5,
        out_specs=[ANY] * 2 + [vmem] * 3,
        scratch_shapes=scratch
        + [
            pltpu.VMEM((2, half, part), LOW),
            pltpu.VMEM((2, half, part), LOW),
            pltpu.SemaphoreType.DMA((3, scatter_marks(depth))),
            pltpu.SemaphoreType.DMA((3, scatter_marks(depth))),
            pltpu.SemaphoreType.DMA((6,)),
            pltpu.SemaphoreType.DMA((7,)),
            pltpu.SemaphoreType.DMA((7,)),
        ],
        compiler_params=pltpu.CompilerParams(
            collective_id=1, has_side_effects=True, vmem_limit_bytes=56 * MEGA
        ),
        name="scatter",
    )(lo, dx, o_part, m_part, q_part)


def angle_tables():
    rates = THETA ** (-np.arange(HEAD_DIM // 2) / (HEAD_DIM // 2))
    rates = np.tile(rates, 4)[None]
    base = np.arange(BLOCK)[:, None] * rates
    jump = np.arange(SPAN)[:, None] * BLOCK * rates
    base = np.concatenate([np.cos(base), np.sin(base)], axis=0)
    jump = np.concatenate([np.cos(jump), np.sin(jump), np.zeros((2, 128))], axis=0)
    return jnp.asarray(base, WIDE), jnp.asarray(jump, WIDE)


def lanes(rows):
    return lax.broadcasted_iota(jnp.int32, (rows, 128), 1)


def turn_parts(meta, base, jump, block):
    offset = meta[0, SPAN + block]
    far_cos = jump[pl.ds(offset, 1), :]
    far_sin = jump[pl.ds(SPAN + offset, 1), :]
    near_cos, near_sin = base[0:BLOCK], base[BLOCK : 2 * BLOCK]
    cosine = near_cos * far_cos - near_sin * far_sin
    sine = near_sin * far_cos + near_cos * far_sin
    low = (lanes(BLOCK) % HEAD_DIM) < HEAD_DIM // 2
    return cosine, jnp.where(low, -sine, sine), low


def turn(values, cosine, sine, low):
    swapped = jnp.where(low, pltpu.roll(values, 96, 1), pltpu.roll(values, 32, 1))
    return values * cosine + swapped * sine


def forward_kernel(meta, rows, weight, base, jump, q_ref, k_ref, v_ref, p_ref, r_ref, c_ref, marks):
    step = pl.program_id(0)
    scale = HEAD_DIM ** (-0.5)

    @pl.when(step < SPAN)
    def _():
        here = pl.ds(step * BLOCK, BLOCK)
        cosine, sine, low = turn_parts(meta, base, jump, step)
        values = jnp.concatenate([rows[0, here], rows[1, here]], axis=1)
        for p in range(3):
            made = contract(values, weight[:, p * 384 : p * 384 + 384], 1, 0)
            q_ref[p, here] = (turn(made[:, 0:128], cosine, sine, low) * scale).astype(LOW)
            k_ref[p, here] = turn(made[:, 128:256], cosine, sine, low).astype(LOW)
            v_ref[p, here] = made[:, 256:384].astype(LOW)
        marks[here] = (lanes(BLOCK) == meta[0, step]).astype(WIDE).astype(LOW)

    @pl.when(step >= SPAN)
    def _():
        turn_number = step - SPAN
        p = turn_number // SPAN
        i = turn_number % SPAN
        here = pl.ds(i * BLOCK, BLOCK)
        lane = lanes(BLOCK)
        queries = q_ref[p, here]
        values = v_ref[p]
        keys = jnp.concatenate([k_ref[p], marks[...]], axis=1)
        barred = jnp.where((lane < SPAN) & (lane != meta[0, i]), NEGATIVE, 0.0).astype(LOW)
        outs = []
        scales = []
        for head in range(2):
            chosen = (lane // HEAD_DIM) == head
            ours = jnp.concatenate([jnp.where(chosen, queries, 0).astype(LOW), barred], axis=1)
            scores = contract(ours, keys, 1, 1)
            top = jnp.max(scores, axis=1, keepdims=True)
            raised = jnp.exp(scores - top)
            inverse = 1.0 / jnp.sum(raised, axis=1, keepdims=True)
            soft = raised.astype(LOW)
            p_ref[0, head] = soft
            outs.append(contract(soft, values, 1, 0))
            scales.append(inverse)
        inverse = jnp.where(lane < HEAD_DIM, scales[0], scales[1])
        r_ref[p, here] = inverse
        c_ref[p, here] = (jnp.where(lane < HEAD_DIM, outs[0], outs[1]) * inverse).astype(LOW)


def forward_call(meta, rows, weight, base, jump):
    length = rows.shape[1]
    trio = jax.ShapeDtypeStruct((3, length, 128), LOW)
    vmem = pl.BlockSpec(memory_space=pltpu.VMEM)
    soft_shape = (SPAN * 3, 2, BLOCK, length)
    return pl.pallas_call(
        forward_kernel,
        grid=(SPAN + 3 * SPAN,),
        out_shape=[
            trio,
            trio,
            trio,
            jax.ShapeDtypeStruct(soft_shape, LOW),
            jax.ShapeDtypeStruct((3, length, 128), WIDE),
            trio,
        ],
        in_specs=[pl.BlockSpec(memory_space=pltpu.SMEM)] + [vmem] * 4,
        out_specs=[
            vmem,
            vmem,
            vmem,
            pl.BlockSpec((1, 2, BLOCK, length), lambda s: (jnp.maximum(s - SPAN, 0), 0, 0, 0)),
            vmem,
            vmem,
        ],
        scratch_shapes=[pltpu.VMEM((length, 128), LOW)],
        compiler_params=pltpu.CompilerParams(vmem_limit_bytes=60 * MEGA),
        name="attend",
    )(meta, rows, weight, base, jump)


def norm_of(summed):
    mean = jnp.mean(summed, axis=1, keepdims=True)
    centred = summed - mean
    variance = jnp.mean(centred * centred, axis=1, keepdims=True)
    scale = lax.rsqrt(variance + EPSILON)
    return centred * scale, scale


def norm_back(scaled, normed, scale):
    total = jnp.mean(scaled, axis=1, keepdims=True)
    cross = jnp.mean(scaled * normed, axis=1, keepdims=True)
    return scale * (scaled - total - normed * cross)


HIDDEN = 512


def middle_kernel(context, rows, cot, m_full, o_full, gains, lo_ref, gc_ref, act_ref, gi_ref, fl_ref,
                  gm_ref, ga_ref, gfs_ref, sums, slopes):
    tile = rows.shape[1]
    part = rows.shape[2]
    pieces = o_full.shape[2] // HIDDEN
    gain1, bias1, gain2, bias2 = (gains[k : k + 1, :] for k in range(4))
    summed = jnp.concatenate([rows[0], rows[1]], axis=1).astype(WIDE)
    for h in range(2):
        summed = summed + contract(context[h], m_full[h, :, 0:part], 1, 1)
    normed1, scale1 = norm_of(summed)
    first = normed1 * gain1 + bias1
    first_low = first.astype(LOW)
    fl_ref[...] = first_low
    mixed = jnp.zeros(first.shape, WIDE)
    for h in range(2):
        for j in range(pieces):
            k = h * pieces + j
            lo_end = part + j * HIDDEN
            inner = contract(first_low, m_full[h, :, lo_end : lo_end + HIDDEN], 1, 0)
            share = 0.5 * (1.0 + lax.erf(inner * ROOT_HALF))
            slopes[:, k * HIDDEN : (k + 1) * HIDDEN] = (
                share + inner * jnp.exp(-0.5 * inner * inner) * INVERSE_ROOT
            )
            act_ref[:, k * HIDDEN : (k + 1) * HIDDEN] = (inner * share).astype(LOW)
    for h in range(2):
        width = pieces * HIDDEN
        mixed = mixed + contract(act_ref[:, h * width : (h + 1) * width], o_full[h], 1, 1)
    normed2, scale2 = norm_of(first + mixed)
    result = (normed2 * gain2 + bias2).astype(LOW)
    for h in range(2):
        lo_ref[h] = result[:, h * part : (h + 1) * part]
    cotangent = jnp.concatenate([cot[0], cot[1]], axis=1).astype(WIDE)
    second_gain = jnp.sum(cotangent * normed2, axis=0, keepdims=True)
    second_bias = jnp.sum(cotangent, axis=0, keepdims=True)
    grad_second = norm_back(cotangent * gain2, normed2, scale2)
    grad_mixed = grad_second.astype(LOW)
    gm_ref[...] = grad_mixed
    for h in range(2):
        for j in range(pieces):
            k = h * pieces + j
            raised = contract(grad_mixed, o_full[h, :, j * HIDDEN : (j + 1) * HIDDEN], 1, 0)
            gi_ref[:, k * HIDDEN : (k + 1) * HIDDEN] = (
                raised * slopes[:, k * HIDDEN : (k + 1) * HIDDEN]
            ).astype(LOW)
    grad_first = grad_second
    for h in range(2):
        width = pieces * HIDDEN
        grad_first = grad_first + contract(
            gi_ref[:, h * width : (h + 1) * width], m_full[h, :, part : part + width], 1, 1
        )
    first_gain = jnp.sum(grad_first * normed1, axis=0, keepdims=True)
    first_bias = jnp.sum(grad_first, axis=0, keepdims=True)
    grad_sum = norm_back(grad_first * gain1, normed1, scale1)
    gfs_ref[...] = grad_sum
    grad_attended = grad_sum.astype(LOW)
    ga_ref[...] = grad_attended
    for h in range(2):
        gc_ref[h] = contract(grad_attended, m_full[h, :, 0:part], 1, 0).astype(LOW)
    found = jnp.concatenate([first_gain, first_bias, second_gain, second_bias], axis=0)

    @pl.when(pl.program_id(0) == 0)
    def _():
        sums[...] = found

    @pl.when(pl.program_id(0) > 0)
    def _():
        sums[...] += found


def middle_call(context, rows, cot, m_full, o_full, gains):
    tile = 256
    half, part = rows.shape[1:]
    width = 2 * part
    hidden = 2 * o_full.shape[2]
    vmem = pl.BlockSpec(memory_space=pltpu.VMEM)
    split = pl.BlockSpec((2, tile, part), lambda i: (0, i, 0))
    flat = pl.BlockSpec((tile, width), lambda i: (i, 0))
    wide = pl.BlockSpec((tile, hidden), lambda i: (i, 0))
    low = lambda *shape: jax.ShapeDtypeStruct(shape, LOW)
    return pl.pallas_call(
        middle_kernel,
        grid=(half // tile,),
        out_shape=[
            low(2, half, part),
            low(2, half, part),
            low(half, hidden),
            low(half, hidden),
            low(half, width),
            low(half, width),
            low(half, width),
            jax.ShapeDtypeStruct((half, width), WIDE),
            jax.ShapeDtypeStruct((4, width), WIDE),
        ],
        in_specs=[split, split, split, vmem, vmem, vmem],
        out_specs=[
            split,
            split,
            wide,
            wide,
            flat,
            flat,
            flat,
            flat,
            pl.BlockSpec((4, width), lambda i: (0, 0)),
        ],
        scratch_shapes=[pltpu.VMEM((tile, hidden), WIDE)],
        compiler_params=pltpu.CompilerParams(vmem_limit_bytes=60 * MEGA),
        name="middle",
    )(context, rows, cot, m_full, o_full, gains)


def backward_kernel(core, meta, base, jump, soft, grads, context, inverse, q_ref, k_ref, v_ref, rows,
                    weight, kept, part_ref, dx_ref, ones, keys_sum, values_sum, made):
    step = pl.program_id(0)
    p = step // SPAN
    i = step % SPAN
    length = q_ref.shape[1]
    scale = HEAD_DIM ** (-0.5)
    lane = lanes(BLOCK)
    here = pl.ds(i * BLOCK, BLOCK)

    @pl.when(step == 0)
    def _():
        ones[...] = (lanes(length) < 2).astype(WIDE).astype(LOW)

    grad = grads[p, here].astype(WIDE)
    turned = grad * inverse[p, here]
    both = turned * context[p, here].astype(WIDE)
    turned_low = turned.astype(LOW)
    queries = q_ref[p, here]
    keys = k_ref[p]
    values = jnp.concatenate([v_ref[p], ones[...]], axis=1)
    turned_flip = jnp.transpose(turned).astype(LOW)
    queries_flip = jnp.transpose(queries.astype(WIDE)).astype(LOW)
    outs = []
    for head in range(2):
        chosen = (lane // HEAD_DIM) == head
        centre = -jnp.sum(jnp.where(chosen, both, 0.0), axis=1, keepdims=True)
        coarse = centre.astype(LOW).astype(WIDE)
        fine = jnp.where(lane == 0, coarse, jnp.where(lane == 1, centre - coarse, 0.0))
        ours = jnp.concatenate(
            [jnp.where(chosen, turned_low, 0).astype(LOW), fine.astype(LOW)], axis=1
        )
        raised = soft[0, head]
        scores = (contract(ours, values, 1, 1) * raised.astype(WIDE)).astype(LOW)
        outs.append(contract(scores, keys, 1, 0))
        mine = slice(head * HEAD_DIM, (head + 1) * HEAD_DIM)
        values_add = contract(turned_flip[mine], raised, 1, 0)
        keys_add = contract(queries_flip[mine], scores, 1, 0)

        @pl.when(i == 0)
        def _():
            values_sum[mine] = values_add
            keys_sum[mine] = keys_add

        @pl.when(i > 0)
        def _():
            values_sum[mine] += values_add
            keys_sum[mine] += keys_add

    cosine, sine, low = turn_parts(meta, base, jump, i)
    grad_queries = jnp.where(lane < HEAD_DIM, outs[0], outs[1]) * scale
    made[p, here, 0:128] = turn(grad_queries, cosine, -sine, low).astype(LOW)

    @pl.when(i == SPAN - 1)
    def _():
        grad_keys = jnp.transpose(keys_sum[...])
        grad_values = jnp.transpose(values_sum[...])
        for b in range(SPAN):
            there = slice(b * BLOCK, (b + 1) * BLOCK)
            cosine, sine, low = turn_parts(meta, base, jump, b)
            made[p, there, 128:256] = turn(grad_keys[there], cosine, -sine, low).astype(LOW)
        made[p, :, 256:384] = grad_values.astype(LOW)
        for h in range(2):
            part = rows.shape[2]
            part_ref[p, h * part : (h + 1) * part] = contract(rows[h], made[p], 0, 0).astype(LOW)

    @pl.when(step == 3 * SPAN - 1)
    def _():
        half = kept.shape[0]
        part = rows.shape[2]
        for other in range(2):
            c = core[0] if other == 0 else 1 - core[0]
            there = pl.ds(c * half, half)
            gained = kept[...] if other == 0 else jnp.zeros(kept.shape, WIDE)
            for pair in range(3):
                gained = gained + contract(made[pair, there], weight[:, pair * 384 : pair * 384 + 384], 1, 1)
            for h in range(2):
                dx_ref[c, h] = gained[:, h * part : (h + 1) * part].astype(LOW)


def backward_call(core, meta, base, jump, soft, grads, context, inverse, q, k, v, rows, weight, kept):
    length = q.shape[1]
    half, width = kept.shape
    part = width // 2
    vmem = pl.BlockSpec(memory_space=pltpu.VMEM)
    smem = pl.BlockSpec(memory_space=pltpu.SMEM)
    return pl.pallas_call(
        backward_kernel,
        grid=(3 * SPAN,),
        out_shape=[
            jax.ShapeDtypeStruct((3, width, 384), LOW),
            jax.ShapeDtypeStruct((2, 2, half, part), LOW),
        ],
        in_specs=[smem, smem, vmem, vmem, pl.BlockSpec((1, 2, BLOCK, length), lambda s: (s, 0, 0, 0))]
        + [vmem] * 9,
        out_specs=[vmem, vmem],
        scratch_shapes=[
            pltpu.VMEM((length, 128), LOW),
            pltpu.VMEM((128, length), WIDE),
            pltpu.VMEM((128, length), WIDE),
            pltpu.VMEM((3, length, 384), LOW),
        ],
        compiler_params=pltpu.CompilerParams(vmem_limit_bytes=60 * MEGA),
        name="attend_back",
    )(core, meta, base, jump, soft, grads, context, inverse, q, k, v, rows, weight, kept)


def swap_halves(values, half, c):
    mine = lax.dynamic_slice_in_dim(values, c * half, half, axis=1)
    theirs = lax.dynamic_slice_in_dim(values, (1 - c) * half, half, axis=1)
    n_wide = lax.axis_size("wide")
    got = lax.ppermute(theirs, "wide", [(w, w ^ 1) for w in range(n_wide)])
    mine, got = (jnp.moveaxis(item, 0, 1).reshape(half, -1) for item in (mine, got))
    return jnp.where(c == 0, jnp.stack([mine, got]), jnp.stack([got, mine]))


def swap_back(values, half, c):
    n_wide = lax.axis_size("wide")
    mine = lax.dynamic_index_in_dim(values, c, 0, keepdims=False)
    theirs = lax.dynamic_index_in_dim(values, 1 - c, 0, keepdims=False)
    got = lax.ppermute(theirs, "wide", [(w, w ^ 1) for w in range(n_wide)])
    whole = jnp.where(c == 0, jnp.concatenate([mine, got]), jnp.concatenate([got, mine]))
    return jnp.moveaxis(whole.reshape(whole.shape[0], -1, 128), 1, 0)


def owned(
    inputs,
    block_segment,
    query_weight,
    key_weight,
    value_weight,
    output_weight,
    inner_weight,
    outer_weight,
    first_gain,
    first_bias,
    second_gain,
    second_bias,
    output_cotangent,
):
    wide = lax.axis_size("wide")
    depth = wide // 4
    r = query_weight.shape[0]
    part = query_weight.shape[1]
    length = inputs.shape[0]
    half = length // 2
    x, w, c, _, _ = place()
    pairs = part // 128
    q_own = jnp.concatenate(
        [
            item[:, p * 128 : (p + 1) * 128]
            for p in range(pairs)
            for item in (query_weight, key_weight, value_weight)
        ],
        axis=1,
    )
    m_own = jnp.concatenate([output_weight.T, inner_weight], axis=1)
    o_own = outer_weight.T
    earlier = jnp.sum((block_segment[None, :] < block_segment[:, None]).astype(jnp.int32), axis=1)
    offsets = jnp.arange(SPAN, dtype=jnp.int32) - earlier
    meta = jnp.zeros((1, 128), jnp.int32)
    meta = meta.at[0, 0:SPAN].set(block_segment).at[0, SPAN : 2 * SPAN].set(offsets)
    widths = [item.shape[1] for item in (q_own, m_own, o_own)]
    cuts = [(item // 128 // 2) * 128 for item in widths]
    meta, cot, rows, q_full, m_full, o_full = gather_call(
        depth, cuts, meta, output_cotangent, inputs, q_own, m_own, o_own
    )
    gains = jnp.stack([first_gain, first_bias, second_gain, second_bias])
    gains = lax.all_gather(gains, "narrow", axis=1, tiled=True)
    weight = lax.dynamic_index_in_dim(q_full, c, 0, keepdims=False).reshape(2 * part, widths[0])
    m_full = m_full.reshape(2, 2 * part, widths[1])
    o_full = o_full.reshape(2, 2 * part, widths[2])
    base, jump = angle_tables()
    q, k, v, soft, inverse, context = forward_call(meta, rows, weight, base, jump)
    all_context = swap_halves(context, half, c)
    own_rows = lax.dynamic_slice_in_dim(rows, c * half, half, axis=1)
    lo, gc, act, gi, fl, gm, ga, kept, sums = middle_call(
        all_context, own_rows, cot, m_full, o_full, gains
    )
    hidden = act.shape[1] // 2
    o_part = jnp.stack(
        [left_transposed(gm, act[:, h * hidden : (h + 1) * hidden]).astype(LOW) for h in range(2)]
    )
    m_part = jnp.stack(
        [
            jnp.concatenate(
                [
                    left_transposed(ga, all_context[h]).astype(LOW),
                    left_transposed(fl, gi[:, h * hidden : (h + 1) * hidden]).astype(LOW),
                ],
                axis=1,
            )
            for h in range(2)
        ]
    )
    grads = swap_back(gc, half, c)
    core = jnp.reshape(c, (1,)).astype(jnp.int32)
    q_part, dx = backward_call(
        core, meta, base, jump, soft, grads, context, inverse, q, k, v, rows, weight, kept
    )
    q_part = jnp.moveaxis(q_part, 0, 1)
    q_part = q_part.reshape(depth, 2, 2, r, widths[0])
    m_part = m_part.reshape(2, depth, 2, 2, r, widths[1])
    o_part = o_part.reshape(2, depth, 2, 2, r, widths[2])
    layer_output, input_gradient, o_sum, m_sum, q_sum = scatter_call(
        depth, [cuts[2], cuts[1], cuts[0]], lo, dx, o_part, m_part, q_part
    )
    q_sum = q_sum.reshape(r, pairs, 3, 128)
    sums = lax.psum_scatter(sums, ("narrow", "wide"), scatter_dimension=1, tiled=True)
    return (
        layer_output,
        input_gradient,
        q_sum[:, :, 0].reshape(r, part),
        q_sum[:, :, 1].reshape(r, part),
        q_sum[:, :, 2].reshape(r, part),
        m_sum[:, 0:part].T,
        m_sum[:, part:],
        o_sum.T,
        sums[0],
        sums[1],
        sums[2],
        sums[3],
    )


def program(*arrays):
    rows = arrays[2].shape[0]
    whole = rows % 16 == 0 and lax.axis_size("narrow") == 2 and lax.axis_size("wide") % 4 == 0
    return owned(*arrays) if whole else shards(*arrays)


def solution(mesh):
    placed = (
        P("wide", "narrow"),
        P("wide"),
        P("wide", "narrow"),
        P("wide", "narrow"),
        P("wide", "narrow"),
        P("narrow", "wide"),
        P("wide", "narrow"),
        P("narrow", "wide"),
        P("narrow"),
        P("narrow"),
        P("narrow"),
        P("narrow"),
        P("wide", "narrow"),
    )
    return jax.shard_map(
        program,
        mesh=mesh,
        in_specs=placed,
        out_specs=(
            P("wide", "narrow"),
            P("wide", "narrow"),
            P("wide", "narrow"),
            P("wide", "narrow"),
            P("wide", "narrow"),
            P("narrow", "wide"),
            P("wide", "narrow"),
            P("narrow", "wide"),
            P(("narrow", "wide")),
            P(("narrow", "wide")),
            P(("narrow", "wide")),
            P(("narrow", "wide")),
        ),
        check_vma=False,
    )
```

```python
import functools

import jax
import jax.numpy as jnp
import numpy as np
from jax import lax
from jax.experimental import pallas as pl
from jax.experimental.pallas import tpu as pltpu
from jax.sharding import PartitionSpec as P

HEAD_DIM = 64
BLOCK = 512
SPAN = 3


EPSILON = 1e-06
NEGATIVE = -1e30
THETA = 10000.0
ROOT_HALF = 0.7071067811865476
INVERSE_ROOT = 0.3989422804014327


def product(left, right):
    return jnp.dot(left, right, preferred_element_type=jnp.float32)


def left_transposed(left, right):
    return lax.dot_general(
        left, right, (((0,), (0,)), ((), ())), preferred_element_type=jnp.float32
    )


def right_transposed(left, right):
    return lax.dot_general(
        left, right, (((1,), (1,)), ((), ())), preferred_element_type=jnp.float32
    )


def whole_features(values):
    return lax.all_gather(values, "narrow", axis=1, tiled=True)


def feature_sums(values):
    return lax.psum_scatter(
        values.astype(jnp.bfloat16), "narrow", scatter_dimension=1, tiled=True
    ).astype(jnp.float32)


def moments(first_sum, second_sum):
    return lax.psum((first_sum, second_sum), "narrow")


def gelu_value(values):
    return 0.5 * values * (1.0 + lax.erf(values * ROOT_HALF))


def gelu_slope(values):
    return (
        0.5 * (1.0 + lax.erf(values * ROOT_HALF))
        + values * jnp.exp(-0.5 * values * values) * INVERSE_ROOT
    )


def rotate(values, cosine, sine):
    half = values.shape[-1] // 2
    first = values[..., :half]
    second = values[..., half:]
    return jnp.concatenate(
        [first * cosine - second * sine, second * cosine + first * sine], axis=-1
    )


def rotate_back(values, cosine, sine):
    half = values.shape[-1] // 2
    first = values[..., :half]
    second = values[..., half:]
    return jnp.concatenate(
        [first * cosine + second * sine, second * cosine - first * sine], axis=-1
    )


def tables(block_segment):
    segment = block_segment.reshape(-1, SPAN)
    earlier = jnp.sum((segment[:, None, :] < segment[:, :, None]).astype(jnp.int32), axis=2)
    offsets = (jnp.arange(SPAN, dtype=jnp.int32)[None, :] - earlier) * BLOCK
    positions = (
        (offsets[:, :, None] + jnp.arange(BLOCK, dtype=jnp.int32)[None, None, :])
        .reshape(-1)
        .astype(jnp.float32)
    )
    half = HEAD_DIM // 2
    rates = THETA ** (-jnp.arange(half, dtype=jnp.float32) / half)
    angle = positions[:, None] * rates[None, :]
    labels = jnp.repeat(segment, BLOCK, axis=1)
    return (jnp.cos(angle)[:, None, :], jnp.sin(angle)[:, None, :], labels)


def normalize(summed, gain, bias, width):
    total, squares = moments(jnp.sum(summed, axis=1), jnp.sum(summed * summed, axis=1))
    mean = total / width
    reciprocal = lax.rsqrt(squares / width - mean * mean + EPSILON)
    normed = (summed - mean[:, None]) * reciprocal[:, None]
    return (normed * gain + bias, normed, reciprocal)


def normalize_back(grad, normed, reciprocal, gain, width):
    scaled = grad * gain
    total, cross = moments(jnp.sum(scaled, axis=1), jnp.sum(scaled * normed, axis=1))
    return reciprocal[:, None] * (scaled - total[:, None] / width - normed * cross[:, None] / width)


def block_scores(block_queries, group_keys, block_labels, group_labels, factor):
    scores = (
        jnp.einsum("qhd,khd->hqk", block_queries, group_keys, preferred_element_type=jnp.float32)
        * factor
    )
    same = block_labels[:, None] == group_labels[None, :]
    return jnp.where(same[None], scores, NEGATIVE)


def attention_forward(queries, keys, values, labels, factor):
    groups, length = labels.shape
    shape = (groups, length) + queries.shape[1:]

    def one_group(items):
        group_queries, group_keys, group_values, group_labels = items
        contexts = []
        totals = []
        for index in range(length // BLOCK):
            low_end = index * BLOCK
            high_end = low_end + BLOCK
            scores = block_scores(
                group_queries[low_end:high_end],
                group_keys,
                group_labels[low_end:high_end],
                group_labels,
                factor,
            )
            top = jnp.max(scores, axis=2, keepdims=True)
            raised = jnp.exp(scores - top)
            summed = jnp.sum(raised, axis=2, keepdims=True)
            soft = (raised / summed).astype(jnp.bfloat16)
            contexts.append(
                jnp.einsum("hqk,khd->qhd", soft, group_values, preferred_element_type=jnp.float32)
            )
            totals.append((top + jnp.log(summed))[..., 0])
        return (jnp.concatenate(contexts, axis=0), jnp.concatenate(totals, axis=1))

    contexts, totals = lax.map(
        one_group, (queries.reshape(shape), keys.reshape(shape), values.reshape(shape), labels)
    )
    return (contexts.reshape(queries.shape), totals)


def attention_backward(queries, keys, values, totals, grad_context, labels, factor):
    groups, length = labels.shape
    shape = (groups, length) + queries.shape[1:]

    def one_group(items):
        group_queries, group_keys, group_values, group_totals, group_grads, group_labels = items
        keys_grad = jnp.zeros(group_keys.shape, jnp.float32)
        values_grad = jnp.zeros(group_values.shape, jnp.float32)
        pieces = []
        for index in range(length // BLOCK):
            low_end = index * BLOCK
            high_end = low_end + BLOCK
            block_queries = group_queries[low_end:high_end]
            block_grads = group_grads[low_end:high_end]
            scores = block_scores(
                block_queries, group_keys, group_labels[low_end:high_end], group_labels, factor
            )
            soft = jnp.exp(scores - group_totals[:, low_end:high_end, None])
            inner = jnp.einsum(
                "qhd,khd->hqk", block_grads, group_values, preferred_element_type=jnp.float32
            )
            centre = jnp.sum(soft * inner, axis=2, keepdims=True)
            scores_grad = (soft * (inner - centre)).astype(jnp.bfloat16)
            pieces.append(
                jnp.einsum(
                    "hqk,khd->qhd", scores_grad, group_keys, preferred_element_type=jnp.float32
                )
                * factor
            )
            keys_grad = (
                keys_grad
                + jnp.einsum(
                    "hqk,qhd->khd", scores_grad, block_queries, preferred_element_type=jnp.float32
                )
                * factor
            )
            values_grad = values_grad + jnp.einsum(
                "hqk,qhd->khd",
                soft.astype(jnp.bfloat16),
                block_grads,
                preferred_element_type=jnp.float32,
            )
        return (jnp.concatenate(pieces, axis=0), keys_grad, values_grad)

    queries_grad, keys_grad, values_grad = lax.map(
        one_group,
        (
            queries.reshape(shape),
            keys.reshape(shape),
            values.reshape(shape),
            totals,
            grad_context.reshape(shape),
            labels,
        ),
    )
    return (
        queries_grad.reshape(queries.shape),
        keys_grad.reshape(queries.shape),
        values_grad.reshape(queries.shape),
    )


def shards(
    inputs,
    block_segment,
    query_weight,
    key_weight,
    value_weight,
    output_weight,
    inner_weight,
    outer_weight,
    first_gain,
    first_bias,
    second_gain,
    second_bias,
    output_cotangent,
):
    width = first_gain.shape[0] * lax.axis_size("narrow")
    tokens = inputs.shape[0]
    factor = HEAD_DIM ** (-0.5)
    cosine, sine, labels = tables(block_segment)
    full_inputs = whole_features(inputs)
    query_full, key_full, value_full, inner_full = (
        lax.all_gather(query_weight, "wide", axis=0, tiled=True),
        lax.all_gather(key_weight, "wide", axis=0, tiled=True),
        lax.all_gather(value_weight, "wide", axis=0, tiled=True),
        lax.all_gather(inner_weight, "wide", axis=0, tiled=True),
    )
    output_full, outer_full = (
        lax.all_gather(output_weight, "wide", axis=1, tiled=True),
        lax.all_gather(outer_weight, "wide", axis=1, tiled=True),
    )
    head_shape = (tokens, query_weight.shape[1] // HEAD_DIM, HEAD_DIM)
    queries = rotate(product(full_inputs, query_full).reshape(head_shape), cosine, sine).astype(
        jnp.bfloat16
    )
    keys = rotate(product(full_inputs, key_full).reshape(head_shape), cosine, sine).astype(
        jnp.bfloat16
    )
    values = product(full_inputs, value_full).astype(jnp.bfloat16).reshape(head_shape)
    context, totals = attention_forward(queries, keys, values, labels, factor)
    context_low = context.reshape(tokens, -1).astype(jnp.bfloat16)
    attended = feature_sums(product(context_low, output_full))
    first, first_normed, first_scale = normalize(
        inputs.astype(jnp.float32) + attended, first_gain, first_bias, width
    )
    first_low = first.astype(jnp.bfloat16)
    feed_rows = whole_features(first_low)
    inner = product(feed_rows, inner_full)
    activated = gelu_value(inner).astype(jnp.bfloat16)
    mixed = feature_sums(product(activated, outer_full))
    second, second_normed, second_scale = normalize(first + mixed, second_gain, second_bias, width)
    layer_output = second.astype(jnp.bfloat16)
    cotangent = output_cotangent.astype(jnp.float32)
    second_gain_grad = jnp.sum(cotangent * second_normed, axis=0)
    second_bias_grad = jnp.sum(cotangent, axis=0)
    grad_second = normalize_back(cotangent, second_normed, second_scale, second_gain, width)
    grad_mixed = grad_second.astype(jnp.bfloat16)
    grad_rows = whole_features(grad_mixed)
    grad_activated = right_transposed(grad_rows, outer_full)
    outer_grad = left_transposed(activated, grad_rows)
    grad_inner = (grad_activated * gelu_slope(inner)).astype(jnp.bfloat16)
    inner_grad = left_transposed(feed_rows, grad_inner)
    grad_first = grad_second + feature_sums(right_transposed(grad_inner, inner_full))
    first_gain_grad = jnp.sum(grad_first * first_normed, axis=0)
    first_bias_grad = jnp.sum(grad_first, axis=0)
    grad_first_sum = normalize_back(grad_first, first_normed, first_scale, first_gain, width)
    attended_rows = whole_features(grad_first_sum.astype(jnp.bfloat16))
    output_grad = left_transposed(context_low, attended_rows)
    grad_context = right_transposed(attended_rows, output_full).astype(jnp.bfloat16)
    queries_grad, keys_grad, values_grad = attention_backward(
        queries, keys, values, totals, grad_context.reshape(head_shape), labels, factor
    )
    queries_grad = rotate_back(queries_grad, cosine, sine).reshape(tokens, -1).astype(jnp.bfloat16)
    keys_grad = rotate_back(keys_grad, cosine, sine).reshape(tokens, -1).astype(jnp.bfloat16)
    values_grad = values_grad.reshape(tokens, -1).astype(jnp.bfloat16)
    query_grad = left_transposed(full_inputs, queries_grad)
    key_grad = left_transposed(full_inputs, keys_grad)
    value_grad = left_transposed(full_inputs, values_grad)
    spread = (
        right_transposed(queries_grad, query_full)
        + right_transposed(keys_grad, key_full)
        + right_transposed(values_grad, value_full)
    )
    input_gradient = (grad_first_sum + feature_sums(spread)).astype(jnp.bfloat16)
    (
        query_total,
        key_total,
        value_total,
        inner_total,
        first_gain_total,
        first_bias_total,
        second_gain_total,
        second_bias_total,
    ) = (
        lax.psum_scatter(query_grad, "wide", scatter_dimension=0, tiled=True),
        lax.psum_scatter(key_grad, "wide", scatter_dimension=0, tiled=True),
        lax.psum_scatter(value_grad, "wide", scatter_dimension=0, tiled=True),
        lax.psum_scatter(inner_grad, "wide", scatter_dimension=0, tiled=True),
        lax.psum_scatter(first_gain_grad, "wide", scatter_dimension=0, tiled=True),
        lax.psum_scatter(first_bias_grad, "wide", scatter_dimension=0, tiled=True),
        lax.psum_scatter(second_gain_grad, "wide", scatter_dimension=0, tiled=True),
        lax.psum_scatter(second_bias_grad, "wide", scatter_dimension=0, tiled=True),
    )
    output_total, outer_total = (
        lax.psum_scatter(output_grad, "wide", scatter_dimension=1, tiled=True),
        lax.psum_scatter(outer_grad, "wide", scatter_dimension=1, tiled=True),
    )
    return (
        layer_output,
        input_gradient,
        query_total,
        key_total,
        value_total,
        output_total,
        inner_total,
        outer_total,
        first_gain_total,
        first_bias_total,
        second_gain_total,
        second_bias_total,
    )


LOW = jnp.bfloat16
WIDE = jnp.float32
MESH = pl.DeviceIdType.MESH
MEGA = 1 << 20
ANY = pl.BlockSpec(memory_space=pl.ANY)


def contract(left, right, left_dim, right_dim):
    return lax.dot_general(
        left, right, (((left_dim,), (right_dim,)), ((), ())), preferred_element_type=WIDE
    )


def place():
    x = lax.axis_index("narrow")
    w = lax.axis_index("wide")
    c = lax.rem(w, 2)
    y = lax.rem(lax.div(w, 2), 2)
    q = lax.div(w, 4)
    return x, w, c, y, q


class Links:
    def __init__(self, depth):
        self.depth = depth
        self.x, self.w, self.c, self.y, self.q = place()
        self.across = (1 - self.x, self.w)
        self.beside = (self.x, self.w + 2 - 4 * self.y)
        self.sibling = (self.x, self.w + 1 - 2 * self.c)
        self.corner = (1 - self.x, self.w + 1 - 2 * self.c)

    def far(self, step):
        return (self.x, lax.rem(self.w + 4 * step, 4 * self.depth))

    def row(self, step):
        return lax.rem(self.q + self.depth - step, self.depth)

    def meet(self):
        barrier = pltpu.get_barrier_semaphore()
        others = [self.across, self.beside, self.sibling, self.corner]
        others += [self.far(step) for step in range(1, self.depth)]
        for other in others:
            pl.semaphore_signal(barrier, 1, device_id=other, device_id_type=MESH)
        pl.semaphore_wait(barrier, len(others))


def remote(source, target, send, recv, device):
    return pltpu.make_async_remote_copy(
        src_ref=source,
        dst_ref=target,
        send_sem=send,
        recv_sem=recv,
        device_id=device,
        device_id_type=MESH,
    )


def gather_marks(depth):
    return 5 * depth + 2


class Gather:
    def __init__(self, links, own, full, cut, whole, send, recv, index, local):
        self.links, self.own, self.full, self.cut = links, own, full, cut
        self.whole, self.local = whole, local
        self.send = lambda k: send.at[index, k]
        self.recv = lambda k: recv.at[index, k]
        self.width = own.shape[-1]

    def slot(self, h, q, y):
        return self.full.at[h, q, y, self.links.c]

    def low(self, ref):
        return ref.at[:, pl.ds(0, self.cut)]

    def high(self, ref):
        return ref.at[:, pl.ds(self.cut, self.width - self.cut)]

    def copy(self, kind, step=0):
        n, d = self.links, self.links.depth
        mine = self.slot(n.x, n.q, n.y)
        column = self.slot(n.x, n.row(step), n.y)
        first = self.own if step == 0 else column
        if kind == "far":
            return self.move(self.own, mine, step - 1, n.far(step))
        if kind == "across":
            return self.move(first, column, d + step, n.across)
        if kind == "beside":
            return self.move(first, column, 2 * d + step, n.beside)
        if kind == "high":
            part = self.high(self.slot(1 - n.x, n.row(step), n.y))
            return self.move(part, part, 3 * d + step, n.beside)
        if kind == "low":
            part = self.low(self.slot(n.x, n.row(step), 1 - n.y))
            return self.move(part, part, 4 * d + step, n.across)
        part = self.full.at[step if self.whole else 1 - n.c, :, :, n.c]
        return self.move(part, part, 5 * d + step, n.sibling)

    def move(self, source, target, mark, device):
        return remote(source, target, self.send(mark), self.recv(mark), device)

    def arrived(self, target, mark):
        self.move(target, target, mark, self.links.sibling).wait_recv()

    def keep(self):
        n = self.links
        return pltpu.make_async_copy(self.own, self.slot(n.x, n.q, n.y), self.local)

    def begin(self):
        self.keep().start()
        self.copy("across").start()
        self.copy("beside").start()
        for step in range(1, self.links.depth):
            self.copy("far", step).start()

    def second(self, step):
        n = self.links
        self.arrived(self.slot(n.x, n.row(step), n.y), step - 1)
        self.copy("across", step).start()
        self.copy("beside", step).start()

    def third(self, step):
        n, d = self.links, self.links.depth
        self.arrived(self.slot(1 - n.x, n.row(step), n.y), d + step)
        self.copy("high", step).start()
        self.arrived(self.slot(n.x, n.row(step), 1 - n.y), 2 * d + step)
        self.copy("low", step).start()

    def fourth(self):
        n, d = self.links, self.links.depth
        for step in range(d):
            got = self.slot(1 - n.x, n.row(step), 1 - n.y)
            self.arrived(self.high(got), 3 * d + step)
            self.arrived(self.low(got), 4 * d + step)
        self.keep().wait()
        for h in range(2 if self.whole else 1):
            self.copy("sibling", h).start()

    def finish(self):
        n, d = self.links, self.links.depth
        for h in range(2 if self.whole else 1):
            self.arrived(self.full.at[h if self.whole else n.c, :, :, 1 - n.c], 5 * d + h)

    def close(self):
        d = self.links.depth
        for step in range(d):
            if step:
                self.copy("far", step).wait_send()
            for kind in ("across", "beside", "high", "low"):
                self.copy(kind, step).wait_send()
        for h in range(2 if self.whole else 1):
            self.copy("sibling", h).wait_send()


class Share:
    def __init__(self, links, in_ref, rows, cot_in, cot, note_in, note, gain_in, gain, send, recv, local):
        n = self.links = links
        half = cot_in.shape[0] // 2
        self.home = n.x == n.c
        s, r = (lambda k: send.at[k]), (lambda k: recv.at[k])
        mine, theirs = pl.ds(n.c * half, half), pl.ds((1 - n.c) * half, half)
        near, far = rows.at[n.x], rows.at[1 - n.x]
        self.rows_across = lambda: remote(in_ref, near, s(0), r(0), n.across)
        self.rows_beside = lambda: remote(in_ref, near, s(1), r(1), n.sibling)
        self.rows_further = lambda: remote(far, far, s(2), r(2), n.sibling)
        self.note = lambda: remote(note_in, note, s(3), r(3), n.sibling)
        self.cot_beside = lambda: remote(cot_in.at[theirs], cot.at[n.x], s(4), r(4), n.sibling)
        self.cot_across = lambda: remote(cot_in.at[mine], cot.at[n.x], s(5), r(5), n.across)
        self.cot_corner = lambda: remote(cot_in.at[theirs], cot.at[n.x], s(6), r(6), n.corner)
        self.gain = lambda: remote(gain_in, gain.at[n.x], s(7), r(7), n.across)
        self.keep = lambda: [
            pltpu.make_async_copy(gain_in, gain.at[n.x], local.at[0]),
        ]
        self.keep_home = lambda: [
            pltpu.make_async_copy(in_ref, near, local.at[1]),
            pltpu.make_async_copy(note_in, note, local.at[2]),
            pltpu.make_async_copy(cot_in.at[mine], cot.at[n.x], local.at[3]),
        ]

    def begin(self):
        @pl.when(self.home)
        def _():
            self.note().start()
            self.rows_beside().start()
            for item in self.keep_home():
                item.start()

        @pl.when(jnp.logical_not(self.home))
        def _():
            self.rows_across().start()

        self.gain().start()
        for item in self.keep():
            item.start()

    def further(self):
        @pl.when(self.home)
        def _():
            self.rows_across().wait_recv()
            self.rows_further().start()
            for item in self.keep_home():
                item.wait()

        @pl.when(jnp.logical_not(self.home))
        def _():
            self.note().wait_recv()
            self.rows_beside().wait_recv()
            self.rows_further().wait_recv()

        for item in self.keep():
            item.wait()

    def later(self):
        @pl.when(self.home)
        def _():
            self.cot_beside().start()

        @pl.when(jnp.logical_not(self.home))
        def _():
            self.cot_across().start()
            self.cot_corner().start()

    def finish(self):
        self.gain().wait()

        @pl.when(self.home)
        def _():
            self.note().wait_send()
            self.rows_beside().wait_send()
            self.rows_further().wait_send()
            self.cot_beside().wait_send()
            self.cot_across().wait_recv()

        @pl.when(jnp.logical_not(self.home))
        def _():
            self.rows_across().wait_send()
            self.cot_across().wait_send()
            self.cot_corner().wait_send()
            self.cot_beside().wait_recv()
            self.cot_corner().wait_recv()


def plus(left, right):
    return (left.astype(WIDE) + right.astype(WIDE)).astype(LOW)


def scatter_marks(depth):
    return depth + 5


class Scatter:
    def __init__(self, links, part, cut, whole, bufs, out, send, recv, index, local):
        self.links, self.part, self.cut, self.whole, self.out = links, part, cut, whole, out
        self.held, self.other, self.x1, self.y1, self.x2, self.y2, self.z = bufs
        self.send = lambda k: send.at[index, k]
        self.recv = lambda k: recv.at[index, k]
        self.local = local
        self.sent = []
        self.rest = part.shape[-1] - cut

    def go(self, source, target, mark, device):
        copy = remote(source, target, self.send(mark), self.recv(mark), device)
        copy.start()
        self.sent.append(copy)

    def arrived(self, target, mark):
        remote(target, target, self.send(mark), self.recv(mark), self.links.sibling).wait_recv()

    def begin(self):
        n = self.links
        if self.whole:
            self.go(self.part.at[:, :, :, 1 - n.c], self.other, 0, n.sibling)
            self.keep = pltpu.make_async_copy(self.part.at[:, :, :, n.c], self.held, self.local)
        else:
            self.go(self.part.at[:, :, 1 - n.c], self.held.at[n.c], 0, n.sibling)
            self.keep = pltpu.make_async_copy(
                self.part.at[:, :, n.c], self.held.at[n.c], self.local
            )
        self.keep.start()

    def join(self, h, y):
        for q in range(self.links.depth):
            self.held[h, q, y] = plus(self.held[h, q, y], self.other[h, q, y])

    def first(self):
        n = self.links
        self.keep.wait()
        if self.whole:
            self.arrived(self.other, 0)
            self.join(1 - n.x, 1 - n.y)
        else:
            self.arrived(self.held.at[1 - n.c], 0)
        corner = self.held.at[1 - n.x, :, 1 - n.y]
        self.go(corner.at[:, :, pl.ds(0, self.cut)], self.x1, 1, n.across)
        self.go(corner.at[:, :, pl.ds(self.cut, self.rest)], self.y1, 2, n.beside)
        if self.whole:
            self.join(n.x, 1 - n.y)
            self.join(1 - n.x, n.y)
            self.join(n.x, n.y)

    def second(self):
        n = self.links
        low, high = pl.ds(0, self.cut), pl.ds(self.cut, self.rest)
        self.arrived(self.x1, 1)
        for q in range(n.depth):
            self.held[n.x, q, 1 - n.y, :, low] = plus(
                self.held[n.x, q, 1 - n.y, :, low], self.x1[q]
            )
        self.go(self.held.at[n.x, :, 1 - n.y], self.y2, 3, n.beside)
        self.arrived(self.y1, 2)
        for q in range(n.depth):
            self.held[1 - n.x, q, n.y, :, high] = plus(
                self.held[1 - n.x, q, n.y, :, high], self.y1[q]
            )
        self.go(self.held.at[1 - n.x, :, n.y], self.x2, 4, n.across)

    def third(self):
        n = self.links
        self.arrived(self.y2, 3)
        self.arrived(self.x2, 4)
        for step in range(1, n.depth):
            q = lax.rem(n.q + step, n.depth)
            self.held[n.x, q, n.y] = plus(
                plus(self.held[n.x, q, n.y], self.x2[q]), self.y2[q]
            )
            self.go(self.held.at[n.x, q, n.y], self.z.at[step - 1], 4 + step, n.far(step))

    def fourth(self):
        n = self.links
        total = (
            self.held[n.x, n.q, n.y].astype(WIDE)
            + self.x2[n.q].astype(WIDE)
            + self.y2[n.q].astype(WIDE)
        )
        for step in range(1, n.depth):
            self.arrived(self.z.at[step - 1], 4 + step)
            total = total + self.z[step - 1].astype(WIDE)
        self.out[...] = total

    def close(self):
        for copy in self.sent:
            copy.wait_send()


def scatter_scratch(depth, r, columns, cut):
    return [
        pltpu.VMEM((2, depth, 2, r, columns), LOW),
        pltpu.VMEM((2, depth, 2, r, columns), LOW),
        pltpu.VMEM((depth, r, cut), LOW),
        pltpu.VMEM((depth, r, columns - cut), LOW),
        pltpu.VMEM((depth, r, columns), LOW),
        pltpu.VMEM((depth, r, columns), LOW),
        pltpu.VMEM((depth - 1, r, columns), LOW),
    ]


class HandOver:
    def __init__(self, links, source, target, send, recv, base, local):
        self.links, self.source, self.target, self.local = links, source, target, local
        self.send = lambda k: send.at[base + k]
        self.recv = lambda k: recv.at[base + k]
        self.half = source.shape[1]

    def rows(self, c):
        return self.target.at[pl.ds(c * self.half, self.half)]

    def copies(self):
        n = self.links
        near, far = self.source.at[n.x], self.source.at[1 - n.x]
        mine = self.rows(n.c)
        return (
            pltpu.make_async_copy(near, mine, self.local),
            remote(far, mine, self.send(0), self.recv(0), n.across),
            remote(near, mine, self.send(1), self.recv(1), n.sibling),
            remote(far, mine, self.send(2), self.recv(2), n.corner),
        )

    def begin(self):
        n = self.links
        keep, across, sibling, corner = self.copies()

        @pl.when(n.x == n.c)
        def _():
            keep.start()
            across.start()

        @pl.when(n.x != n.c)
        def _():
            sibling.start()
            corner.start()

    def finish(self):
        n = self.links
        keep, across, sibling, corner = self.copies()
        mine, theirs = self.rows(n.c), self.rows(1 - n.c)

        @pl.when(n.x == n.c)
        def _():
            keep.wait()
            across.wait_send()
            remote(theirs, theirs, self.send(1), self.recv(1), n.sibling).wait_recv()

        @pl.when(n.x != n.c)
        def _():
            sibling.wait_send()
            corner.wait_send()
            remote(mine, mine, self.send(0), self.recv(0), n.across).wait_recv()
            remote(theirs, theirs, self.send(2), self.recv(2), n.corner).wait_recv()


def scatter_kernel(depth, cuts, lo_in, dx_in, o_part, m_part, q_part,
                   lo_out, dx_out, o_out, m_out, q_out, *scratch):
    bufs = [scratch[7 * k : 7 * k + 7] for k in range(3)]
    dx_own, dx_other, send, recv, local, extra_send, extra_recv = scratch[21:]
    n = Links(depth)
    n.meet()
    spread_out = remote(
        dx_in.at[1 - n.c], dx_other, extra_send.at[6], extra_recv.at[6], n.sibling
    )
    spread_out.start()
    spread_own = pltpu.make_async_copy(dx_in.at[n.c], dx_own, local.at[3])
    spread_own.start()
    scatters = [
        Scatter(n, part, cut, whole, buf, out, send, recv, k, local.at[k])
        for k, (part, out, cut, whole, buf) in enumerate(
            zip(
                (o_part, m_part, q_part), (o_out, m_out, q_out), cuts, (True, True, False), bufs
            )
        )
    ]
    for item in scatters:
        item.begin()
    spread_own.wait()
    spread_out.wait_recv()
    for h in range(2):
        dx_own[h] = plus(dx_own[h], dx_other[h])
    lo_over = HandOver(n, lo_in, lo_out, extra_send, extra_recv, 0, local.at[4])
    dx_over = HandOver(n, dx_own, dx_out, extra_send, extra_recv, 3, local.at[5])
    dx_over.begin()
    lo_over.begin()
    for item in scatters:
        item.first()
    for item in scatters:
        item.second()
    for item in scatters:
        item.third()
    for item in scatters:
        item.fourth()
    for item in scatters:
        item.close()
    spread_out.wait_send()
    lo_over.finish()
    dx_over.finish()


def scatter_call(depth, cuts, lo, dx, o_part, m_part, q_part):
    r = o_part.shape[-2]
    half, part = lo.shape[1:]
    widths = [item.shape[-1] for item in (o_part, m_part, q_part)]
    scratch = []
    for columns, cut in zip(widths, cuts):
        scratch += scatter_scratch(depth, r, columns, cut)
    vmem = pl.BlockSpec(memory_space=pltpu.VMEM)
    return pl.pallas_call(
        functools.partial(scatter_kernel, depth, cuts),
        out_shape=[jax.ShapeDtypeStruct((2 * half, part), LOW)] * 2
        + [jax.ShapeDtypeStruct((r, columns), WIDE) for columns in widths],
        in_specs=[ANY] * 5,
        out_specs=[ANY] * 2 + [vmem] * 3,
        scratch_shapes=scratch
        + [
            pltpu.VMEM((2, half, part), LOW),
            pltpu.VMEM((2, half, part), LOW),
            pltpu.SemaphoreType.DMA((3, scatter_marks(depth))),
            pltpu.SemaphoreType.DMA((3, scatter_marks(depth))),
            pltpu.SemaphoreType.DMA((6,)),
            pltpu.SemaphoreType.DMA((7,)),
            pltpu.SemaphoreType.DMA((7,)),
        ],
        compiler_params=pltpu.CompilerParams(
            collective_id=1, has_side_effects=True, vmem_limit_bytes=56 * MEGA
        ),
        name="scatter",
    )(lo, dx, o_part, m_part, q_part)


def angle_tables():
    rates = THETA ** (-np.arange(HEAD_DIM // 2) / (HEAD_DIM // 2))
    rates = np.tile(rates, 4)[None]
    base = np.arange(BLOCK)[:, None] * rates
    jump = np.arange(SPAN)[:, None] * BLOCK * rates
    base = np.concatenate([np.cos(base), np.sin(base)], axis=0)
    jump = np.concatenate([np.cos(jump), np.sin(jump), np.zeros((2, 128))], axis=0)
    return jnp.asarray(base, WIDE), jnp.asarray(jump, WIDE)


def lanes(rows):
    return lax.broadcasted_iota(jnp.int32, (rows, 128), 1)


def turn_parts(meta, base, jump, block):
    offset = meta[0, SPAN + block]
    far_cos = jump[pl.ds(offset, 1), :]
    far_sin = jump[pl.ds(SPAN + offset, 1), :]
    near_cos, near_sin = base[0:BLOCK], base[BLOCK : 2 * BLOCK]
    cosine = near_cos * far_cos - near_sin * far_sin
    sine = near_sin * far_cos + near_cos * far_sin
    low = (lanes(BLOCK) % HEAD_DIM) < HEAD_DIM // 2
    return cosine, jnp.where(low, -sine, sine), low


def turn(values, cosine, sine, low):
    swapped = jnp.where(low, pltpu.roll(values, 96, 1), pltpu.roll(values, 32, 1))
    return values * cosine + swapped * sine


def weight_loads(full, h, flat, marks):
    depth, r = full.shape[1], full.shape[4]
    return [
        pltpu.make_async_copy(
            full.at[h, q, y, c], flat.at[pl.ds(k * r, r)], marks.at[k]
        )
        for k, (q, y, c) in enumerate(
            (q, y, c) for q in range(depth) for y in range(2) for c in range(2)
        )
    ]


def forward_kernel(depth, cuts, note_in, gain_in, cot_in, in_ref, q_own, m_own, o_own, base, jump,
                   note, gain, cot, rows, q_full, m_full, o_full, all_context, q_ref, k_ref, v_ref,
                   p_ref, r_ref, c_ref, marks, meta, held, weight, piece, send, recv, local, extra_send,
                   extra_recv, context_send, context_recv):
    step = pl.program_id(0)
    scale = HEAD_DIM ** (-0.5)
    n = Links(depth)
    half = in_ref.shape[0] // 2
    gathers = [
        Gather(n, own, full, cut, whole, send, recv, k, local.at[k])
        for k, (own, full, cut, whole) in enumerate(
            zip((q_own, m_own, o_own), (q_full, m_full, o_full), cuts, (False, True, True))
        )
    ]
    share = Share(
        n, in_ref, rows, cot_in, cot, note_in, note, gain_in, gain, extra_send, extra_recv,
        local.at[pl.ds(3, 4)],
    )

    def context_copy(p):
        there = c_ref.at[p, pl.ds((1 - n.c) * half, half)]
        return remote(there, all_context.at[n.c, p], context_send.at[p], context_recv.at[p], n.sibling)

    def context_keep(p):
        here = c_ref.at[p, pl.ds(n.c * half, half)]
        return pltpu.make_async_copy(here, all_context.at[n.c, p], local.at[10 + p])

    @pl.when(step == 0)
    def _():
        n.meet()
        share.begin()
        gathers[0].begin()
        for k in range(1, depth):
            gathers[0].second(k)
        for k in range(depth):
            gathers[0].third(k)
        gathers[1].begin()
        share.further()
        loads = [
            pltpu.make_async_copy(rows, held, local.at[7]),
            pltpu.make_async_copy(note, meta, local.at[8]),
        ]
        for item in loads:
            item.start()
        gathers[0].fourth()
        gathers[0].finish()
        loads += weight_loads(q_full, n.c, weight, piece)
        for item in loads[2:]:
            item.start()
        for item in loads:
            item.wait()

    hooks = {
        1: [gathers[2].begin],
        2: [functools.partial(gathers[1].second, k) for k in range(1, depth)],
        5: [functools.partial(gathers[1].third, k) for k in range(depth)],
        6: [functools.partial(gathers[2].second, k) for k in range(1, depth)] + [share.later],
        8: [gathers[1].fourth],
        9: [functools.partial(gathers[2].third, k) for k in range(depth)],
    }
    for at, actions in hooks.items():

        @pl.when(step == at)
        def _():
            for action in actions:
                action()

    @pl.when(step < SPAN)
    def _():
        here = pl.ds(step * BLOCK, BLOCK)
        cosine, sine, low = turn_parts(meta, base, jump, step)
        values = jnp.concatenate([held[0, here], held[1, here]], axis=1)

        for p in range(3):
            made = contract(values, weight[:, p * 384 : p * 384 + 384], 1, 0)
            q_ref[p, here] = (turn(made[:, 0:128], cosine, sine, low) * scale).astype(LOW)
            k_ref[p, here] = turn(made[:, 128:256], cosine, sine, low).astype(LOW)
            v_ref[p, here] = made[:, 256:384].astype(LOW)
        marks[here] = (lanes(BLOCK) == meta[0, step]).astype(WIDE).astype(LOW)

    @pl.when(step >= SPAN)
    def _():
        turn_number = step - SPAN
        p = turn_number // SPAN
        i = turn_number % SPAN
        here = pl.ds(i * BLOCK, BLOCK)
        lane = lanes(BLOCK)
        queries = q_ref[p, here]
        values = v_ref[p]
        keys = jnp.concatenate([k_ref[p], marks[...]], axis=1)
        barred = jnp.where((lane < SPAN) & (lane != meta[0, i]), NEGATIVE, 0.0).astype(LOW)
        outs = []
        scales = []
        for head in range(2):
            chosen = (lane // HEAD_DIM) == head
            ours = jnp.concatenate([jnp.where(chosen, queries, 0).astype(LOW), barred], axis=1)
            scores = contract(ours, keys, 1, 1)
            top = jnp.max(scores, axis=1, keepdims=True)
            raised = jnp.exp(scores - top)
            inverse = 1.0 / jnp.sum(raised, axis=1, keepdims=True)
            soft = raised.astype(LOW)
            p_ref[0, head] = soft
            outs.append(contract(soft, values, 1, 0))
            scales.append(inverse)
        inverse = jnp.where(lane < HEAD_DIM, scales[0], scales[1])
        r_ref[p, here] = inverse
        c_ref[p, here] = (jnp.where(lane < HEAD_DIM, outs[0], outs[1]) * inverse).astype(LOW)

    for p in range(3):

        @pl.when(step == 2 * SPAN - 1 + p * SPAN)
        def _():
            context_copy(p).start()
            context_keep(p).start()

    @pl.when(step == 4 * SPAN - 1)
    def _():
        gathers[2].fourth()
        gathers[1].finish()
        gathers[2].finish()
        for item in gathers:
            item.close()
        share.finish()
        for p in range(3):
            context_copy(p).wait()
            context_keep(p).wait()


def forward_call(depth, cuts, note, gain, cot, rows, q_own, m_own, o_own, base, jump):
    length, part = rows.shape
    half = length // 2
    r = q_own.shape[0]
    low = lambda *shape: jax.ShapeDtypeStruct(shape, LOW)
    full = [low(2, depth, 2, 2, r, own.shape[1]) for own in (q_own, m_own, o_own)]
    trio = low(3, length, 128)
    vmem = pl.BlockSpec(memory_space=pltpu.VMEM)
    marks = pltpu.SemaphoreType.DMA((3, gather_marks(depth)))
    return pl.pallas_call(
        functools.partial(forward_kernel, depth, cuts),
        grid=(SPAN + 3 * SPAN,),
        out_shape=[
            jax.ShapeDtypeStruct(note.shape, note.dtype),
            jax.ShapeDtypeStruct((2,) + gain.shape, WIDE),
            low(2, half, part),
            low(2, length, part),
        ]
        + full
        + [
            low(2, 3, half, 128),
            trio,
            trio,
            trio,
            low(SPAN * 3, 2, BLOCK, length),
            jax.ShapeDtypeStruct((3, length, 128), WIDE),
            trio,
        ],
        in_specs=[ANY] * 7 + [vmem] * 2,
        out_specs=[ANY] * 8
        + [vmem] * 3
        + [
            pl.BlockSpec((1, 2, BLOCK, length), lambda s: (jnp.maximum(s - SPAN, 0), 0, 0, 0)),
            vmem,
            vmem,
        ],
        scratch_shapes=[
            pltpu.VMEM((length, 128), LOW),
            pltpu.SMEM(note.shape, note.dtype),
            pltpu.VMEM((2, length, part), LOW),
            pltpu.VMEM((4 * depth * r, q_own.shape[1]), LOW),
            pltpu.SemaphoreType.DMA((4 * depth,)),
            marks,
            marks,
            pltpu.SemaphoreType.DMA((13,)),
            pltpu.SemaphoreType.DMA((8,)),
            pltpu.SemaphoreType.DMA((8,)),
            pltpu.SemaphoreType.DMA((3,)),
            pltpu.SemaphoreType.DMA((3,)),
        ],
        compiler_params=pltpu.CompilerParams(
            collective_id=0, has_side_effects=True, vmem_limit_bytes=60 * MEGA
        ),
        name="attend",
    )(note, gain, cot, rows, q_own, m_own, o_own, base, jump)


def norm_of(summed):
    mean = jnp.mean(summed, axis=1, keepdims=True)
    centred = summed - mean
    variance = jnp.mean(centred * centred, axis=1, keepdims=True)
    scale = lax.rsqrt(variance + EPSILON)
    return centred * scale, scale


def norm_back(scaled, normed, scale):
    total = jnp.mean(scaled, axis=1, keepdims=True)
    cross = jnp.mean(scaled * normed, axis=1, keepdims=True)
    return scale * (scaled - total - normed * cross)


HIDDEN = 512


def middle_kernel(context, rows, cot, m_full, o_full, gains, lo_ref, gc_ref, act_ref, gi_ref, fl_ref,
                  gm_ref, ga_ref, gfs_ref, sums, slopes):
    tile = rows.shape[1]
    part = rows.shape[2]
    pieces = o_full.shape[2] // HIDDEN
    whole = jnp.concatenate([gains[0], gains[1]], axis=1)
    gain1, bias1, gain2, bias2 = (whole[k : k + 1, :] for k in range(4))
    summed = jnp.concatenate([rows[0], rows[1]], axis=1).astype(WIDE)
    for h in range(2):
        seen = jnp.concatenate([context[h, p] for p in range(3)], axis=1)
        summed = summed + contract(seen, m_full[h, :, 0:part], 1, 1)
    normed1, scale1 = norm_of(summed)
    first = normed1 * gain1 + bias1
    first_low = first.astype(LOW)
    fl_ref[...] = first_low
    mixed = jnp.zeros(first.shape, WIDE)
    for h in range(2):
        for j in range(pieces):
            k = h * pieces + j
            lo_end = part + j * HIDDEN
            inner = contract(first_low, m_full[h, :, lo_end : lo_end + HIDDEN], 1, 0)
            share = 0.5 * (1.0 + lax.erf(inner * ROOT_HALF))
            slopes[:, k * HIDDEN : (k + 1) * HIDDEN] = (
                share + inner * jnp.exp(-0.5 * inner * inner) * INVERSE_ROOT
            )
            act_ref[:, k * HIDDEN : (k + 1) * HIDDEN] = (inner * share).astype(LOW)
    for h in range(2):
        width = pieces * HIDDEN
        mixed = mixed + contract(act_ref[:, h * width : (h + 1) * width], o_full[h], 1, 1)
    normed2, scale2 = norm_of(first + mixed)
    result = (normed2 * gain2 + bias2).astype(LOW)
    for h in range(2):
        lo_ref[h] = result[:, h * part : (h + 1) * part]
    cotangent = jnp.concatenate([cot[0], cot[1]], axis=1).astype(WIDE)
    second_gain = jnp.sum(cotangent * normed2, axis=0, keepdims=True)
    second_bias = jnp.sum(cotangent, axis=0, keepdims=True)
    grad_second = norm_back(cotangent * gain2, normed2, scale2)
    grad_mixed = grad_second.astype(LOW)
    gm_ref[...] = grad_mixed
    for h in range(2):
        for j in range(pieces):
            k = h * pieces + j
            raised = contract(grad_mixed, o_full[h, :, j * HIDDEN : (j + 1) * HIDDEN], 1, 0)
            gi_ref[:, k * HIDDEN : (k + 1) * HIDDEN] = (
                raised * slopes[:, k * HIDDEN : (k + 1) * HIDDEN]
            ).astype(LOW)
    grad_first = grad_second
    for h in range(2):
        width = pieces * HIDDEN
        grad_first = grad_first + contract(
            gi_ref[:, h * width : (h + 1) * width], m_full[h, :, part : part + width], 1, 1
        )
    first_gain = jnp.sum(grad_first * normed1, axis=0, keepdims=True)
    first_bias = jnp.sum(grad_first, axis=0, keepdims=True)
    grad_sum = norm_back(grad_first * gain1, normed1, scale1)
    gfs_ref[...] = grad_sum
    grad_attended = grad_sum.astype(LOW)
    ga_ref[...] = grad_attended
    for h in range(2):
        gc_ref[h] = contract(grad_attended, m_full[h, :, 0:part], 1, 0).astype(LOW)
    found = jnp.concatenate([first_gain, first_bias, second_gain, second_bias], axis=0)

    @pl.when(pl.program_id(0) == 0)
    def _():
        sums[...] = found

    @pl.when(pl.program_id(0) > 0)
    def _():
        sums[...] += found


def middle_call(context, rows, cot, m_full, o_full, gains):
    tile = 256
    half, part = rows.shape[1:]
    width = 2 * part
    hidden = 2 * o_full.shape[2]
    vmem = pl.BlockSpec(memory_space=pltpu.VMEM)
    split = pl.BlockSpec((2, tile, part), lambda i: (0, i, 0))
    flat = pl.BlockSpec((tile, width), lambda i: (i, 0))
    wide = pl.BlockSpec((tile, hidden), lambda i: (i, 0))
    low = lambda *shape: jax.ShapeDtypeStruct(shape, LOW)
    return pl.pallas_call(
        middle_kernel,
        grid=(half // tile,),
        out_shape=[
            low(2, half, part),
            low(2, half, part),
            low(half, hidden),
            low(half, hidden),
            low(half, width),
            low(half, width),
            low(half, width),
            jax.ShapeDtypeStruct((half, width), WIDE),
            jax.ShapeDtypeStruct((4, width), WIDE),
        ],
        in_specs=[
            pl.BlockSpec((2, 3, tile, 128), lambda i: (0, 0, i, 0)),
            split,
            split,
            vmem,
            vmem,
            vmem,
        ],
        out_specs=[
            split,
            split,
            wide,
            wide,
            flat,
            flat,
            flat,
            flat,
            pl.BlockSpec((4, width), lambda i: (0, 0)),
        ],
        scratch_shapes=[pltpu.VMEM((tile, hidden), WIDE)],
        compiler_params=pltpu.CompilerParams(vmem_limit_bytes=60 * MEGA),
        name="middle",
    )(context, rows, cot, m_full, o_full, gains)


def backward_kernel(core, meta, base, jump, soft, grads, context, inverse, q_ref, k_ref, v_ref, rows,
                    weight, kept, part_ref, dx_ref, ones, keys_sum, values_sum, made):
    step = pl.program_id(0)
    p = step // SPAN
    i = step % SPAN
    length = q_ref.shape[1]
    scale = HEAD_DIM ** (-0.5)
    lane = lanes(BLOCK)
    here = pl.ds(i * BLOCK, BLOCK)

    @pl.when(step == 0)
    def _():
        ones[...] = (lanes(length) < 2).astype(WIDE).astype(LOW)

    grad = grads[p, here].astype(WIDE)
    turned = grad * inverse[p, here]
    both = turned * context[p, here].astype(WIDE)
    turned_low = turned.astype(LOW)
    queries = q_ref[p, here]
    keys = k_ref[p]
    values = jnp.concatenate([v_ref[p], ones[...]], axis=1)
    turned_flip = jnp.transpose(turned).astype(LOW)
    queries_flip = jnp.transpose(queries.astype(WIDE)).astype(LOW)
    outs = []
    for head in range(2):
        chosen = (lane // HEAD_DIM) == head
        centre = -jnp.sum(jnp.where(chosen, both, 0.0), axis=1, keepdims=True)
        coarse = centre.astype(LOW).astype(WIDE)
        fine = jnp.where(lane == 0, coarse, jnp.where(lane == 1, centre - coarse, 0.0))
        ours = jnp.concatenate(
            [jnp.where(chosen, turned_low, 0).astype(LOW), fine.astype(LOW)], axis=1
        )
        raised = soft[0, head]
        scores = (contract(ours, values, 1, 1) * raised.astype(WIDE)).astype(LOW)
        outs.append(contract(scores, keys, 1, 0))
        mine = slice(head * HEAD_DIM, (head + 1) * HEAD_DIM)
        values_add = contract(turned_flip[mine], raised, 1, 0)
        keys_add = contract(queries_flip[mine], scores, 1, 0)

        @pl.when(i == 0)
        def _():
            values_sum[mine] = values_add
            keys_sum[mine] = keys_add

        @pl.when(i > 0)
        def _():
            values_sum[mine] += values_add
            keys_sum[mine] += keys_add

    cosine, sine, low = turn_parts(meta, base, jump, i)
    grad_queries = jnp.where(lane < HEAD_DIM, outs[0], outs[1]) * scale
    made[p, here, 0:128] = turn(grad_queries, cosine, -sine, low).astype(LOW)

    @pl.when(i == SPAN - 1)
    def _():
        grad_keys = jnp.transpose(keys_sum[...])
        grad_values = jnp.transpose(values_sum[...])
        for b in range(SPAN):
            there = slice(b * BLOCK, (b + 1) * BLOCK)
            cosine, sine, low = turn_parts(meta, base, jump, b)
            made[p, there, 128:256] = turn(grad_keys[there], cosine, -sine, low).astype(LOW)
        made[p, :, 256:384] = grad_values.astype(LOW)
        for h in range(2):
            part = rows.shape[2]
            part_ref[p, h * part : (h + 1) * part] = contract(rows[h], made[p], 0, 0).astype(LOW)

    @pl.when(step == 3 * SPAN - 1)
    def _():
        half = kept.shape[0]
        part = rows.shape[2]
        for other in range(2):
            c = core[0] if other == 0 else 1 - core[0]
            there = pl.ds(c * half, half)
            gained = kept[...] if other == 0 else jnp.zeros(kept.shape, WIDE)
            for pair in range(3):
                gained = gained + contract(made[pair, there], weight[:, pair * 384 : pair * 384 + 384], 1, 1)
            for h in range(2):
                dx_ref[c, h] = gained[:, h * part : (h + 1) * part].astype(LOW)


def backward_call(core, meta, base, jump, soft, grads, context, inverse, q, k, v, rows, weight, kept):
    length = q.shape[1]
    half, width = kept.shape
    part = width // 2
    vmem = pl.BlockSpec(memory_space=pltpu.VMEM)
    smem = pl.BlockSpec(memory_space=pltpu.SMEM)
    return pl.pallas_call(
        backward_kernel,
        grid=(3 * SPAN,),
        out_shape=[
            jax.ShapeDtypeStruct((3, width, 384), LOW),
            jax.ShapeDtypeStruct((2, 2, half, part), LOW),
        ],
        in_specs=[smem, smem, vmem, vmem, pl.BlockSpec((1, 2, BLOCK, length), lambda s: (s, 0, 0, 0))]
        + [vmem] * 9,
        out_specs=[vmem, vmem],
        scratch_shapes=[
            pltpu.VMEM((length, 128), LOW),
            pltpu.VMEM((128, length), WIDE),
            pltpu.VMEM((128, length), WIDE),
            pltpu.VMEM((3, length, 384), LOW),
        ],
        compiler_params=pltpu.CompilerParams(vmem_limit_bytes=60 * MEGA),
        name="attend_back",
    )(core, meta, base, jump, soft, grads, context, inverse, q, k, v, rows, weight, kept)


def swap_back(values, half, c):
    n_wide = lax.axis_size("wide")
    mine = lax.dynamic_index_in_dim(values, c, 0, keepdims=False)
    theirs = lax.dynamic_index_in_dim(values, 1 - c, 0, keepdims=False)
    got = lax.ppermute(theirs, "wide", [(w, w ^ 1) for w in range(n_wide)])
    whole = jnp.where(c == 0, jnp.concatenate([mine, got]), jnp.concatenate([got, mine]))
    return jnp.moveaxis(whole.reshape(whole.shape[0], -1, 128), 1, 0)


def owned(
    inputs,
    block_segment,
    query_weight,
    key_weight,
    value_weight,
    output_weight,
    inner_weight,
    outer_weight,
    first_gain,
    first_bias,
    second_gain,
    second_bias,
    output_cotangent,
):
    wide = lax.axis_size("wide")
    depth = wide // 4
    r = query_weight.shape[0]
    part = query_weight.shape[1]
    length = inputs.shape[0]
    half = length // 2
    x, w, c, _, _ = place()
    pairs = part // 128
    q_own = jnp.concatenate(
        [
            item[:, p * 128 : (p + 1) * 128]
            for p in range(pairs)
            for item in (query_weight, key_weight, value_weight)
        ],
        axis=1,
    )
    m_own = jnp.concatenate([output_weight.T, inner_weight], axis=1)
    o_own = outer_weight.T
    earlier = jnp.sum((block_segment[None, :] < block_segment[:, None]).astype(jnp.int32), axis=1)
    offsets = jnp.arange(SPAN, dtype=jnp.int32) - earlier
    meta = jnp.zeros((1, 128), jnp.int32)
    meta = meta.at[0, 0:SPAN].set(block_segment).at[0, SPAN : 2 * SPAN].set(offsets)
    widths = [item.shape[1] for item in (q_own, m_own, o_own)]
    cuts = [(item // 128 // 5) * 128 for item in widths]
    gains = jnp.stack([first_gain, first_bias, second_gain, second_bias])
    gains = jnp.concatenate([gains, gains], axis=0)
    base, jump = angle_tables()
    meta, gains, cot, rows, q_full, m_full, o_full, pairs_context, q, k, v, soft, inverse, context = (
        forward_call(
            depth, cuts, meta, gains, output_cotangent, inputs, q_own, m_own, o_own, base, jump
        )
    )
    weight = lax.dynamic_index_in_dim(q_full, c, 0, keepdims=False).reshape(2 * part, widths[0])
    m_full = m_full.reshape(2, 2 * part, widths[1])
    o_full = o_full.reshape(2, 2 * part, widths[2])
    own_rows = lax.dynamic_slice_in_dim(rows, c * half, half, axis=1)
    lo, gc, act, gi, fl, gm, ga, kept, sums = middle_call(
        pairs_context, own_rows, cot, m_full, o_full, gains
    )
    all_context = jnp.moveaxis(pairs_context, 1, 2).reshape(2, half, part)
    hidden = act.shape[1] // 2
    o_part = jnp.stack(
        [left_transposed(gm, act[:, h * hidden : (h + 1) * hidden]).astype(LOW) for h in range(2)]
    )
    m_part = jnp.stack(
        [
            jnp.concatenate(
                [
                    left_transposed(ga, all_context[h]).astype(LOW),
                    left_transposed(fl, gi[:, h * hidden : (h + 1) * hidden]).astype(LOW),
                ],
                axis=1,
            )
            for h in range(2)
        ]
    )
    grads = swap_back(gc, half, c)
    core = jnp.reshape(c, (1,)).astype(jnp.int32)
    q_part, dx = backward_call(
        core, meta, base, jump, soft, grads, context, inverse, q, k, v, rows, weight, kept
    )
    q_part = jnp.moveaxis(q_part, 0, 1)
    q_part = q_part.reshape(depth, 2, 2, r, widths[0])
    m_part = m_part.reshape(2, depth, 2, 2, r, widths[1])
    o_part = o_part.reshape(2, depth, 2, 2, r, widths[2])
    layer_output, input_gradient, o_sum, m_sum, q_sum = scatter_call(
        depth, [cuts[2], cuts[1], cuts[0]], lo, dx, o_part, m_part, q_part
    )
    q_sum = q_sum.reshape(r, pairs, 3, 128)
    sums = lax.psum_scatter(sums, ("narrow", "wide"), scatter_dimension=1, tiled=True)
    return (
        layer_output,
        input_gradient,
        q_sum[:, :, 0].reshape(r, part),
        q_sum[:, :, 1].reshape(r, part),
        q_sum[:, :, 2].reshape(r, part),
        m_sum[:, 0:part].T,
        m_sum[:, part:],
        o_sum.T,
        sums[0],
        sums[1],
        sums[2],
        sums[3],
    )


def program(*arrays):
    rows = arrays[2].shape[0]
    whole = rows % 16 == 0 and lax.axis_size("narrow") == 2 and lax.axis_size("wide") % 4 == 0
    return owned(*arrays) if whole else shards(*arrays)


def solution(mesh):
    placed = (
        P("wide", "narrow"),
        P("wide"),
        P("wide", "narrow"),
        P("wide", "narrow"),
        P("wide", "narrow"),
        P("narrow", "wide"),
        P("wide", "narrow"),
        P("narrow", "wide"),
        P("narrow"),
        P("narrow"),
        P("narrow"),
        P("narrow"),
        P("wide", "narrow"),
    )
    return jax.shard_map(
        program,
        mesh=mesh,
        in_specs=placed,
        out_specs=(
            P("wide", "narrow"),
            P("wide", "narrow"),
            P("wide", "narrow"),
            P("wide", "narrow"),
            P("wide", "narrow"),
            P("narrow", "wide"),
            P("wide", "narrow"),
            P("narrow", "wide"),
            P(("narrow", "wide")),
            P(("narrow", "wide")),
            P(("narrow", "wide")),
            P(("narrow", "wide")),
        ),
        check_vma=False,
    )
```

```python
import functools

import jax
import jax.numpy as jnp
import numpy as np
from jax import lax
from jax.experimental import pallas as pl
from jax.experimental.pallas import tpu as pltpu
from jax.sharding import PartitionSpec as P

HEAD_DIM = 64
BLOCK = 512
SPAN = 3


EPSILON = 1e-06
NEGATIVE = -1e30
THETA = 10000.0
ROOT_HALF = 0.7071067811865476
INVERSE_ROOT = 0.3989422804014327


def product(left, right):
    return jnp.dot(left, right, preferred_element_type=jnp.float32)


def left_transposed(left, right):
    return lax.dot_general(
        left, right, (((0,), (0,)), ((), ())), preferred_element_type=jnp.float32
    )


def right_transposed(left, right):
    return lax.dot_general(
        left, right, (((1,), (1,)), ((), ())), preferred_element_type=jnp.float32
    )


def whole_features(values):
    return lax.all_gather(values, "narrow", axis=1, tiled=True)


def feature_sums(values):
    return lax.psum_scatter(
        values.astype(jnp.bfloat16), "narrow", scatter_dimension=1, tiled=True
    ).astype(jnp.float32)


def moments(first_sum, second_sum):
    return lax.psum((first_sum, second_sum), "narrow")


def gelu_value(values):
    return 0.5 * values * (1.0 + lax.erf(values * ROOT_HALF))


def gelu_slope(values):
    return (
        0.5 * (1.0 + lax.erf(values * ROOT_HALF))
        + values * jnp.exp(-0.5 * values * values) * INVERSE_ROOT
    )


def rotate(values, cosine, sine):
    half = values.shape[-1] // 2
    first = values[..., :half]
    second = values[..., half:]
    return jnp.concatenate(
        [first * cosine - second * sine, second * cosine + first * sine], axis=-1
    )


def rotate_back(values, cosine, sine):
    half = values.shape[-1] // 2
    first = values[..., :half]
    second = values[..., half:]
    return jnp.concatenate(
        [first * cosine + second * sine, second * cosine - first * sine], axis=-1
    )


def tables(block_segment):
    segment = block_segment.reshape(-1, SPAN)
    earlier = jnp.sum((segment[:, None, :] < segment[:, :, None]).astype(jnp.int32), axis=2)
    offsets = (jnp.arange(SPAN, dtype=jnp.int32)[None, :] - earlier) * BLOCK
    positions = (
        (offsets[:, :, None] + jnp.arange(BLOCK, dtype=jnp.int32)[None, None, :])
        .reshape(-1)
        .astype(jnp.float32)
    )
    half = HEAD_DIM // 2
    rates = THETA ** (-jnp.arange(half, dtype=jnp.float32) / half)
    angle = positions[:, None] * rates[None, :]
    labels = jnp.repeat(segment, BLOCK, axis=1)
    return (jnp.cos(angle)[:, None, :], jnp.sin(angle)[:, None, :], labels)


def normalize(summed, gain, bias, width):
    total, squares = moments(jnp.sum(summed, axis=1), jnp.sum(summed * summed, axis=1))
    mean = total / width
    reciprocal = lax.rsqrt(squares / width - mean * mean + EPSILON)
    normed = (summed - mean[:, None]) * reciprocal[:, None]
    return (normed * gain + bias, normed, reciprocal)


def normalize_back(grad, normed, reciprocal, gain, width):
    scaled = grad * gain
    total, cross = moments(jnp.sum(scaled, axis=1), jnp.sum(scaled * normed, axis=1))
    return reciprocal[:, None] * (scaled - total[:, None] / width - normed * cross[:, None] / width)


def block_scores(block_queries, group_keys, block_labels, group_labels, factor):
    scores = (
        jnp.einsum("qhd,khd->hqk", block_queries, group_keys, preferred_element_type=jnp.float32)
        * factor
    )
    same = block_labels[:, None] == group_labels[None, :]
    return jnp.where(same[None], scores, NEGATIVE)


def attention_forward(queries, keys, values, labels, factor):
    groups, length = labels.shape
    shape = (groups, length) + queries.shape[1:]

    def one_group(items):
        group_queries, group_keys, group_values, group_labels = items
        contexts = []
        totals = []
        for index in range(length // BLOCK):
            low_end = index * BLOCK
            high_end = low_end + BLOCK
            scores = block_scores(
                group_queries[low_end:high_end],
                group_keys,
                group_labels[low_end:high_end],
                group_labels,
                factor,
            )
            top = jnp.max(scores, axis=2, keepdims=True)
            raised = jnp.exp(scores - top)
            summed = jnp.sum(raised, axis=2, keepdims=True)
            soft = (raised / summed).astype(jnp.bfloat16)
            contexts.append(
                jnp.einsum("hqk,khd->qhd", soft, group_values, preferred_element_type=jnp.float32)
            )
            totals.append((top + jnp.log(summed))[..., 0])
        return (jnp.concatenate(contexts, axis=0), jnp.concatenate(totals, axis=1))

    contexts, totals = lax.map(
        one_group, (queries.reshape(shape), keys.reshape(shape), values.reshape(shape), labels)
    )
    return (contexts.reshape(queries.shape), totals)


def attention_backward(queries, keys, values, totals, grad_context, labels, factor):
    groups, length = labels.shape
    shape = (groups, length) + queries.shape[1:]

    def one_group(items):
        group_queries, group_keys, group_values, group_totals, group_grads, group_labels = items
        keys_grad = jnp.zeros(group_keys.shape, jnp.float32)
        values_grad = jnp.zeros(group_values.shape, jnp.float32)
        pieces = []
        for index in range(length // BLOCK):
            low_end = index * BLOCK
            high_end = low_end + BLOCK
            block_queries = group_queries[low_end:high_end]
            block_grads = group_grads[low_end:high_end]
            scores = block_scores(
                block_queries, group_keys, group_labels[low_end:high_end], group_labels, factor
            )
            soft = jnp.exp(scores - group_totals[:, low_end:high_end, None])
            inner = jnp.einsum(
                "qhd,khd->hqk", block_grads, group_values, preferred_element_type=jnp.float32
            )
            centre = jnp.sum(soft * inner, axis=2, keepdims=True)
            scores_grad = (soft * (inner - centre)).astype(jnp.bfloat16)
            pieces.append(
                jnp.einsum(
                    "hqk,khd->qhd", scores_grad, group_keys, preferred_element_type=jnp.float32
                )
                * factor
            )
            keys_grad = (
                keys_grad
                + jnp.einsum(
                    "hqk,qhd->khd", scores_grad, block_queries, preferred_element_type=jnp.float32
                )
                * factor
            )
            values_grad = values_grad + jnp.einsum(
                "hqk,qhd->khd",
                soft.astype(jnp.bfloat16),
                block_grads,
                preferred_element_type=jnp.float32,
            )
        return (jnp.concatenate(pieces, axis=0), keys_grad, values_grad)

    queries_grad, keys_grad, values_grad = lax.map(
        one_group,
        (
            queries.reshape(shape),
            keys.reshape(shape),
            values.reshape(shape),
            totals,
            grad_context.reshape(shape),
            labels,
        ),
    )
    return (
        queries_grad.reshape(queries.shape),
        keys_grad.reshape(queries.shape),
        values_grad.reshape(queries.shape),
    )


def shards(
    inputs,
    block_segment,
    query_weight,
    key_weight,
    value_weight,
    output_weight,
    inner_weight,
    outer_weight,
    first_gain,
    first_bias,
    second_gain,
    second_bias,
    output_cotangent,
):
    width = first_gain.shape[0] * lax.axis_size("narrow")
    tokens = inputs.shape[0]
    factor = HEAD_DIM ** (-0.5)
    cosine, sine, labels = tables(block_segment)
    full_inputs = whole_features(inputs)
    query_full, key_full, value_full, inner_full = (
        lax.all_gather(query_weight, "wide", axis=0, tiled=True),
        lax.all_gather(key_weight, "wide", axis=0, tiled=True),
        lax.all_gather(value_weight, "wide", axis=0, tiled=True),
        lax.all_gather(inner_weight, "wide", axis=0, tiled=True),
    )
    output_full, outer_full = (
        lax.all_gather(output_weight, "wide", axis=1, tiled=True),
        lax.all_gather(outer_weight, "wide", axis=1, tiled=True),
    )
    head_shape = (tokens, query_weight.shape[1] // HEAD_DIM, HEAD_DIM)
    queries = rotate(product(full_inputs, query_full).reshape(head_shape), cosine, sine).astype(
        jnp.bfloat16
    )
    keys = rotate(product(full_inputs, key_full).reshape(head_shape), cosine, sine).astype(
        jnp.bfloat16
    )
    values = product(full_inputs, value_full).astype(jnp.bfloat16).reshape(head_shape)
    context, totals = attention_forward(queries, keys, values, labels, factor)
    context_low = context.reshape(tokens, -1).astype(jnp.bfloat16)
    attended = feature_sums(product(context_low, output_full))
    first, first_normed, first_scale = normalize(
        inputs.astype(jnp.float32) + attended, first_gain, first_bias, width
    )
    first_low = first.astype(jnp.bfloat16)
    feed_rows = whole_features(first_low)
    inner = product(feed_rows, inner_full)
    activated = gelu_value(inner).astype(jnp.bfloat16)
    mixed = feature_sums(product(activated, outer_full))
    second, second_normed, second_scale = normalize(first + mixed, second_gain, second_bias, width)
    layer_output = second.astype(jnp.bfloat16)
    cotangent = output_cotangent.astype(jnp.float32)
    second_gain_grad = jnp.sum(cotangent * second_normed, axis=0)
    second_bias_grad = jnp.sum(cotangent, axis=0)
    grad_second = normalize_back(cotangent, second_normed, second_scale, second_gain, width)
    grad_mixed = grad_second.astype(jnp.bfloat16)
    grad_rows = whole_features(grad_mixed)
    grad_activated = right_transposed(grad_rows, outer_full)
    outer_grad = left_transposed(activated, grad_rows)
    grad_inner = (grad_activated * gelu_slope(inner)).astype(jnp.bfloat16)
    inner_grad = left_transposed(feed_rows, grad_inner)
    grad_first = grad_second + feature_sums(right_transposed(grad_inner, inner_full))
    first_gain_grad = jnp.sum(grad_first * first_normed, axis=0)
    first_bias_grad = jnp.sum(grad_first, axis=0)
    grad_first_sum = normalize_back(grad_first, first_normed, first_scale, first_gain, width)
    attended_rows = whole_features(grad_first_sum.astype(jnp.bfloat16))
    output_grad = left_transposed(context_low, attended_rows)
    grad_context = right_transposed(attended_rows, output_full).astype(jnp.bfloat16)
    queries_grad, keys_grad, values_grad = attention_backward(
        queries, keys, values, totals, grad_context.reshape(head_shape), labels, factor
    )
    queries_grad = rotate_back(queries_grad, cosine, sine).reshape(tokens, -1).astype(jnp.bfloat16)
    keys_grad = rotate_back(keys_grad, cosine, sine).reshape(tokens, -1).astype(jnp.bfloat16)
    values_grad = values_grad.reshape(tokens, -1).astype(jnp.bfloat16)
    query_grad = left_transposed(full_inputs, queries_grad)
    key_grad = left_transposed(full_inputs, keys_grad)
    value_grad = left_transposed(full_inputs, values_grad)
    spread = (
        right_transposed(queries_grad, query_full)
        + right_transposed(keys_grad, key_full)
        + right_transposed(values_grad, value_full)
    )
    input_gradient = (grad_first_sum + feature_sums(spread)).astype(jnp.bfloat16)
    (
        query_total,
        key_total,
        value_total,
        inner_total,
        first_gain_total,
        first_bias_total,
        second_gain_total,
        second_bias_total,
    ) = (
        lax.psum_scatter(query_grad, "wide", scatter_dimension=0, tiled=True),
        lax.psum_scatter(key_grad, "wide", scatter_dimension=0, tiled=True),
        lax.psum_scatter(value_grad, "wide", scatter_dimension=0, tiled=True),
        lax.psum_scatter(inner_grad, "wide", scatter_dimension=0, tiled=True),
        lax.psum_scatter(first_gain_grad, "wide", scatter_dimension=0, tiled=True),
        lax.psum_scatter(first_bias_grad, "wide", scatter_dimension=0, tiled=True),
        lax.psum_scatter(second_gain_grad, "wide", scatter_dimension=0, tiled=True),
        lax.psum_scatter(second_bias_grad, "wide", scatter_dimension=0, tiled=True),
    )
    output_total, outer_total = (
        lax.psum_scatter(output_grad, "wide", scatter_dimension=1, tiled=True),
        lax.psum_scatter(outer_grad, "wide", scatter_dimension=1, tiled=True),
    )
    return (
        layer_output,
        input_gradient,
        query_total,
        key_total,
        value_total,
        output_total,
        inner_total,
        outer_total,
        first_gain_total,
        first_bias_total,
        second_gain_total,
        second_bias_total,
    )


LOW = jnp.bfloat16
WIDE = jnp.float32
MESH = pl.DeviceIdType.MESH
MEGA = 1 << 20
ANY = pl.BlockSpec(memory_space=pl.ANY)


def contract(left, right, left_dim, right_dim):
    return lax.dot_general(
        left, right, (((left_dim,), (right_dim,)), ((), ())), preferred_element_type=WIDE
    )


def place():
    x = lax.axis_index("narrow")
    w = lax.axis_index("wide")
    c = lax.rem(w, 2)
    y = lax.rem(lax.div(w, 2), 2)
    q = lax.div(w, 4)
    return x, w, c, y, q


class Links:
    def __init__(self, depth):
        self.depth = depth
        self.x, self.w, self.c, self.y, self.q = place()
        self.across = (1 - self.x, self.w)
        self.beside = (self.x, self.w + 2 - 4 * self.y)
        self.sibling = (self.x, self.w + 1 - 2 * self.c)
        self.corner = (1 - self.x, self.w + 1 - 2 * self.c)

    def far(self, step):
        return (self.x, lax.rem(self.w + 4 * step, 4 * self.depth))

    def row(self, step):
        return lax.rem(self.q + self.depth - step, self.depth)

    def meet(self, chip_only=False):
        barrier = pltpu.get_barrier_semaphore()
        others = [self.sibling]
        if not chip_only:
            others += [self.across, self.beside, self.corner]
            others += [self.far(step) for step in range(1, self.depth)]
        for other in others:
            pl.semaphore_signal(barrier, 1, device_id=other, device_id_type=MESH)
        pl.semaphore_wait(barrier, len(others))


def remote(source, target, send, recv, device):
    return pltpu.make_async_remote_copy(
        src_ref=source,
        dst_ref=target,
        send_sem=send,
        recv_sem=recv,
        device_id=device,
        device_id_type=MESH,
    )


def gather_marks(depth):
    return 5 * depth + 2


class Gather:
    def __init__(self, links, own, full, cut, whole, send, recv, index, local):
        self.links, self.own, self.full, self.cut = links, own, full, cut
        self.whole, self.local = whole, local
        self.send = lambda k: send.at[index, k]
        self.recv = lambda k: recv.at[index, k]
        self.width = own.shape[-1]

    def slot(self, h, q, y):
        return self.full.at[h, q, y, self.links.c]

    def low(self, ref):
        return ref.at[:, pl.ds(0, self.cut)]

    def high(self, ref):
        return ref.at[:, pl.ds(self.cut, self.width - self.cut)]

    def copy(self, kind, step=0):
        n, d = self.links, self.links.depth
        mine = self.slot(n.x, n.q, n.y)
        column = self.slot(n.x, n.row(step), n.y)
        first = self.own if step == 0 else column
        if kind == "far":
            return self.move(self.own, mine, step - 1, n.far(step))
        if kind == "across":
            return self.move(first, column, d + step, n.across)
        if kind == "beside":
            return self.move(first, column, 2 * d + step, n.beside)
        if kind == "high":
            part = self.high(self.slot(1 - n.x, n.row(step), n.y))
            return self.move(part, part, 3 * d + step, n.beside)
        if kind == "low":
            part = self.low(self.slot(n.x, n.row(step), 1 - n.y))
            return self.move(part, part, 4 * d + step, n.across)
        part = self.full.at[step if self.whole else 1 - n.c, :, :, n.c]
        return self.move(part, part, 5 * d + step, n.sibling)

    def move(self, source, target, mark, device):
        return remote(source, target, self.send(mark), self.recv(mark), device)

    def arrived(self, target, mark):
        self.move(target, target, mark, self.links.sibling).wait_recv()

    def keep(self):
        n = self.links
        return pltpu.make_async_copy(self.own, self.slot(n.x, n.q, n.y), self.local)

    def begin(self):
        self.keep().start()
        self.copy("across").start()
        self.copy("beside").start()
        for step in range(1, self.links.depth):
            self.copy("far", step).start()

    def second(self, step):
        n = self.links
        self.arrived(self.slot(n.x, n.row(step), n.y), step - 1)
        self.copy("across", step).start()
        self.copy("beside", step).start()

    def third(self, step):
        n, d = self.links, self.links.depth
        self.arrived(self.slot(1 - n.x, n.row(step), n.y), d + step)
        self.copy("high", step).start()
        self.arrived(self.slot(n.x, n.row(step), 1 - n.y), 2 * d + step)
        self.copy("low", step).start()

    def fourth(self):
        n, d = self.links, self.links.depth
        for step in range(d):
            got = self.slot(1 - n.x, n.row(step), 1 - n.y)
            self.arrived(self.high(got), 3 * d + step)
            self.arrived(self.low(got), 4 * d + step)
        self.keep().wait()
        for h in range(2 if self.whole else 1):
            self.copy("sibling", h).start()

    def finish(self):
        n, d = self.links, self.links.depth
        for h in range(2 if self.whole else 1):
            self.arrived(self.full.at[h if self.whole else n.c, :, :, 1 - n.c], 5 * d + h)

    def close(self):
        d = self.links.depth
        for step in range(d):
            if step:
                self.copy("far", step).wait_send()
            for kind in ("across", "beside", "high", "low"):
                self.copy(kind, step).wait_send()
        for h in range(2 if self.whole else 1):
            self.copy("sibling", h).wait_send()


class Share:
    def __init__(self, links, in_ref, rows, cot_in, cot, note_in, note, gain_in, gain, send, recv, local):
        n = self.links = links
        half = cot_in.shape[0] // 2
        self.home = n.x == n.c
        s, r = (lambda k: send.at[k]), (lambda k: recv.at[k])
        mine, theirs = pl.ds(n.c * half, half), pl.ds((1 - n.c) * half, half)
        near, far = rows.at[n.x], rows.at[1 - n.x]
        self.rows_across = lambda: remote(in_ref, near, s(0), r(0), n.across)
        self.rows_beside = lambda: remote(in_ref, near, s(1), r(1), n.sibling)
        self.rows_further = lambda: remote(far, far, s(2), r(2), n.sibling)
        self.note = lambda: remote(note_in, note, s(3), r(3), n.sibling)
        self.cot_beside = lambda: remote(cot_in.at[theirs], cot.at[n.x], s(4), r(4), n.sibling)
        self.cot_across = lambda: remote(cot_in.at[mine], cot.at[n.x], s(5), r(5), n.across)
        self.cot_corner = lambda: remote(cot_in.at[theirs], cot.at[n.x], s(6), r(6), n.corner)
        self.gain = lambda: remote(gain_in, gain.at[n.x], s(7), r(7), n.across)
        self.keep = lambda: [
            pltpu.make_async_copy(gain_in, gain.at[n.x], local.at[0]),
        ]
        self.keep_home = lambda: [
            pltpu.make_async_copy(in_ref, near, local.at[1]),
            pltpu.make_async_copy(note_in, note, local.at[2]),
            pltpu.make_async_copy(cot_in.at[mine], cot.at[n.x], local.at[3]),
        ]

    def begin(self):
        @pl.when(self.home)
        def _():
            self.note().start()
            self.rows_beside().start()
            for item in self.keep_home():
                item.start()

        @pl.when(jnp.logical_not(self.home))
        def _():
            self.rows_across().start()

        self.gain().start()
        for item in self.keep():
            item.start()

    def further(self):
        @pl.when(self.home)
        def _():
            self.rows_across().wait_recv()
            self.rows_further().start()
            for item in self.keep_home():
                item.wait()

        @pl.when(jnp.logical_not(self.home))
        def _():
            self.note().wait_recv()
            self.rows_beside().wait_recv()
            self.rows_further().wait_recv()

        for item in self.keep():
            item.wait()

    def later(self):
        @pl.when(self.home)
        def _():
            self.cot_beside().start()

        @pl.when(jnp.logical_not(self.home))
        def _():
            self.cot_across().start()
            self.cot_corner().start()

    def finish(self):
        self.gain().wait()

        @pl.when(self.home)
        def _():
            self.note().wait_send()
            self.rows_beside().wait_send()
            self.rows_further().wait_send()
            self.cot_beside().wait_send()
            self.cot_across().wait_recv()

        @pl.when(jnp.logical_not(self.home))
        def _():
            self.rows_across().wait_send()
            self.cot_across().wait_send()
            self.cot_corner().wait_send()
            self.cot_beside().wait_recv()
            self.cot_corner().wait_recv()


def plus(left, right):
    return (left.astype(WIDE) + right.astype(WIDE)).astype(left.dtype)


def scatter_marks(depth):
    return depth + 5


class Scatter:
    def __init__(self, links, kind, part, cut, bufs, out, send, recv, index, local):
        self.links, self.kind, self.part, self.cut, self.out = links, kind, part, cut, out
        self.held, self.other, self.x1, self.y1, self.x2, self.y2, self.z = bufs
        self.send = lambda k: send.at[index, k]
        self.recv = lambda k: recv.at[index, k]
        self.local = local
        self.rest = self.held.shape[-1] - cut

    def low(self, ref):
        return ref.at[:, :, pl.ds(0, self.cut)]

    def high(self, ref):
        return ref.at[:, :, pl.ds(self.cut, self.rest)]

    def move(self, source, target, mark, device):
        return remote(source, target, self.send(mark), self.recv(mark), device)

    def copy(self, kind, step=0):
        n = self.links
        corner = self.held.at[1 - n.x, :, 1 - n.y]
        if kind == "sibling" and self.kind == "join":
            return self.move(self.part.at[:, :, :, 1 - n.c], self.other, 0, n.sibling)
        if kind == "sibling":
            return self.move(self.part.at[:, :, 1 - n.c], self.held.at[n.c], 0, n.sibling)
        if kind == "x1":
            return self.move(self.low(corner), self.x1, 1, n.across)
        if kind == "y1":
            return self.move(self.high(corner), self.y1, 2, n.beside)
        if kind == "y2":
            return self.move(self.held.at[n.x, :, 1 - n.y], self.y2, 3, n.beside)
        if kind == "x2":
            return self.move(self.held.at[1 - n.x, :, n.y], self.x2, 4, n.across)
        q = lax.rem(n.q + step, n.depth)
        return self.move(self.held.at[n.x, q, n.y], self.z.at[step - 1], 4 + step, n.far(step))

    def keep(self):
        n = self.links
        if self.kind == "held":
            return pltpu.make_async_copy(self.part, self.held, self.local)
        if self.kind == "join":
            return pltpu.make_async_copy(self.part.at[:, :, :, n.c], self.held, self.local)
        return pltpu.make_async_copy(self.part.at[:, :, n.c], self.held.at[n.c], self.local)

    def arrived(self, target, mark):
        self.move(target, target, mark, self.links.sibling).wait_recv()

    def begin(self):
        self.keep().start()
        if self.kind != "held":
            self.copy("sibling").start()

    def first(self):
        n = self.links
        self.keep().wait()
        if self.kind == "join":
            self.arrived(self.other, 0)
            self.held[...] = plus(self.held[...], self.other[...])
        if self.kind == "swap":
            self.arrived(self.held.at[1 - n.c], 0)
        self.copy("x1").start()
        self.copy("y1").start()

    def second(self):
        n = self.links
        low, high = pl.ds(0, self.cut), pl.ds(self.cut, self.rest)
        self.arrived(self.x1, 1)
        for q in range(n.depth):
            self.held[n.x, q, 1 - n.y, :, low] = plus(
                self.held[n.x, q, 1 - n.y, :, low], self.x1[q]
            )
        self.copy("y2").start()
        self.arrived(self.y1, 2)
        for q in range(n.depth):
            self.held[1 - n.x, q, n.y, :, high] = plus(
                self.held[1 - n.x, q, n.y, :, high], self.y1[q]
            )
        self.copy("x2").start()

    def third(self):
        n = self.links
        self.arrived(self.y2, 3)
        self.arrived(self.x2, 4)
        for step in range(1, n.depth):
            q = lax.rem(n.q + step, n.depth)
            self.held[n.x, q, n.y] = plus(plus(self.held[n.x, q, n.y], self.x2[q]), self.y2[q])
            self.copy("z", step).start()

    def fourth(self):
        n = self.links
        total = (
            self.held[n.x, n.q, n.y].astype(WIDE)
            + self.x2[n.q].astype(WIDE)
            + self.y2[n.q].astype(WIDE)
        )
        for step in range(1, n.depth):
            self.arrived(self.z.at[step - 1], 4 + step)
            total = total + self.z[step - 1].astype(WIDE)
        self.out[...] = total

    def close(self):
        if self.kind != "held":
            self.copy("sibling").wait_send()
        for kind in ("x1", "y1", "x2", "y2"):
            self.copy(kind).wait_send()
        for step in range(1, self.links.depth):
            self.copy("z", step).wait_send()


def scatter_scratch(depth, r, columns, cut, join=False, kind=LOW):
    small = (1, 1, 1, 8, 128)
    return [
        pltpu.VMEM((2, depth, 2, r, columns), kind),
        pltpu.VMEM((2, depth, 2, r, columns) if join else small, kind),
        pltpu.VMEM((depth, r, cut), kind),
        pltpu.VMEM((depth, r, columns - cut), kind),
        pltpu.VMEM((depth, r, columns), kind),
        pltpu.VMEM((depth, r, columns), kind),
        pltpu.VMEM((depth - 1, r, columns), kind),
    ]


class HandOver:
    def __init__(self, links, source, target, send, recv, base, local):
        self.links, self.source, self.target, self.local = links, source, target, local
        self.send = lambda k: send.at[base + k]
        self.recv = lambda k: recv.at[base + k]
        self.half = source.shape[1]

    def rows(self, c):
        return self.target.at[pl.ds(c * self.half, self.half)]

    def copies(self):
        n = self.links
        near, far = self.source.at[n.x], self.source.at[1 - n.x]
        mine = self.rows(n.c)
        return (
            pltpu.make_async_copy(near, mine, self.local),
            remote(far, mine, self.send(0), self.recv(0), n.across),
            remote(near, mine, self.send(1), self.recv(1), n.sibling),
            remote(far, mine, self.send(2), self.recv(2), n.corner),
        )

    def begin(self):
        n = self.links
        keep, across, sibling, corner = self.copies()

        @pl.when(n.x == n.c)
        def _():
            keep.start()
            across.start()

        @pl.when(n.x != n.c)
        def _():
            sibling.start()
            corner.start()

    def finish(self):
        n = self.links
        keep, across, sibling, corner = self.copies()
        mine, theirs = self.rows(n.c), self.rows(1 - n.c)

        @pl.when(n.x == n.c)
        def _():
            keep.wait()
            across.wait_send()
            remote(theirs, theirs, self.send(1), self.recv(1), n.sibling).wait_recv()

        @pl.when(n.x != n.c)
        def _():
            sibling.wait_send()
            corner.wait_send()
            remote(mine, mine, self.send(0), self.recv(0), n.across).wait_recv()
            remote(theirs, theirs, self.send(2), self.recv(2), n.corner).wait_recv()


def angle_tables():
    rates = THETA ** (-np.arange(HEAD_DIM // 2) / (HEAD_DIM // 2))
    rates = np.tile(rates, 4)[None]
    base = np.arange(BLOCK)[:, None] * rates
    jump = np.arange(SPAN)[:, None] * BLOCK * rates
    base = np.concatenate([np.cos(base), np.sin(base)], axis=0)
    jump = np.concatenate([np.cos(jump), np.sin(jump), np.zeros((2, 128))], axis=0)
    return jnp.asarray(base, WIDE), jnp.asarray(jump, WIDE)


def lanes(rows):
    return lax.broadcasted_iota(jnp.int32, (rows, 128), 1)


def turn_parts(meta, base, jump, block):
    offset = meta[0, SPAN + block]
    far_cos = jump[pl.ds(offset, 1), :]
    far_sin = jump[pl.ds(SPAN + offset, 1), :]
    near_cos, near_sin = base[0:BLOCK], base[BLOCK : 2 * BLOCK]
    cosine = near_cos * far_cos - near_sin * far_sin
    sine = near_sin * far_cos + near_cos * far_sin
    low = (lanes(BLOCK) % HEAD_DIM) < HEAD_DIM // 2
    return cosine, jnp.where(low, -sine, sine), low


def turn(values, cosine, sine, low):
    swapped = jnp.where(low, pltpu.roll(values, 96, 1), pltpu.roll(values, 32, 1))
    return values * cosine + swapped * sine


def weight_loads(full, h, flat, marks):
    depth, r = full.shape[1], full.shape[4]
    return [
        pltpu.make_async_copy(
            full.at[h, q, y, c], flat.at[pl.ds(k * r, r)], marks.at[k]
        )
        for k, (q, y, c) in enumerate(
            (q, y, c) for q in range(depth) for y in range(2) for c in range(2)
        )
    ]


def forward_kernel(depth, cuts, note_in, gain_in, cot_in, in_ref, q_own, m_own, o_own, base, jump,
                   note, gain, cot, rows, q_full, m_full, o_full, all_context, q_ref, k_ref, v_ref,
                   p_ref, r_ref, c_ref, marks, meta, held, weight, piece, send, recv, local, extra_send,
                   extra_recv, context_send, context_recv):
    step = pl.program_id(0)
    scale = HEAD_DIM ** (-0.5)
    n = Links(depth)
    half = in_ref.shape[0] // 2
    gathers = [
        Gather(n, own, full, cut, whole, send, recv, k, local.at[k])
        for k, (own, full, cut, whole) in enumerate(
            zip((q_own, m_own, o_own), (q_full, m_full, o_full), cuts, (False, True, True))
        )
    ]
    share = Share(
        n, in_ref, rows, cot_in, cot, note_in, note, gain_in, gain, extra_send, extra_recv,
        local.at[pl.ds(3, 4)],
    )

    def context_copy(p):
        there = c_ref.at[p, pl.ds((1 - n.c) * half, half)]
        return remote(there, all_context.at[n.c, p], context_send.at[p], context_recv.at[p], n.sibling)

    def context_keep(p):
        here = c_ref.at[p, pl.ds(n.c * half, half)]
        return pltpu.make_async_copy(here, all_context.at[n.c, p], local.at[10 + p])

    @pl.when(step == 0)
    def _():
        n.meet()
        share.begin()
        gathers[0].begin()
        for k in range(1, depth):
            gathers[0].second(k)
        for k in range(depth):
            gathers[0].third(k)
        gathers[1].begin()
        share.further()
        loads = [
            pltpu.make_async_copy(rows, held, local.at[7]),
            pltpu.make_async_copy(note, meta, local.at[8]),
        ]
        for item in loads:
            item.start()
        gathers[0].fourth()
        gathers[0].finish()
        loads += weight_loads(q_full, n.c, weight, piece)
        for item in loads[2:]:
            item.start()
        for item in loads:
            item.wait()

    hooks = {
        1: [gathers[2].begin],
        2: [functools.partial(gathers[1].second, k) for k in range(1, depth)],
        5: [functools.partial(gathers[1].third, k) for k in range(depth)],
        6: [functools.partial(gathers[2].second, k) for k in range(1, depth)] + [share.later],
        8: [gathers[1].fourth],
        9: [functools.partial(gathers[2].third, k) for k in range(depth)],
    }
    for at, actions in hooks.items():

        @pl.when(step == at)
        def _():
            for action in actions:
                action()

    @pl.when(step < SPAN)
    def _():
        here = pl.ds(step * BLOCK, BLOCK)
        cosine, sine, low = turn_parts(meta, base, jump, step)
        values = jnp.concatenate([held[0, here], held[1, here]], axis=1)

        for p in range(3):
            made = contract(values, weight[:, p * 384 : p * 384 + 384], 1, 0)
            q_ref[p, here] = (turn(made[:, 0:128], cosine, sine, low) * scale).astype(LOW)
            k_ref[p, here] = turn(made[:, 128:256], cosine, sine, low).astype(LOW)
            v_ref[p, here] = made[:, 256:384].astype(LOW)
        marks[here] = (lanes(BLOCK) == meta[0, step]).astype(WIDE).astype(LOW)

    @pl.when(step >= SPAN)
    def _():
        turn_number = step - SPAN
        p = turn_number // SPAN
        i = turn_number % SPAN
        here = pl.ds(i * BLOCK, BLOCK)
        lane = lanes(BLOCK)
        queries = q_ref[p, here]
        values = v_ref[p]
        keys = jnp.concatenate([k_ref[p], marks[...]], axis=1)
        barred = jnp.where((lane < SPAN) & (lane != meta[0, i]), NEGATIVE, 0.0).astype(LOW)
        outs = []
        scales = []
        for head in range(2):
            chosen = (lane // HEAD_DIM) == head
            ours = jnp.concatenate([jnp.where(chosen, queries, 0).astype(LOW), barred], axis=1)
            scores = contract(ours, keys, 1, 1)
            top = jnp.max(scores, axis=1, keepdims=True)
            raised = jnp.exp(scores - top)
            inverse = 1.0 / jnp.sum(raised, axis=1, keepdims=True)
            soft = raised.astype(LOW)
            p_ref[0, head] = soft
            outs.append(contract(soft, values, 1, 0))
            scales.append(inverse)
        inverse = jnp.where(lane < HEAD_DIM, scales[0], scales[1])
        r_ref[p, here] = inverse
        c_ref[p, here] = (jnp.where(lane < HEAD_DIM, outs[0], outs[1]) * inverse).astype(LOW)

    for p in range(3):

        @pl.when(step == 2 * SPAN - 1 + p * SPAN)
        def _():
            context_copy(p).start()
            context_keep(p).start()

    @pl.when(step == 4 * SPAN - 1)
    def _():
        gathers[2].fourth()
        gathers[1].finish()
        gathers[2].finish()
        for item in gathers:
            item.close()
        share.finish()
        for p in range(3):
            context_copy(p).wait()
            context_keep(p).wait()


def forward_call(depth, cuts, note, gain, cot, rows, q_own, m_own, o_own, base, jump):
    length, part = rows.shape
    half = length // 2
    r = q_own.shape[0]
    low = lambda *shape: jax.ShapeDtypeStruct(shape, LOW)
    full = [low(2, depth, 2, 2, r, own.shape[1]) for own in (q_own, m_own, o_own)]
    trio = low(3, length, 128)
    vmem = pl.BlockSpec(memory_space=pltpu.VMEM)
    marks = pltpu.SemaphoreType.DMA((3, gather_marks(depth)))
    return pl.pallas_call(
        functools.partial(forward_kernel, depth, cuts),
        grid=(SPAN + 3 * SPAN,),
        out_shape=[
            jax.ShapeDtypeStruct(note.shape, note.dtype),
            jax.ShapeDtypeStruct((2,) + gain.shape, WIDE),
            low(2, half, part),
            low(2, length, part),
        ]
        + full
        + [
            low(2, 3, half, 128),
            trio,
            trio,
            trio,
            low(SPAN * 3, 2, BLOCK, length),
            jax.ShapeDtypeStruct((3, length, 128), WIDE),
            trio,
        ],
        in_specs=[ANY] * 7 + [vmem] * 2,
        out_specs=[ANY] * 8
        + [vmem] * 3
        + [
            pl.BlockSpec((1, 2, BLOCK, length), lambda s: (jnp.maximum(s - SPAN, 0), 0, 0, 0)),
            vmem,
            vmem,
        ],
        scratch_shapes=[
            pltpu.VMEM((length, 128), LOW),
            pltpu.SMEM(note.shape, note.dtype),
            pltpu.VMEM((2, length, part), LOW),
            pltpu.VMEM((4 * depth * r, q_own.shape[1]), LOW),
            pltpu.SemaphoreType.DMA((4 * depth,)),
            marks,
            marks,
            pltpu.SemaphoreType.DMA((13,)),
            pltpu.SemaphoreType.DMA((8,)),
            pltpu.SemaphoreType.DMA((8,)),
            pltpu.SemaphoreType.DMA((3,)),
            pltpu.SemaphoreType.DMA((3,)),
        ],
        compiler_params=pltpu.CompilerParams(
            collective_id=0, has_side_effects=True, vmem_limit_bytes=60 * MEGA
        ),
        name="attend",
    )(note, gain, cot, rows, q_own, m_own, o_own, base, jump)


def norm_of(summed):
    mean = jnp.mean(summed, axis=1, keepdims=True)
    centred = summed - mean
    variance = jnp.mean(centred * centred, axis=1, keepdims=True)
    scale = lax.rsqrt(variance + EPSILON)
    return centred * scale, scale


def norm_back(scaled, normed, scale):
    total = jnp.mean(scaled, axis=1, keepdims=True)
    cross = jnp.mean(scaled * normed, axis=1, keepdims=True)
    return scale * (scaled - total - normed * cross)


HIDDEN = 512


def middle_kernel(depth, context, rows, cot, gains, m_full, o_full, lo_ref, gfs_ref, sums, grads,
                  o_held, m_held, m_mat, o_mat, act, gi, fl, gm, ga, gc, slopes, o_part, m_part,
                  o_other, m_other, local, send, recv):
    step = pl.program_id(0)
    tile, part = rows.shape[1:]
    half = fl.shape[0]
    tiles = half // tile
    r = o_part.shape[-2]
    pieces = o_mat.shape[2] // HIDDEN
    width = pieces * HIDDEN
    n = Links(depth)
    here = pl.ds(step * tile, tile)
    loads = lambda: (
        pltpu.make_async_copy(m_full, m_mat, local.at[0]),
        pltpu.make_async_copy(o_full, o_mat, local.at[1]),
    )

    def grads_keep():
        own = grads.at[:, pl.ds(n.c * half, half)]
        return pltpu.make_async_copy(gc.at[n.c], own, local.at[2])

    def grads_copy():
        own = grads.at[:, pl.ds(n.c * half, half)]
        return remote(gc.at[1 - n.c], own, send.at[4], recv.at[4], n.sibling)

    def part_copy(k):
        source, target = ((o_part, o_other) if k < 2 else (m_part, m_other))
        h = k % 2
        return remote(
            source.at[h, :, :, 1 - n.c], target.at[h], send.at[k], recv.at[k], n.sibling
        )

    def join(k):
        source, target = ((o_part, o_other) if k < 2 else (m_part, m_other))
        h = k % 2
        part_copy(k).wait_recv()
        for q in range(depth):
            for y in range(2):
                target[h, q, y] = plus(source[h, q, y, n.c], target[h, q, y])

    def held_copy(k):
        source, target = ((o_other, o_held) if k < 2 else (m_other, m_held))
        return pltpu.make_async_copy(source.at[k % 2], target.at[k % 2], local.at[3 + k])

    @pl.when(step == 0)
    def _():
        for item in loads():
            item.start()
        n.meet(True)
        loads()[0].wait()

    @pl.when(step < tiles)
    def _():
        whole = jnp.concatenate([gains[0], gains[1]], axis=1)
        gain1, bias1, gain2, bias2 = (whole[k : k + 1, :] for k in range(4))
        summed = jnp.concatenate([rows[0], rows[1]], axis=1).astype(WIDE)
        for h in range(2):
            seen = jnp.concatenate([context[h, p, here] for p in range(3)], axis=1)
            summed = summed + contract(seen, m_mat[h, :, 0:part], 1, 1)
        normed1, scale1 = norm_of(summed)
        first = normed1 * gain1 + bias1
        first_low = first.astype(LOW)
        fl[here] = first_low
        for h in range(2):
            for j in range(pieces):
                lo_end = part + j * HIDDEN
                there = slice(h * width + j * HIDDEN, h * width + (j + 1) * HIDDEN)
                inner = contract(first_low, m_mat[h, :, lo_end : lo_end + HIDDEN], 1, 0)
                share = 0.5 * (1.0 + lax.erf(inner * ROOT_HALF))
                slopes[:, there] = share + inner * jnp.exp(-0.5 * inner * inner) * INVERSE_ROOT
                act[here, there] = (inner * share).astype(LOW)

        @pl.when(step == 0)
        def _():
            loads()[1].wait()

        mixed = first
        for h in range(2):
            mixed = mixed + contract(act[here, h * width : (h + 1) * width], o_mat[h], 1, 1)
        normed2, scale2 = norm_of(mixed)
        result = (normed2 * gain2 + bias2).astype(LOW)
        for h in range(2):
            lo_ref[h] = result[:, h * part : (h + 1) * part]
        cotangent = jnp.concatenate([cot[0], cot[1]], axis=1).astype(WIDE)
        second_gain = jnp.sum(cotangent * normed2, axis=0, keepdims=True)
        second_bias = jnp.sum(cotangent, axis=0, keepdims=True)
        grad_second = norm_back(cotangent * gain2, normed2, scale2)
        grad_mixed = grad_second.astype(LOW)
        gm[here] = grad_mixed
        for h in range(2):
            for j in range(pieces):
                there = slice(h * width + j * HIDDEN, h * width + (j + 1) * HIDDEN)
                raised = contract(grad_mixed, o_mat[h, :, j * HIDDEN : (j + 1) * HIDDEN], 1, 0)
                gi[here, there] = (raised * slopes[:, there]).astype(LOW)
        grad_first = grad_second
        for h in range(2):
            grad_first = grad_first + contract(
                gi[here, h * width : (h + 1) * width], m_mat[h, :, part : part + width], 1, 1
            )
        first_gain = jnp.sum(grad_first * normed1, axis=0, keepdims=True)
        first_bias = jnp.sum(grad_first, axis=0, keepdims=True)
        grad_sum = norm_back(grad_first * gain1, normed1, scale1)
        gfs_ref[...] = grad_sum
        grad_attended = grad_sum.astype(LOW)
        ga[here] = grad_attended
        for h in range(2):
            made = contract(grad_attended, m_mat[h, :, 0:part], 1, 0).astype(LOW)
            for p in range(3):
                gc[h, p, here] = made[:, p * 128 : (p + 1) * 128]
        found = jnp.concatenate([first_gain, first_bias, second_gain, second_bias], axis=0)

        @pl.when(step == 0)
        def _():
            sums[...] = found

        @pl.when(step > 0)
        def _():
            sums[...] += found

    @pl.when(step == tiles - 1)
    def _():
        grads_keep().start()
        grads_copy().start()

    def put(target, h, row, column, values):
        shards = values.shape[0] // r
        for k in range(shards):
            w = row // r + k
            target[h, w // 4, (w // 2) % 2, w % 2, :, column : column + values.shape[1]] = values[
                k * r : (k + 1) * r
            ]

    for k in range(4):

        @pl.when(step == tiles + k)
        def _():
            h = k % 2
            target = o_part if k < 2 else m_part
            for row in range(0, 2 * part, part):
                for j in range(pieces):
                    there = slice(h * width + j * HIDDEN, h * width + (j + 1) * HIDDEN)
                    if k < 2:
                        made = contract(gm[:, row : row + part], act[:, there], 0, 0)
                        put(target, h, row, j * HIDDEN, made.astype(LOW))
                    else:
                        made = contract(fl[:, row : row + part], gi[:, there], 0, 0)
                        put(target, h, row, part + j * HIDDEN, made.astype(LOW))
                if k >= 2:
                    seen = jnp.concatenate([context[h, p] for p in range(3)], axis=1)
                    made = contract(ga[:, row : row + part], seen, 0, 0)
                    put(target, h, row, 0, made.astype(LOW))
            part_copy(k).start()
            if k:
                join(k - 1)
                held_copy(k - 1).start()
            if k == 3:
                join(3)
                held_copy(3).start()
                for item in range(4):
                    held_copy(item).wait()
                    part_copy(item).wait_send()
                grads_keep().wait()
                grads_copy().wait()


def once(shape):
    zeros = (0,) * len(shape)
    return pl.BlockSpec(shape, lambda *_: zeros, pipeline_mode=pl.Buffered(1))


def middle_call(depth, context, rows, cot, m_full, o_full, gains):
    tile = 256
    half, part = cot.shape[1:]
    tiles = half // tile
    width = 2 * part
    hidden = 2 * o_full.shape[2]
    r = width // (4 * depth)
    columns = (o_full.shape[2], m_full.shape[2])
    low = lambda *shape: jax.ShapeDtypeStruct(shape, LOW)
    held = [(2, depth, 2, r, item) for item in columns]
    last = lambda i: jnp.minimum(i, tiles - 1)
    c = lambda: lax.rem(lax.axis_index("wide"), 2)
    return pl.pallas_call(
        functools.partial(middle_kernel, depth),
        grid=(tiles + 4,),
        out_shape=[
            low(2, half, part),
            jax.ShapeDtypeStruct((half, width), WIDE),
            jax.ShapeDtypeStruct((4, width), WIDE),
            low(3, 2 * half, 128),
        ]
        + [low(*item) for item in held],
        in_specs=[
            once((2, 3, half, 128)),
            pl.BlockSpec((2, tile, part), lambda i: (0, c() * tiles + last(i), 0)),
            pl.BlockSpec((2, tile, part), lambda i: (0, last(i), 0)),
            once(gains.shape),
            ANY,
            ANY,
        ],
        out_specs=[
            pl.BlockSpec((2, tile, part), lambda i: (0, last(i), 0)),
            pl.BlockSpec((tile, width), lambda i: (last(i), 0)),
            pl.BlockSpec((4, width), lambda i: (0, 0)),
            ANY,
            ANY,
            ANY,
        ],
        scratch_shapes=[
            pltpu.VMEM(m_full.shape, LOW),
            pltpu.VMEM(o_full.shape, LOW),
            pltpu.VMEM((half, hidden), LOW),
            pltpu.VMEM((half, hidden), LOW),
            pltpu.VMEM((half, width), LOW),
            pltpu.VMEM((half, width), LOW),
            pltpu.VMEM((half, width), LOW),
            pltpu.VMEM((2, 3, half, 128), LOW),
            pltpu.VMEM((tile, hidden), WIDE),
        ]
        + [pltpu.VMEM((2, depth, 2, 2, r, item), LOW) for item in columns]
        + [pltpu.VMEM(item, LOW) for item in held]
        + [
            pltpu.SemaphoreType.DMA((7,)),
            pltpu.SemaphoreType.DMA((5,)),
            pltpu.SemaphoreType.DMA((5,)),
        ],
        compiler_params=pltpu.CompilerParams(
            collective_id=1, has_side_effects=True, vmem_limit_bytes=62 * MEGA
        ),
        name="middle",
    )(context, rows, cot, gains, m_full, o_full)


def backward_kernel(depth, cuts, meta, base, jump, soft, grads, context, inverse, q_ref, k_ref, v_ref,
                    rows, kept, q_full, lo_in, o_in, m_in, t_in, lo_out, dx_out, o_out, m_out, q_out,
                    t_out, *scratch):
    ones, keys_sum, values_sum, made, weight, q_part, dx_own, dx_give, dx_other = scratch[:9]
    bufs = [scratch[9 + 7 * k : 16 + 7 * k] for k in range(6)]
    piece, send, recv, local, extra_send, extra_recv = scratch[51:]
    step = pl.program_id(0)
    p = step // SPAN
    i = step % SPAN
    length = q_ref.shape[1]
    scale = HEAD_DIM ** (-0.5)
    lane = lanes(BLOCK)
    here = pl.ds(i * BLOCK, BLOCK)
    n = Links(depth)
    r = o_in.shape[-2]
    half, width = kept.shape
    part = width // 2
    kinds = ("held", "held", "swap", "swap", "swap", "join")
    parts = (o_in, m_in) + tuple(q_part.at[k] for k in range(3)) + (t_in,)
    outs = (o_out, m_out) + tuple(q_out.at[k] for k in range(3)) + (t_out,)
    every = [
        Scatter(n, kind, item, cut, buf, out, send, recv, k, local.at[k])
        for k, (kind, item, cut, buf, out) in enumerate(zip(kinds, parts, cuts, bufs, outs))
    ]
    outer, inner, pair0, pair1, pair2, small = every
    lo_over = HandOver(n, lo_in, lo_out, extra_send, extra_recv, 0, local.at[6])
    dx_over = HandOver(n, dx_own, dx_out, extra_send, extra_recv, 3, local.at[7])
    dx_swap = lambda: remote(dx_give, dx_other, extra_send.at[6], extra_recv.at[6], n.sibling)

    @pl.when(step == 0)
    def _():
        ones[...] = (lanes(length) < 2).astype(WIDE).astype(LOW)
        for item in weight_loads(q_full, n.c, weight, piece):
            item.start()
        outer.begin()
        inner.begin()
        n.meet()
        small.begin()
        outer.first()
        inner.first()
        small.first()
        for item in weight_loads(q_full, n.c, weight, piece):
            item.wait()

    hooks = {
        1: [outer.second, small.second, lo_over.begin],
        2: [inner.second, small.third],
        3: [small.fourth, pair0.first],
        4: [outer.third, pair0.second],
        5: [pair0.third],
        6: [inner.third, outer.fourth, pair1.first],
        7: [pair1.second, pair0.fourth],
        8: [pair1.third, inner.fourth],
    }
    for at, actions in hooks.items():

        @pl.when(step == at)
        def _():
            for action in actions:
                action()

    grad = grads[p, here].astype(WIDE)
    turned = grad * inverse[p, here]
    both = turned * context[p, here].astype(WIDE)
    turned_low = turned.astype(LOW)
    queries = q_ref[p, here]
    keys = k_ref[p]
    values = jnp.concatenate([v_ref[p], ones[...]], axis=1)
    turned_flip = jnp.transpose(turned).astype(LOW)
    queries_flip = jnp.transpose(queries.astype(WIDE)).astype(LOW)
    found = []
    for head in range(2):
        chosen = (lane // HEAD_DIM) == head
        centre = -jnp.sum(jnp.where(chosen, both, 0.0), axis=1, keepdims=True)
        coarse = centre.astype(LOW).astype(WIDE)
        fine = jnp.where(lane == 0, coarse, jnp.where(lane == 1, centre - coarse, 0.0))
        ours = jnp.concatenate(
            [jnp.where(chosen, turned_low, 0).astype(LOW), fine.astype(LOW)], axis=1
        )
        raised = soft[0, head]
        scores = (contract(ours, values, 1, 1) * raised.astype(WIDE)).astype(LOW)
        found.append(contract(scores, keys, 1, 0))
        mine = slice(head * HEAD_DIM, (head + 1) * HEAD_DIM)
        values_add = contract(turned_flip[mine], raised, 1, 0)
        keys_add = contract(queries_flip[mine], scores, 1, 0)

        @pl.when(i == 0)
        def _():
            values_sum[mine] = values_add
            keys_sum[mine] = keys_add

        @pl.when(i > 0)
        def _():
            values_sum[mine] += values_add
            keys_sum[mine] += keys_add

    cosine, sine, low = turn_parts(meta, base, jump, i)
    grad_queries = jnp.where(lane < HEAD_DIM, found[0], found[1]) * scale
    made[p, here, 0:128] = turn(grad_queries, cosine, -sine, low).astype(LOW)

    @pl.when(i == SPAN - 1)
    def _():
        grad_keys = jnp.transpose(keys_sum[...])
        grad_values = jnp.transpose(values_sum[...])
        for b in range(SPAN):
            there = slice(b * BLOCK, (b + 1) * BLOCK)
            cosine, sine, low = turn_parts(meta, base, jump, b)
            made[p, there, 128:256] = turn(grad_keys[there], cosine, -sine, low).astype(LOW)
        made[p, :, 256:384] = grad_values.astype(LOW)
        for h in range(2):
            found = contract(rows[h], made[p], 0, 0).astype(LOW)
            for k in range(part // r):
                w = h * (part // r) + k
                q_part[p, w // 4, (w // 2) % 2, w % 2] = found[k * r : (k + 1) * r]

    for k in range(3):

        @pl.when(step == k * SPAN + SPAN - 1)
        def _():
            every[2 + k].begin()

    @pl.when(step == 3 * SPAN - 1)
    def _():
        for own in (False, True):
            there = pl.ds((n.c if own else 1 - n.c) * half, half)
            gained = kept[...] if own else jnp.zeros(kept.shape, WIDE)
            for k in range(3):
                gained = gained + contract(
                    made[k, there], weight[:, k * 384 : k * 384 + 384], 1, 1
                )
            target = dx_own if own else dx_give
            for h in range(2):
                target[h] = gained[:, h * part : (h + 1) * part].astype(LOW)
            if own:
                pair2.second()
            else:
                dx_swap().start()
                pair2.first()
        dx_swap().wait_recv()
        for h in range(2):
            dx_own[h] = plus(dx_own[h], dx_other[h])
        dx_over.begin()
        pair2.third()
        pair1.fourth()
        pair2.fourth()
        for item in every:
            item.close()
        dx_swap().wait_send()
        lo_over.finish()
        dx_over.finish()


def backward_call(depth, cuts, meta, base, jump, soft, grads, context, inverse, q, k, v, rows, kept,
                  q_full, lo, o_held, m_held, t_part):
    length = q.shape[1]
    half, width = kept.shape
    part = width // 2
    r = o_held.shape[-2]
    trio = once((3, length, 128))
    low = lambda *shape: jax.ShapeDtypeStruct(shape, LOW)
    widths = (o_held.shape[-1], m_held.shape[-1])
    shape = lambda *item: jax.ShapeDtypeStruct(item, WIDE)
    outs = [shape(r, widths[0]), shape(r, widths[1]), shape(3, r, 384), shape(*t_part.shape[-2:])]
    scratch = [
        pltpu.VMEM((length, 128), LOW),
        pltpu.VMEM((128, length), WIDE),
        pltpu.VMEM((128, length), WIDE),
        pltpu.VMEM((3, length, 384), LOW),
        pltpu.VMEM((width, 3 * 384), LOW),
        pltpu.VMEM((3, depth, 2, 2, r, 384), LOW),
        pltpu.VMEM((2, half, part), LOW),
        pltpu.VMEM((2, half, part), LOW),
        pltpu.VMEM((2, half, part), LOW),
    ]
    for at, columns in enumerate(widths + (384,) * 3):
        scratch += scatter_scratch(depth, r, columns, cuts[at])
    scratch += scatter_scratch(depth, t_part.shape[-2], t_part.shape[-1], cuts[5], True, WIDE)
    marks = pltpu.SemaphoreType.DMA((6, scatter_marks(depth)))
    return pl.pallas_call(
        functools.partial(backward_kernel, depth, cuts),
        grid=(3 * SPAN,),
        out_shape=[low(2 * half, part)] * 2 + outs,
        in_specs=[
            pl.BlockSpec(memory_space=pltpu.SMEM),
            once(base.shape),
            once(jump.shape),
            pl.BlockSpec((1, 2, BLOCK, length), lambda s: (s, 0, 0, 0)),
            trio,
            trio,
            trio,
            trio,
            trio,
            trio,
            once(rows.shape),
            once(kept.shape),
        ]
        + [ANY] * 5,
        out_specs=[ANY] * 2 + [once(item.shape) for item in outs],
        scratch_shapes=scratch
        + [
            pltpu.SemaphoreType.DMA((4 * depth,)),
            marks,
            marks,
            pltpu.SemaphoreType.DMA((8,)),
            pltpu.SemaphoreType.DMA((7,)),
            pltpu.SemaphoreType.DMA((7,)),
        ],
        compiler_params=pltpu.CompilerParams(
            collective_id=2, has_side_effects=True, vmem_limit_bytes=63 * MEGA
        ),
        name="attend_back",
    )(meta, base, jump, soft, grads, context, inverse, q, k, v, rows, kept, q_full, lo, o_held, m_held, t_part)


def owned(
    inputs,
    block_segment,
    query_weight,
    key_weight,
    value_weight,
    output_weight,
    inner_weight,
    outer_weight,
    first_gain,
    first_bias,
    second_gain,
    second_bias,
    output_cotangent,
):
    wide = lax.axis_size("wide")
    depth = wide // 4
    r = query_weight.shape[0]
    part = query_weight.shape[1]
    length = inputs.shape[0]
    half = length // 2
    x, w, c, _, _ = place()
    pairs = part // 128
    q_own = jnp.concatenate(
        [
            item[:, p * 128 : (p + 1) * 128]
            for p in range(pairs)
            for item in (query_weight, key_weight, value_weight)
        ],
        axis=1,
    )
    m_own = jnp.concatenate([output_weight.T, inner_weight], axis=1)
    o_own = outer_weight.T
    earlier = jnp.sum((block_segment[None, :] < block_segment[:, None]).astype(jnp.int32), axis=1)
    offsets = jnp.arange(SPAN, dtype=jnp.int32) - earlier
    meta = jnp.zeros((1, 128), jnp.int32)
    meta = meta.at[0, 0:SPAN].set(block_segment).at[0, SPAN : 2 * SPAN].set(offsets)
    widths = [item.shape[1] for item in (q_own, m_own, o_own)]
    cuts = [(item // 128 // 5) * 128 for item in widths]
    gains = jnp.stack([first_gain, first_bias, second_gain, second_bias])
    gains = jnp.concatenate([gains, gains], axis=0)
    base, jump = angle_tables()
    meta, gains, cot, rows, q_full, m_full, o_full, pairs_context, q, k, v, soft, inverse, context = (
        forward_call(
            depth, cuts, meta, gains, output_cotangent, inputs, q_own, m_own, o_own, base, jump
        )
    )
    lo, kept, sums, grads, o_held, m_held = middle_call(
        depth,
        pairs_context,
        rows,
        cot,
        m_full.reshape(2, 2 * part, widths[1]),
        o_full.reshape(2, 2 * part, widths[2]),
        gains,
    )
    few = 2 * part // (2 * wide)
    spots = jnp.moveaxis(sums.reshape(2, 2, 2, wide, few), (2, 3), (0, 1))
    spots = jnp.pad(jnp.moveaxis(spots, 2, 3), ((0, 0), (0, 0), (0, 6), (0, 0), (0, 128 - few)))
    spots = spots.reshape(2, depth, 2, 2, 8, 256)
    layer_output, input_gradient, o_sum, m_sum, q_sum, found = backward_call(
        depth,
        [cuts[2], cuts[1], 128, 128, 128, 128],
        meta,
        base,
        jump,
        soft,
        grads,
        context,
        inverse,
        q,
        k,
        v,
        rows,
        kept,
        q_full,
        lo,
        o_held,
        m_held,
        spots,
    )
    q_sum = jnp.moveaxis(q_sum, 0, 1).reshape(r, pairs, 3, 128)
    return (
        layer_output,
        input_gradient,
        q_sum[:, :, 0].reshape(r, part),
        q_sum[:, :, 1].reshape(r, part),
        q_sum[:, :, 2].reshape(r, part),
        m_sum[:, 0:part].T,
        m_sum[:, part:],
        o_sum.T,
        found[0, 0:few],
        found[1, 0:few],
        found[0, 128 : 128 + few],
        found[1, 128 : 128 + few],
    )


def program(*arrays):
    rows = arrays[2].shape[0]
    whole = rows % 16 == 0 and lax.axis_size("narrow") == 2 and lax.axis_size("wide") % 4 == 0
    return owned(*arrays) if whole else shards(*arrays)


def solution(mesh):
    placed = (
        P("wide", "narrow"),
        P("wide"),
        P("wide", "narrow"),
        P("wide", "narrow"),
        P("wide", "narrow"),
        P("narrow", "wide"),
        P("wide", "narrow"),
        P("narrow", "wide"),
        P("narrow"),
        P("narrow"),
        P("narrow"),
        P("narrow"),
        P("wide", "narrow"),
    )
    return jax.shard_map(
        program,
        mesh=mesh,
        in_specs=placed,
        out_specs=(
            P("wide", "narrow"),
            P("wide", "narrow"),
            P("wide", "narrow"),
            P("wide", "narrow"),
            P("wide", "narrow"),
            P("narrow", "wide"),
            P("wide", "narrow"),
            P("narrow", "wide"),
            P(("narrow", "wide")),
            P(("narrow", "wide")),
            P(("narrow", "wide")),
            P(("narrow", "wide")),
        ),
        check_vma=False,
    )
```

```python
import functools

import jax
import jax.numpy as jnp
import numpy as np
from jax import lax
from jax.experimental import pallas as pl
from jax.experimental.pallas import tpu as pltpu
from jax.sharding import PartitionSpec as P

HEAD_DIM = 64
BLOCK = 512
SPAN = 3


EPSILON = 1e-06
NEGATIVE = -1e30
THETA = 10000.0
ROOT_HALF = 0.7071067811865476
INVERSE_ROOT = 0.3989422804014327


def product(left, right):
    return jnp.dot(left, right, preferred_element_type=jnp.float32)


def left_transposed(left, right):
    return lax.dot_general(
        left, right, (((0,), (0,)), ((), ())), preferred_element_type=jnp.float32
    )


def right_transposed(left, right):
    return lax.dot_general(
        left, right, (((1,), (1,)), ((), ())), preferred_element_type=jnp.float32
    )


def whole_features(values):
    return lax.all_gather(values, "narrow", axis=1, tiled=True)


def feature_sums(values):
    return lax.psum_scatter(
        values.astype(jnp.bfloat16), "narrow", scatter_dimension=1, tiled=True
    ).astype(jnp.float32)


def moments(first_sum, second_sum):
    return lax.psum((first_sum, second_sum), "narrow")


def gelu_value(values):
    return 0.5 * values * (1.0 + lax.erf(values * ROOT_HALF))


def gelu_slope(values):
    return (
        0.5 * (1.0 + lax.erf(values * ROOT_HALF))
        + values * jnp.exp(-0.5 * values * values) * INVERSE_ROOT
    )


def rotate(values, cosine, sine):
    half = values.shape[-1] // 2
    first = values[..., :half]
    second = values[..., half:]
    return jnp.concatenate(
        [first * cosine - second * sine, second * cosine + first * sine], axis=-1
    )


def rotate_back(values, cosine, sine):
    half = values.shape[-1] // 2
    first = values[..., :half]
    second = values[..., half:]
    return jnp.concatenate(
        [first * cosine + second * sine, second * cosine - first * sine], axis=-1
    )


def tables(block_segment):
    segment = block_segment.reshape(-1, SPAN)
    earlier = jnp.sum((segment[:, None, :] < segment[:, :, None]).astype(jnp.int32), axis=2)
    offsets = (jnp.arange(SPAN, dtype=jnp.int32)[None, :] - earlier) * BLOCK
    positions = (
        (offsets[:, :, None] + jnp.arange(BLOCK, dtype=jnp.int32)[None, None, :])
        .reshape(-1)
        .astype(jnp.float32)
    )
    half = HEAD_DIM // 2
    rates = THETA ** (-jnp.arange(half, dtype=jnp.float32) / half)
    angle = positions[:, None] * rates[None, :]
    labels = jnp.repeat(segment, BLOCK, axis=1)
    return (jnp.cos(angle)[:, None, :], jnp.sin(angle)[:, None, :], labels)


def normalize(summed, gain, bias, width):
    total, squares = moments(jnp.sum(summed, axis=1), jnp.sum(summed * summed, axis=1))
    mean = total / width
    reciprocal = lax.rsqrt(squares / width - mean * mean + EPSILON)
    normed = (summed - mean[:, None]) * reciprocal[:, None]
    return (normed * gain + bias, normed, reciprocal)


def normalize_back(grad, normed, reciprocal, gain, width):
    scaled = grad * gain
    total, cross = moments(jnp.sum(scaled, axis=1), jnp.sum(scaled * normed, axis=1))
    return reciprocal[:, None] * (scaled - total[:, None] / width - normed * cross[:, None] / width)


def block_scores(block_queries, group_keys, block_labels, group_labels, factor):
    scores = (
        jnp.einsum("qhd,khd->hqk", block_queries, group_keys, preferred_element_type=jnp.float32)
        * factor
    )
    same = block_labels[:, None] == group_labels[None, :]
    return jnp.where(same[None], scores, NEGATIVE)


def attention_forward(queries, keys, values, labels, factor):
    groups, length = labels.shape
    shape = (groups, length) + queries.shape[1:]

    def one_group(items):
        group_queries, group_keys, group_values, group_labels = items
        contexts = []
        totals = []
        for index in range(length // BLOCK):
            low_end = index * BLOCK
            high_end = low_end + BLOCK
            scores = block_scores(
                group_queries[low_end:high_end],
                group_keys,
                group_labels[low_end:high_end],
                group_labels,
                factor,
            )
            top = jnp.max(scores, axis=2, keepdims=True)
            raised = jnp.exp(scores - top)
            summed = jnp.sum(raised, axis=2, keepdims=True)
            soft = (raised / summed).astype(jnp.bfloat16)
            contexts.append(
                jnp.einsum("hqk,khd->qhd", soft, group_values, preferred_element_type=jnp.float32)
            )
            totals.append((top + jnp.log(summed))[..., 0])
        return (jnp.concatenate(contexts, axis=0), jnp.concatenate(totals, axis=1))

    contexts, totals = lax.map(
        one_group, (queries.reshape(shape), keys.reshape(shape), values.reshape(shape), labels)
    )
    return (contexts.reshape(queries.shape), totals)


def attention_backward(queries, keys, values, totals, grad_context, labels, factor):
    groups, length = labels.shape
    shape = (groups, length) + queries.shape[1:]

    def one_group(items):
        group_queries, group_keys, group_values, group_totals, group_grads, group_labels = items
        keys_grad = jnp.zeros(group_keys.shape, jnp.float32)
        values_grad = jnp.zeros(group_values.shape, jnp.float32)
        pieces = []
        for index in range(length // BLOCK):
            low_end = index * BLOCK
            high_end = low_end + BLOCK
            block_queries = group_queries[low_end:high_end]
            block_grads = group_grads[low_end:high_end]
            scores = block_scores(
                block_queries, group_keys, group_labels[low_end:high_end], group_labels, factor
            )
            soft = jnp.exp(scores - group_totals[:, low_end:high_end, None])
            inner = jnp.einsum(
                "qhd,khd->hqk", block_grads, group_values, preferred_element_type=jnp.float32
            )
            centre = jnp.sum(soft * inner, axis=2, keepdims=True)
            scores_grad = (soft * (inner - centre)).astype(jnp.bfloat16)
            pieces.append(
                jnp.einsum(
                    "hqk,khd->qhd", scores_grad, group_keys, preferred_element_type=jnp.float32
                )
                * factor
            )
            keys_grad = (
                keys_grad
                + jnp.einsum(
                    "hqk,qhd->khd", scores_grad, block_queries, preferred_element_type=jnp.float32
                )
                * factor
            )
            values_grad = values_grad + jnp.einsum(
                "hqk,qhd->khd",
                soft.astype(jnp.bfloat16),
                block_grads,
                preferred_element_type=jnp.float32,
            )
        return (jnp.concatenate(pieces, axis=0), keys_grad, values_grad)

    queries_grad, keys_grad, values_grad = lax.map(
        one_group,
        (
            queries.reshape(shape),
            keys.reshape(shape),
            values.reshape(shape),
            totals,
            grad_context.reshape(shape),
            labels,
        ),
    )
    return (
        queries_grad.reshape(queries.shape),
        keys_grad.reshape(queries.shape),
        values_grad.reshape(queries.shape),
    )


def shards(
    inputs,
    block_segment,
    query_weight,
    key_weight,
    value_weight,
    output_weight,
    inner_weight,
    outer_weight,
    first_gain,
    first_bias,
    second_gain,
    second_bias,
    output_cotangent,
):
    width = first_gain.shape[0] * lax.axis_size("narrow")
    tokens = inputs.shape[0]
    factor = HEAD_DIM ** (-0.5)
    cosine, sine, labels = tables(block_segment)
    full_inputs = whole_features(inputs)
    query_full, key_full, value_full, inner_full = (
        lax.all_gather(query_weight, "wide", axis=0, tiled=True),
        lax.all_gather(key_weight, "wide", axis=0, tiled=True),
        lax.all_gather(value_weight, "wide", axis=0, tiled=True),
        lax.all_gather(inner_weight, "wide", axis=0, tiled=True),
    )
    output_full, outer_full = (
        lax.all_gather(output_weight, "wide", axis=1, tiled=True),
        lax.all_gather(outer_weight, "wide", axis=1, tiled=True),
    )
    head_shape = (tokens, query_weight.shape[1] // HEAD_DIM, HEAD_DIM)
    queries = rotate(product(full_inputs, query_full).reshape(head_shape), cosine, sine).astype(
        jnp.bfloat16
    )
    keys = rotate(product(full_inputs, key_full).reshape(head_shape), cosine, sine).astype(
        jnp.bfloat16
    )
    values = product(full_inputs, value_full).astype(jnp.bfloat16).reshape(head_shape)
    context, totals = attention_forward(queries, keys, values, labels, factor)
    context_low = context.reshape(tokens, -1).astype(jnp.bfloat16)
    attended = feature_sums(product(context_low, output_full))
    first, first_normed, first_scale = normalize(
        inputs.astype(jnp.float32) + attended, first_gain, first_bias, width
    )
    first_low = first.astype(jnp.bfloat16)
    feed_rows = whole_features(first_low)
    inner = product(feed_rows, inner_full)
    activated = gelu_value(inner).astype(jnp.bfloat16)
    mixed = feature_sums(product(activated, outer_full))
    second, second_normed, second_scale = normalize(first + mixed, second_gain, second_bias, width)
    layer_output = second.astype(jnp.bfloat16)
    cotangent = output_cotangent.astype(jnp.float32)
    second_gain_grad = jnp.sum(cotangent * second_normed, axis=0)
    second_bias_grad = jnp.sum(cotangent, axis=0)
    grad_second = normalize_back(cotangent, second_normed, second_scale, second_gain, width)
    grad_mixed = grad_second.astype(jnp.bfloat16)
    grad_rows = whole_features(grad_mixed)
    grad_activated = right_transposed(grad_rows, outer_full)
    outer_grad = left_transposed(activated, grad_rows)
    grad_inner = (grad_activated * gelu_slope(inner)).astype(jnp.bfloat16)
    inner_grad = left_transposed(feed_rows, grad_inner)
    grad_first = grad_second + feature_sums(right_transposed(grad_inner, inner_full))
    first_gain_grad = jnp.sum(grad_first * first_normed, axis=0)
    first_bias_grad = jnp.sum(grad_first, axis=0)
    grad_first_sum = normalize_back(grad_first, first_normed, first_scale, first_gain, width)
    attended_rows = whole_features(grad_first_sum.astype(jnp.bfloat16))
    output_grad = left_transposed(context_low, attended_rows)
    grad_context = right_transposed(attended_rows, output_full).astype(jnp.bfloat16)
    queries_grad, keys_grad, values_grad = attention_backward(
        queries, keys, values, totals, grad_context.reshape(head_shape), labels, factor
    )
    queries_grad = rotate_back(queries_grad, cosine, sine).reshape(tokens, -1).astype(jnp.bfloat16)
    keys_grad = rotate_back(keys_grad, cosine, sine).reshape(tokens, -1).astype(jnp.bfloat16)
    values_grad = values_grad.reshape(tokens, -1).astype(jnp.bfloat16)
    query_grad = left_transposed(full_inputs, queries_grad)
    key_grad = left_transposed(full_inputs, keys_grad)
    value_grad = left_transposed(full_inputs, values_grad)
    spread = (
        right_transposed(queries_grad, query_full)
        + right_transposed(keys_grad, key_full)
        + right_transposed(values_grad, value_full)
    )
    input_gradient = (grad_first_sum + feature_sums(spread)).astype(jnp.bfloat16)
    (
        query_total,
        key_total,
        value_total,
        inner_total,
        first_gain_total,
        first_bias_total,
        second_gain_total,
        second_bias_total,
    ) = (
        lax.psum_scatter(query_grad, "wide", scatter_dimension=0, tiled=True),
        lax.psum_scatter(key_grad, "wide", scatter_dimension=0, tiled=True),
        lax.psum_scatter(value_grad, "wide", scatter_dimension=0, tiled=True),
        lax.psum_scatter(inner_grad, "wide", scatter_dimension=0, tiled=True),
        lax.psum_scatter(first_gain_grad, "wide", scatter_dimension=0, tiled=True),
        lax.psum_scatter(first_bias_grad, "wide", scatter_dimension=0, tiled=True),
        lax.psum_scatter(second_gain_grad, "wide", scatter_dimension=0, tiled=True),
        lax.psum_scatter(second_bias_grad, "wide", scatter_dimension=0, tiled=True),
    )
    output_total, outer_total = (
        lax.psum_scatter(output_grad, "wide", scatter_dimension=1, tiled=True),
        lax.psum_scatter(outer_grad, "wide", scatter_dimension=1, tiled=True),
    )
    return (
        layer_output,
        input_gradient,
        query_total,
        key_total,
        value_total,
        output_total,
        inner_total,
        outer_total,
        first_gain_total,
        first_bias_total,
        second_gain_total,
        second_bias_total,
    )


LOW = jnp.bfloat16
WIDE = jnp.float32
MESH = pl.DeviceIdType.MESH
MEGA = 1 << 20
ANY = pl.BlockSpec(memory_space=pl.ANY)


def contract(left, right, left_dim, right_dim):
    return lax.dot_general(
        left, right, (((left_dim,), (right_dim,)), ((), ())), preferred_element_type=WIDE
    )


def place():
    x = lax.axis_index("narrow")
    w = lax.axis_index("wide")
    c = lax.rem(w, 2)
    y = lax.rem(lax.div(w, 2), 2)
    q = lax.div(w, 4)
    return x, w, c, y, q


class Links:
    def __init__(self, depth):
        self.depth = depth
        self.x, self.w, self.c, self.y, self.q = place()
        self.across = (1 - self.x, self.w)
        self.beside = (self.x, self.w + 2 - 4 * self.y)
        self.sibling = (self.x, self.w + 1 - 2 * self.c)
        self.corner = (1 - self.x, self.w + 1 - 2 * self.c)

    def far(self, step):
        return (self.x, lax.rem(self.w + 4 * step, 4 * self.depth))

    def row(self, step):
        return lax.rem(self.q + self.depth - step, self.depth)

    def meet(self, pair_only=False):
        barrier = pltpu.get_barrier_semaphore()
        others = [self.sibling, self.across, self.corner]
        if not pair_only:
            others += [self.beside]
            others += [self.far(step) for step in range(1, self.depth)]
        for other in others:
            pl.semaphore_signal(barrier, 1, device_id=other, device_id_type=MESH)
        pl.semaphore_wait(barrier, len(others))


def remote(source, target, send, recv, device):
    return pltpu.make_async_remote_copy(
        src_ref=source,
        dst_ref=target,
        send_sem=send,
        recv_sem=recv,
        device_id=device,
        device_id_type=MESH,
    )


def gather_marks(depth):
    return 5 * depth + 2


class Gather:
    def __init__(self, links, own, full, cut, whole, send, recv, index, local):
        self.links, self.own, self.full, self.cut = links, own, full, cut
        self.whole, self.local = whole, local
        self.send = lambda k: send.at[index, k]
        self.recv = lambda k: recv.at[index, k]
        self.width = own.shape[-1]

    def slot(self, h, q, y):
        return self.full.at[h, q, y, self.links.c]

    def low(self, ref):
        return ref.at[:, pl.ds(0, self.cut)]

    def high(self, ref):
        return ref.at[:, pl.ds(self.cut, self.width - self.cut)]

    def copy(self, kind, step=0):
        n, d = self.links, self.links.depth
        mine = self.slot(n.x, n.q, n.y)
        column = self.slot(n.x, n.row(step), n.y)
        first = self.own if step == 0 else column
        if kind == "far":
            return self.move(self.own, mine, step - 1, n.far(step))
        if kind == "across":
            return self.move(first, column, d + step, n.across)
        if kind == "beside":
            return self.move(first, column, 2 * d + step, n.beside)
        if kind == "high":
            part = self.high(self.slot(1 - n.x, n.row(step), n.y))
            return self.move(part, part, 3 * d + step, n.beside)
        if kind == "low":
            part = self.low(self.slot(n.x, n.row(step), 1 - n.y))
            return self.move(part, part, 4 * d + step, n.across)
        part = self.full.at[step if self.whole else 1 - n.c, :, :, n.c]
        return self.move(part, part, 5 * d + step, n.sibling)

    def move(self, source, target, mark, device):
        return remote(source, target, self.send(mark), self.recv(mark), device)

    def arrived(self, target, mark):
        self.move(target, target, mark, self.links.sibling).wait_recv()

    def keep(self):
        n = self.links
        return pltpu.make_async_copy(self.own, self.slot(n.x, n.q, n.y), self.local)

    def begin(self):
        self.begin_far()
        self.begin_near()

    def begin_far(self):
        for step in range(1, self.links.depth):
            self.copy("far", step).start()

    def begin_near(self):
        self.keep().start()
        self.copy("across").start()
        self.copy("beside").start()

    def second(self, step):
        n = self.links
        self.arrived(self.slot(n.x, n.row(step), n.y), step - 1)
        self.copy("across", step).start()
        self.copy("beside", step).start()

    def third(self, step):
        n, d = self.links, self.links.depth
        self.arrived(self.slot(1 - n.x, n.row(step), n.y), d + step)
        self.copy("high", step).start()
        self.arrived(self.slot(n.x, n.row(step), 1 - n.y), 2 * d + step)
        self.copy("low", step).start()

    def fourth(self):
        n, d = self.links, self.links.depth
        for step in range(d):
            got = self.slot(1 - n.x, n.row(step), 1 - n.y)
            self.arrived(self.high(got), 3 * d + step)
            self.arrived(self.low(got), 4 * d + step)
        self.keep().wait()
        for h in range(2 if self.whole else 1):
            self.copy("sibling", h).start()

    def finish(self):
        n, d = self.links, self.links.depth
        for h in range(2 if self.whole else 1):
            self.arrived(self.full.at[h if self.whole else n.c, :, :, 1 - n.c], 5 * d + h)

    def halfway(self):
        n, d = self.links, self.links.depth
        self.keep().wait()
        for step in range(d):
            self.arrived(self.slot(1 - n.x, n.row(step), n.y), d + step)
            self.arrived(self.slot(n.x, n.row(step), 1 - n.y), 2 * d + step)
            if step:
                self.copy("far", step).wait_send()
            for kind in ("across", "beside"):
                self.copy(kind, step).wait_send()

    def close(self):
        d = self.links.depth
        for step in range(d):
            if step:
                self.copy("far", step).wait_send()
            for kind in ("across", "beside", "high", "low"):
                self.copy(kind, step).wait_send()
        for h in range(2 if self.whole else 1):
            self.copy("sibling", h).wait_send()


class Finish:
    def __init__(self, links, full, flat, cut, send, recv, base, local):
        self.links, self.full, self.flat, self.cut, self.local = links, full, flat, cut, local
        self.send = lambda k: send.at[base + k]
        self.recv = lambda k: recv.at[base + k]
        self.r, self.width = full.shape[-2:]

    def slot(self, h, q, y, c):
        w = (q * 2 + y) * 2 + c
        return self.flat.at[h, pl.ds(pl.multiple_of(w * self.r, self.r), self.r)]

    def low(self, ref):
        return ref.at[:, pl.ds(0, self.cut)]

    def high(self, ref):
        return ref.at[:, pl.ds(self.cut, self.width - self.cut)]

    def hop(self, kind, step):
        n, d = self.links, self.links.depth
        q = n.row(step)
        h, y, part, mark, device = {
            "high": (1 - n.x, n.y, self.high, step, n.beside),
            "low": (n.x, 1 - n.y, self.low, d + step, n.across),
        }[kind]
        source, target = part(self.full.at[h, q, y, n.c]), part(self.slot(h, q, y, n.c))
        return remote(source, target, self.send(mark), self.recv(mark), device)

    def spread(self, h, q, y):
        n, d = self.links, self.links.depth
        mark = 2 * d + (h * d + q) * 2 + y
        part = self.slot(h, q, y, n.c)
        return remote(part, part, self.send(mark), self.recv(mark), n.sibling)

    def loads(self):
        n, d = self.links, self.links.depth
        return [
            pltpu.make_async_copy(
                self.full.at[h, q, y, n.c], self.slot(h, q, y, n.c), self.local.at[k * d + q]
            )
            for k, (h, y) in enumerate(((n.x, n.y), (1 - n.x, n.y), (n.x, 1 - n.y)))
            for q in range(d)
        ]

    def everywhere(self, act):
        for h in range(2):
            for q in range(self.links.depth):
                for y in range(2):
                    act(self.spread(h, q, y))

    def begin(self):
        for step in range(self.links.depth):
            self.hop("high", step).start()
            self.hop("low", step).start()
        for item in self.loads():
            item.start()

    def fourth(self):
        n, d = self.links, self.links.depth
        for item in self.loads():
            item.wait()
        for step in range(d):
            got = self.slot(1 - n.x, n.row(step), 1 - n.y, n.c)
            for part, mark in ((self.high(got), step), (self.low(got), d + step)):
                remote(part, part, self.send(mark), self.recv(mark), n.sibling).wait_recv()
        self.everywhere(lambda item: item.start())

    def finish(self):
        n = self.links
        for h in range(2):
            for q in range(n.depth):
                for y in range(2):
                    mark = 2 * n.depth + (h * n.depth + q) * 2 + y
                    got = self.slot(h, q, y, 1 - n.c)
                    remote(got, got, self.send(mark), self.recv(mark), n.sibling).wait_recv()

    def close(self):
        for step in range(self.links.depth):
            self.hop("high", step).wait_send()
            self.hop("low", step).wait_send()
        self.everywhere(lambda item: item.wait_send())


class Share:
    def __init__(self, links, in_ref, rows, note_in, note, gain_in, gain, send, recv, local):
        n = self.links = links
        self.home = n.x == n.c
        s, r = (lambda k: send.at[k]), (lambda k: recv.at[k])
        near, far = rows.at[n.x], rows.at[1 - n.x]
        self.rows_across = lambda: remote(in_ref, near, s(0), r(0), n.across)
        self.rows_beside = lambda: remote(in_ref, near, s(1), r(1), n.sibling)
        self.rows_further = lambda: remote(far, far, s(2), r(2), n.sibling)
        self.note = lambda: remote(note_in, note, s(3), r(3), n.sibling)
        self.gain = lambda: remote(gain_in, gain.at[n.x], s(4), r(4), n.across)
        self.gain_keep = lambda: pltpu.make_async_copy(gain_in, gain.at[n.x], local.at[0])
        self.rows_keep = lambda: pltpu.make_async_copy(in_ref, near, local.at[1])
        self.note_keep = lambda: pltpu.make_async_copy(note_in, note, local.at[2])

    def begin(self):
        @pl.when(self.home)
        def _():
            self.note().start()
            self.rows_beside().start()
            self.rows_keep().start()
            self.note_keep().start()

        @pl.when(jnp.logical_not(self.home))
        def _():
            self.rows_across().start()

    def further(self):
        self.gain().start()
        self.gain_keep().start()

        @pl.when(self.home)
        def _():
            self.rows_across().wait_recv()
            self.rows_further().start()
            self.rows_keep().wait()
            self.note_keep().wait()

        @pl.when(jnp.logical_not(self.home))
        def _():
            self.note().wait_recv()
            self.rows_beside().wait_recv()
            self.rows_further().wait_recv()

        self.gain_keep().wait()

    def finish(self):
        self.gain().wait()

        @pl.when(self.home)
        def _():
            self.note().wait_send()
            self.rows_beside().wait_send()
            self.rows_further().wait_send()

        @pl.when(jnp.logical_not(self.home))
        def _():
            self.rows_across().wait_send()


class Pull:
    def __init__(self, links, source, target, send, recv, base, local):
        n = self.links = links
        half = source.shape[0] // 2
        self.home = n.x == n.c
        s, r = (lambda k: send.at[base + k]), (lambda k: recv.at[base + k])
        mine, theirs = source.at[pl.ds(n.c * half, half)], source.at[pl.ds((1 - n.c) * half, half)]
        near = target.at[n.x]
        self.keep = lambda: pltpu.make_async_copy(mine, near, local)
        self.beside = lambda: remote(theirs, near, s(0), r(0), n.sibling)
        self.across = lambda: remote(mine, near, s(1), r(1), n.across)
        self.corner = lambda: remote(theirs, near, s(2), r(2), n.corner)

    def begin(self):
        @pl.when(self.home)
        def _():
            self.keep().start()
            self.beside().start()

        @pl.when(jnp.logical_not(self.home))
        def _():
            self.across().start()
            self.corner().start()

    def finish(self):
        @pl.when(self.home)
        def _():
            self.keep().wait()
            self.beside().wait_send()
            self.across().wait_recv()

        @pl.when(jnp.logical_not(self.home))
        def _():
            self.across().wait_send()
            self.corner().wait_send()
            self.beside().wait_recv()
            self.corner().wait_recv()


def plus(left, right):
    return (left.astype(WIDE) + right.astype(WIDE)).astype(left.dtype)


def scatter_marks(depth):
    return depth + 5


class Scatter:
    def __init__(self, links, kind, part, cut, bufs, out, send, recv, index, local):
        self.links, self.kind, self.part, self.cut, self.out = links, kind, part, cut, out
        self.held, self.other, self.x1, self.y1, self.x2, self.y2, self.z = bufs
        self.send = lambda k: send.at[index, k]
        self.recv = lambda k: recv.at[index, k]
        self.local = local
        self.rest = self.held.shape[-1] - cut

    def low(self, ref):
        return ref.at[:, :, pl.ds(0, self.cut)]

    def high(self, ref):
        return ref.at[:, :, pl.ds(self.cut, self.rest)]

    def move(self, source, target, mark, device):
        return remote(source, target, self.send(mark), self.recv(mark), device)

    def copy(self, kind, step=0):
        n = self.links
        if kind == "sibling" and self.kind == "join":
            return self.move(self.part.at[:, :, :, 1 - n.c], self.other, 0, n.sibling)
        if kind == "sibling":
            return self.move(self.part.at[:, :, 1 - n.c], self.held.at[n.c], 0, n.sibling)
        if kind == "x1":
            return self.move(self.low(self.held.at[1 - n.x, :, 1 - n.y]), self.x1, 1, n.across)
        if kind == "y1":
            return self.move(self.high(self.held.at[1 - n.x, :, 1 - n.y]), self.y1, 2, n.beside)
        source = self.part if self.kind == "later" else self.held
        if kind == "y2":
            return self.move(source.at[n.x, :, 1 - n.y], self.y2, 3, n.beside)
        if kind == "x2":
            return self.move(source.at[1 - n.x, :, n.y], self.x2, 4, n.across)
        q = lax.rem(n.q + step, n.depth)
        return self.move(self.mine(q), self.z.at[step - 1], 4 + step, n.far(step))

    def mine(self, q):
        n = self.links
        return self.held.at[q] if self.kind == "later" else self.held.at[n.x, q, n.y]

    def keep(self):
        n = self.links
        if self.kind == "later":
            return pltpu.make_async_copy(self.part.at[n.x, :, n.y], self.held, self.local)
        if self.kind == "join":
            return pltpu.make_async_copy(self.part.at[:, :, :, n.c], self.held, self.local)
        return pltpu.make_async_copy(self.part.at[:, :, n.c], self.held.at[n.c], self.local)

    def arrived(self, target, mark):
        self.move(target, target, mark, self.links.sibling).wait_recv()

    def begin(self):
        self.keep().start()
        if self.kind != "later":
            self.copy("sibling").start()
        else:
            self.copy("x2").start()
            self.copy("y2").start()

    def first(self):
        n = self.links
        self.keep().wait()
        if self.kind == "join":
            self.arrived(self.other, 0)
            self.held[...] = plus(self.held[...], self.other[...])
        if self.kind == "swap":
            self.arrived(self.held.at[1 - n.c], 0)
        self.copy("x1").start()
        self.copy("y1").start()

    def second(self):
        n = self.links
        low, high = pl.ds(0, self.cut), pl.ds(self.cut, self.rest)
        self.arrived(self.x1, 1)
        for q in range(n.depth):
            self.held[n.x, q, 1 - n.y, :, low] = plus(
                self.held[n.x, q, 1 - n.y, :, low], self.x1[q]
            )
        self.copy("y2").start()
        self.arrived(self.y1, 2)
        for q in range(n.depth):
            self.held[1 - n.x, q, n.y, :, high] = plus(
                self.held[1 - n.x, q, n.y, :, high], self.y1[q]
            )
        self.copy("x2").start()

    def third(self):
        n = self.links
        if self.kind == "later":
            self.keep().wait()
        self.arrived(self.y2, 3)
        self.arrived(self.x2, 4)
        for step in range(1, n.depth):
            q = lax.rem(n.q + step, n.depth)
            mine = self.mine(q)
            mine[...] = plus(plus(mine[...], self.x2[q]), self.y2[q])
            self.copy("z", step).start()

    def fourth(self):
        n = self.links
        total = (
            self.mine(n.q)[...].astype(WIDE)
            + self.x2[n.q].astype(WIDE)
            + self.y2[n.q].astype(WIDE)
        )
        for step in range(1, n.depth):
            self.arrived(self.z.at[step - 1], 4 + step)
            total = total + self.z[step - 1].astype(WIDE)
        self.out(total)

    def close(self):
        first = () if self.kind == "later" else ("sibling", "x1", "y1")
        for kind in first + ("x2", "y2"):
            self.copy(kind).wait_send()
        for step in range(1, self.links.depth):
            self.copy("z", step).wait_send()


def scatter_scratch(depth, r, columns, cut, kind="swap", of=LOW):
    small = (8, 128)
    later = kind == "later"
    return [
        pltpu.VMEM((depth, r, columns) if later else (2, depth, 2, r, columns), of),
        pltpu.VMEM((2, depth, 2, r, columns) if kind == "join" else small, of),
        pltpu.VMEM(small if later else (depth, r, cut), of),
        pltpu.VMEM(small if later else (depth, r, columns - cut), of),
        pltpu.VMEM((depth, r, columns), of),
        pltpu.VMEM((depth, r, columns), of),
        pltpu.VMEM((depth - 1, r, columns), of),
    ]


class HandOver:
    def __init__(self, links, source, target, send, recv, base, local):
        self.links, self.source, self.target, self.local = links, source, target, local
        self.send = lambda k: send.at[base + k]
        self.recv = lambda k: recv.at[base + k]
        self.half = source.shape[1]

    def rows(self, c):
        return self.target.at[pl.ds(c * self.half, self.half)]

    def copies(self):
        n = self.links
        near, far = self.source.at[n.x], self.source.at[1 - n.x]
        mine = self.rows(n.c)
        return (
            pltpu.make_async_copy(near, mine, self.local),
            remote(far, mine, self.send(0), self.recv(0), n.across),
            remote(near, mine, self.send(1), self.recv(1), n.sibling),
            remote(far, mine, self.send(2), self.recv(2), n.corner),
        )

    def begin(self):
        n = self.links
        keep, across, sibling, corner = self.copies()

        @pl.when(n.x == n.c)
        def _():
            keep.start()
            across.start()

        @pl.when(n.x != n.c)
        def _():
            sibling.start()
            corner.start()

    def finish(self):
        n = self.links
        keep, across, sibling, corner = self.copies()
        mine, theirs = self.rows(n.c), self.rows(1 - n.c)

        @pl.when(n.x == n.c)
        def _():
            keep.wait()
            across.wait_send()
            remote(theirs, theirs, self.send(1), self.recv(1), n.sibling).wait_recv()

        @pl.when(n.x != n.c)
        def _():
            sibling.wait_send()
            corner.wait_send()
            remote(mine, mine, self.send(0), self.recv(0), n.across).wait_recv()
            remote(theirs, theirs, self.send(2), self.recv(2), n.corner).wait_recv()


def angle_tables():
    rates = THETA ** (-np.arange(HEAD_DIM // 2) / (HEAD_DIM // 2))
    rates = np.tile(rates, 4)[None]
    base = np.arange(BLOCK)[:, None] * rates
    jump = np.arange(SPAN)[:, None] * BLOCK * rates
    base = np.concatenate([np.cos(base), np.sin(base)], axis=0)
    jump = np.concatenate([np.cos(jump), np.sin(jump), np.zeros((2, 128))], axis=0)
    return jnp.asarray(base, WIDE), jnp.asarray(jump, WIDE)


def lanes(rows):
    return lax.broadcasted_iota(jnp.int32, (rows, 128), 1)


def turn_parts(meta, base, jump, block):
    segment = meta[0, block]
    earlier = [(meta[0, other] < segment).astype(jnp.int32) for other in range(SPAN)]
    offset = block - sum(earlier)
    far_cos = jump[pl.ds(offset, 1), :]
    far_sin = jump[pl.ds(SPAN + offset, 1), :]
    near_cos, near_sin = base[0:BLOCK], base[BLOCK : 2 * BLOCK]
    cosine = near_cos * far_cos - near_sin * far_sin
    sine = near_sin * far_cos + near_cos * far_sin
    low = (lanes(BLOCK) % HEAD_DIM) < HEAD_DIM // 2
    return cosine, jnp.where(low, -sine, sine), low


def turn(values, cosine, sine, low):
    swapped = jnp.where(low, pltpu.roll(values, 96, 1), pltpu.roll(values, 32, 1))
    return values * cosine + swapped * sine


def weight_loads(full, h, flat, marks):
    depth, r = full.shape[1], full.shape[4]
    return [
        pltpu.make_async_copy(
            full.at[h, q, y, c], flat.at[pl.ds(k * r, r)], marks.at[k]
        )
        for k, (q, y, c) in enumerate(
            (q, y, c) for q in range(depth) for y in range(2) for c in range(2)
        )
    ]


def forward_kernel(depth, cuts, note_in, in_ref, gain1, gain2, gain3, gain4, query, key, value, output,
                   inner, o_own, base, jump,
                   note, gain, rows, q_full, m_full, o_full, all_context, q_ref, k_ref, v_ref,
                   p_ref, r_ref, c_ref, marks, meta, held, weight, gain_in, q_own, m_own, piece, send, recv, local, extra_send,
                   extra_recv, context_send, context_recv):
    step = pl.program_id(0)
    scale = HEAD_DIM ** (-0.5)
    n = Links(depth)
    half = in_ref.shape[0] // 2
    gathers = [
        Gather(n, own, full, cut, whole, send, recv, k, local.at[k])
        for k, (own, full, cut, whole) in enumerate(
            zip((q_own, m_own, o_own), (q_full, m_full, o_full), cuts, (False, True, True))
        )
    ]
    share = Share(
        n, in_ref, held, note_in, note, gain_in, gain, extra_send, extra_recv, local.at[pl.ds(3, 3)]
    )
    rows_keep = lambda: pltpu.make_async_copy(held, rows, local.at[7])

    def context_copy(p):
        there = c_ref.at[p, pl.ds((1 - n.c) * half, half)]
        return remote(there, all_context.at[n.c, p], context_send.at[p], context_recv.at[p], n.sibling)

    def context_keep(p):
        here = c_ref.at[p, pl.ds(n.c * half, half)]
        return pltpu.make_async_copy(here, all_context.at[n.c, p], local.at[10 + p])

    @pl.when(step == 0)
    def _():
        for k, item in enumerate((gain1, gain2, gain3, gain4)):
            gain_in[k : k + 1] = item[...].reshape(1, -1)
            gain_in[4 + k : 5 + k] = item[...].reshape(1, -1)
        for p in range(3):
            for k, item in enumerate((query, key, value)):
                column = p * 384 + k * 128
                q_own[:, column : column + 128] = item[:, p * 128 : (p + 1) * 128]
        m_own[:, 0 : output.shape[1]] = output[...]
        m_own[:, output.shape[1] :] = inner[...]
        n.meet()
        gathers[0].begin()
        share.begin()
        gathers[1].begin_far()
        gathers[2].begin_far()
        for k in range(1, depth):
            gathers[0].second(k)
        for k in range(depth):
            gathers[0].third(k)
        gathers[1].begin_near()
        gathers[2].begin_near()
        share.further()
        rows_keep().start()
        loads = [pltpu.make_async_copy(note, meta, local.at[8])]
        loads[0].start()
        gathers[0].fourth()
        gathers[0].finish()
        loads += weight_loads(q_full, n.c, weight, piece)
        for item in loads[1:]:
            item.start()
        for item in loads:
            item.wait()

    hooks = {
        2: [functools.partial(gathers[1].second, k) for k in range(1, depth)],
        4: [functools.partial(gathers[2].second, k) for k in range(1, depth)],
        6: [functools.partial(gathers[1].third, k) for k in range(depth)],
        10: [gathers[1].fourth],
    }
    for at, actions in hooks.items():

        @pl.when(step == at)
        def _():
            for action in actions:
                action()

    @pl.when(step < SPAN)
    def _():
        here = pl.ds(step * BLOCK, BLOCK)
        cosine, sine, low = turn_parts(meta, base, jump, step)
        values = jnp.concatenate([held[0, here], held[1, here]], axis=1)

        for p in range(3):
            made = contract(values, weight[:, p * 384 : p * 384 + 384], 1, 0)
            q_ref[p, here] = (turn(made[:, 0:128], cosine, sine, low) * scale).astype(LOW)
            k_ref[p, here] = turn(made[:, 128:256], cosine, sine, low).astype(LOW)
            v_ref[p, here] = made[:, 256:384].astype(LOW)
        marks[here] = (lanes(BLOCK) == meta[0, step]).astype(WIDE).astype(LOW)

    @pl.when(step >= SPAN)
    def _():
        turn_number = step - SPAN
        p = turn_number // SPAN
        i = turn_number % SPAN
        here = pl.ds(i * BLOCK, BLOCK)
        lane = lanes(BLOCK)
        queries = q_ref[p, here]
        values = v_ref[p]
        keys = jnp.concatenate([k_ref[p], marks[...]], axis=1)
        barred = jnp.where((lane < SPAN) & (lane != meta[0, i]), NEGATIVE, 0.0).astype(LOW)
        outs = []
        scales = []
        for head in range(2):
            chosen = (lane // HEAD_DIM) == head
            ours = jnp.concatenate([jnp.where(chosen, queries, 0).astype(LOW), barred], axis=1)
            scores = contract(ours, keys, 1, 1)
            top = jnp.max(scores, axis=1, keepdims=True)
            raised = jnp.exp(scores - top)
            inverse = 1.0 / jnp.sum(raised, axis=1, keepdims=True)
            soft = raised.astype(LOW)
            p_ref[0, head] = soft
            outs.append(contract(soft, values, 1, 0))
            scales.append(inverse)
        inverse = jnp.where(lane < HEAD_DIM, scales[0], scales[1])
        r_ref[p, here] = inverse
        c_ref[p, here] = (jnp.where(lane < HEAD_DIM, outs[0], outs[1]) * inverse).astype(LOW)

    for p in range(3):

        @pl.when(step == 2 * SPAN - 1 + p * SPAN)
        def _():
            context_copy(p).start()
            context_keep(p).start()

    @pl.when(step == 4 * SPAN - 1)
    def _():
        gathers[1].finish()
        gathers[2].halfway()
        gathers[0].close()
        gathers[1].close()
        share.finish()
        rows_keep().wait()
        for p in range(3):
            context_copy(p).wait()
            context_keep(p).wait()


def forward_call(depth, cuts, note, gains, rows, weights, base, jump):
    length, part = rows.shape
    half = length // 2
    r, hidden = weights[-1].shape
    columns = (3 * part, part + hidden, hidden)
    low = lambda *shape: jax.ShapeDtypeStruct(shape, LOW)
    full = [low(2, depth, 2, 2, r, item) for item in columns]
    trio = low(3, length, 128)
    vmem = pl.BlockSpec(memory_space=pltpu.VMEM)
    marks = pltpu.SemaphoreType.DMA((3, gather_marks(depth)))
    return pl.pallas_call(
        functools.partial(forward_kernel, depth, cuts),
        grid=(SPAN + 3 * SPAN,),
        out_shape=[
            jax.ShapeDtypeStruct(note.shape, note.dtype),
            jax.ShapeDtypeStruct((2, 8, part), WIDE),
            low(2, length, part),
        ]
        + full
        + [
            low(2, 3, half, 128),
            trio,
            trio,
            trio,
            low(SPAN * 3, 2, BLOCK, length),
            jax.ShapeDtypeStruct((3, length, 128), WIDE),
            trio,
        ],
        in_specs=[ANY] * 2 + [once(item.shape) for item in (*gains, *weights, base, jump)],
        out_specs=[ANY] * 7
        + [vmem] * 3
        + [
            pl.BlockSpec((1, 2, BLOCK, length), lambda s: (jnp.maximum(s - SPAN, 0), 0, 0, 0)),
            vmem,
            vmem,
        ],
        scratch_shapes=[
            pltpu.VMEM((length, 128), LOW),
            pltpu.SMEM(note.shape, note.dtype),
            pltpu.VMEM((2, length, part), LOW),
            pltpu.VMEM((4 * depth * r, columns[0]), LOW),
            pltpu.VMEM((8, part), WIDE),
            pltpu.VMEM((r, columns[0]), LOW),
            pltpu.VMEM((r, columns[1]), LOW),
            pltpu.SemaphoreType.DMA((4 * depth,)),
            marks,
            marks,
            pltpu.SemaphoreType.DMA((13,)),
            pltpu.SemaphoreType.DMA((8,)),
            pltpu.SemaphoreType.DMA((8,)),
            pltpu.SemaphoreType.DMA((3,)),
            pltpu.SemaphoreType.DMA((3,)),
        ],
        compiler_params=pltpu.CompilerParams(
            collective_id=0, has_side_effects=True, vmem_limit_bytes=60 * MEGA
        ),
        name="attend",
    )(note, rows, *gains, *weights, base, jump)


def norm_of(summed):
    mean = jnp.mean(summed, axis=1, keepdims=True)
    centred = summed - mean
    variance = jnp.mean(centred * centred, axis=1, keepdims=True)
    scale = lax.rsqrt(variance + EPSILON)
    return centred * scale, scale


def norm_back(scaled, normed, scale):
    total = jnp.mean(scaled, axis=1, keepdims=True)
    cross = jnp.mean(scaled * normed, axis=1, keepdims=True)
    return scale * (scaled - total - normed * cross)


HIDDEN = 512


def middle_kernel(depth, cuts, context, rows, gains, cot_in, m_full, o_full, lo_out, gfs_ref, sums, grads,
                  o_held, m_held, m_mat, o_mat, act, gi, fl, gm, ga, gc, n1, n2, scales, cot, lo,
                  o_part, m_part, o_other, m_other, ox, oy, mx, my, local, send, recv, load):
    step = pl.program_id(0)
    tile, part = rows.shape[1:]
    half = fl.shape[0]
    tiles = half // tile
    r = o_part.shape[-2]
    pieces = o_mat.shape[2] // HIDDEN
    width = pieces * HIDDEN
    n = Links(depth)
    here = pl.ds(lax.rem(step, tiles) * tile, tile)
    pull = Pull(n, cot_in, cot, send, recv, 5, local.at[7])
    lo_over = HandOver(n, lo, lo_out, send, recv, 8, local.at[8])
    finish = Finish(n, o_full, o_mat, cuts[0], send, recv, 15, load)
    m_load = lambda: pltpu.make_async_copy(m_full, m_mat, local.at[0])

    def grads_keep():
        own = grads.at[:, pl.ds(n.c * half, half)]
        return pltpu.make_async_copy(gc.at[n.c], own, local.at[2])

    def grads_copy():
        own = grads.at[:, pl.ds(n.c * half, half)]
        return remote(gc.at[1 - n.c], own, send.at[4], recv.at[4], n.sibling)

    order = ((0, 1 - n.x), (1, 1 - n.x), (0, n.x), (1, n.x))
    chunks = ((o_part, o_other, ox, oy, o_held), (m_part, m_other, mx, my, m_held))

    def part_copy(k):
        chunk, h = order[k]
        source, target = chunks[chunk][:2]
        return remote(
            source.at[h, :, :, 1 - n.c], target.at[h], send.at[k], recv.at[k], n.sibling
        )

    def join(k):
        chunk, h = order[k]
        source, target = chunks[chunk][:2]
        part_copy(k).wait_recv()
        for q in range(depth):
            for y in range(2):
                target[h, q, y] = plus(source[h, q, y, n.c], target[h, q, y])

    def hop(chunk, across):
        target, x1, y1 = chunks[chunk][1:4]
        corner = target.at[1 - n.x, :, 1 - n.y]
        mark = 11 + 2 * chunk + across
        if across:
            part = corner.at[:, :, pl.ds(0, x1.shape[-1])]
            return remote(part, x1, send.at[mark], recv.at[mark], n.across)
        part = corner.at[:, :, pl.ds(x1.shape[-1], y1.shape[-1])]
        return remote(part, y1, send.at[mark], recv.at[mark], n.beside)

    def land(chunk):
        target, x1, y1, held = chunks[chunk][1:5]
        low, high = pl.ds(0, x1.shape[-1]), pl.ds(x1.shape[-1], y1.shape[-1])
        hop(chunk, True).wait_recv()
        hop(chunk, False).wait_recv()
        for q in range(depth):
            target[n.x, q, 1 - n.y, :, low] = plus(target[n.x, q, 1 - n.y, :, low], x1[q])
            target[1 - n.x, q, n.y, :, high] = plus(target[1 - n.x, q, n.y, :, high], y1[q])

    def held_copy(chunk):
        return pltpu.make_async_copy(chunks[chunk][1], chunks[chunk][4], local.at[3 + chunk])

    @pl.when(step == 0)
    def _():
        m_load().start()
        n.meet()
        finish.begin()
        pull.begin()
        m_load().wait()

    @pl.when(step < tiles)
    def _():
        whole = jnp.concatenate([gains[0], gains[1]], axis=1)
        gain1, bias1, gain2, bias2 = (whole[k : k + 1, :] for k in range(4))
        summed = jnp.concatenate([rows[0], rows[1]], axis=1).astype(WIDE)
        for h in range(2):
            seen = jnp.concatenate([context[h, p, here] for p in range(3)], axis=1)
            summed = summed + contract(seen, m_mat[h, :, 0:part], 1, 1)
        normed1, scale1 = norm_of(summed)
        n1[here] = normed1
        scales[here, 0:1] = scale1
        first = normed1 * gain1 + bias1
        first_low = first.astype(LOW)
        fl[here] = first_low
        for h in range(2):
            for j in range(pieces):
                lo_end = part + j * HIDDEN
                there = slice(h * width + j * HIDDEN, h * width + (j + 1) * HIDDEN)
                inner = contract(first_low, m_mat[h, :, lo_end : lo_end + HIDDEN], 1, 0)
                share = 0.5 * (1.0 + lax.erf(inner * ROOT_HALF))
                slope = share + inner * jnp.exp(-0.5 * inner * inner) * INVERSE_ROOT
                gi[here, there] = slope.astype(LOW)
                act[here, there] = (inner * share).astype(LOW)

    @pl.when(step == tiles)
    def _():
        finish.fourth()
        finish.finish()

    @pl.when((step >= tiles) & (step < 2 * tiles))
    def _():
        whole = jnp.concatenate([gains[0], gains[1]], axis=1)
        gain1, bias1, gain2, bias2 = (whole[k : k + 1, :] for k in range(4))
        mixed = n1[here] * gain1 + bias1
        for h in range(2):
            mixed = mixed + contract(act[here, h * width : (h + 1) * width], o_mat[h], 1, 1)
        normed2, scale2 = norm_of(mixed)
        n2[here] = normed2
        scales[here, 1:2] = scale2
        result = (normed2 * gain2 + bias2).astype(LOW)
        for h in range(2):
            lo[h, here] = result[:, h * part : (h + 1) * part]

    @pl.when(step == 2 * tiles)
    def _():
        pull.finish()
        lo_over.begin()

    @pl.when((step >= 2 * tiles) & (step < 3 * tiles))
    def _():
        whole = jnp.concatenate([gains[0], gains[1]], axis=1)
        gain1, bias1, gain2, bias2 = (whole[k : k + 1, :] for k in range(4))
        normed1, scale1 = n1[here], scales[here, 0:1]
        normed2, scale2 = n2[here], scales[here, 1:2]
        cotangent = jnp.concatenate([cot[0, here], cot[1, here]], axis=1).astype(WIDE)
        second_gain = jnp.sum(cotangent * normed2, axis=0, keepdims=True)
        second_bias = jnp.sum(cotangent, axis=0, keepdims=True)
        grad_second = norm_back(cotangent * gain2, normed2, scale2)
        grad_mixed = grad_second.astype(LOW)
        gm[here] = grad_mixed
        for h in range(2):
            for j in range(pieces):
                there = slice(h * width + j * HIDDEN, h * width + (j + 1) * HIDDEN)
                raised = contract(grad_mixed, o_mat[h, :, j * HIDDEN : (j + 1) * HIDDEN], 1, 0)
                gi[here, there] = (raised * gi[here, there].astype(WIDE)).astype(LOW)
        grad_first = grad_second
        for h in range(2):
            grad_first = grad_first + contract(
                gi[here, h * width : (h + 1) * width], m_mat[h, :, part : part + width], 1, 1
            )
        first_gain = jnp.sum(grad_first * normed1, axis=0, keepdims=True)
        first_bias = jnp.sum(grad_first, axis=0, keepdims=True)
        grad_sum = norm_back(grad_first * gain1, normed1, scale1)
        gfs_ref[...] = grad_sum
        grad_attended = grad_sum.astype(LOW)
        ga[here] = grad_attended
        for h in range(2):
            made = contract(grad_attended, m_mat[h, :, 0:part], 1, 0).astype(LOW)
            for p in range(3):
                gc[h, p, here] = made[:, p * 128 : (p + 1) * 128]
        found = jnp.concatenate([first_gain, first_bias, second_gain, second_bias], axis=0)

        @pl.when(step == 2 * tiles)
        def _():
            sums[...] = found

        @pl.when(step > 2 * tiles)
        def _():
            sums[...] += found

    @pl.when(step == 3 * tiles - 1)
    def _():
        grads_keep().start()
        grads_copy().start()

    def put(target, h, row, column, values):
        shards = values.shape[0] // r
        for k in range(shards):
            w = row // r + k
            target[h, w // 4, (w // 2) % 2, w % 2, :, column : column + values.shape[1]] = values[
                k * r : (k + 1) * r
            ]

    for k in range(4):

        @pl.when(step == 3 * tiles + k)
        def _():
            chunk, h = order[k]
            target = chunks[chunk][0]
            for row in range(0, 2 * part, part):
                for j in range(pieces):
                    start = pl.multiple_of(h * width + j * HIDDEN, HIDDEN)
                    there = pl.ds(start, HIDDEN)
                    if chunk == 0:
                        made = contract(gm[:, row : row + part], act[:, there], 0, 0)
                        put(target, h, row, j * HIDDEN, made.astype(LOW))
                    else:
                        made = contract(fl[:, row : row + part], gi[:, there], 0, 0)
                        put(target, h, row, part + j * HIDDEN, made.astype(LOW))
                if chunk == 1:
                    seen = jnp.concatenate([context[h, p] for p in range(3)], axis=1)
                    made = contract(ga[:, row : row + part], seen, 0, 0)
                    put(target, h, row, 0, made.astype(LOW))
            part_copy(k).start()
            if k:
                join(k - 1)
            if k in (1, 2):
                hop(k - 1, True).start()
                hop(k - 1, False).start()
            if k == 3:
                land(0)
                held_copy(0).start()
                join(3)
                land(1)
                held_copy(1).start()
                grads_keep().wait()
                grads_copy().wait()
                for item in range(4):
                    part_copy(item).wait_send()
                for item in range(2):
                    hop(item, True).wait_send()
                    hop(item, False).wait_send()
                    held_copy(item).wait()
                lo_over.finish()
                finish.close()


def once(shape):
    zeros = (0,) * len(shape)
    return pl.BlockSpec(shape, lambda *_: zeros, pipeline_mode=pl.Buffered(1))


def middle_call(depth, cuts, context, rows, cot, m_full, o_full, gains):
    tile = 256
    half, part = cot.shape[0] // 2, cot.shape[1]
    tiles = half // tile
    width = 2 * part
    hidden = 2 * o_full.shape[-1]
    r = width // (4 * depth)
    columns = (o_full.shape[-1], m_full.shape[2])
    low = lambda *shape: jax.ShapeDtypeStruct(shape, LOW)
    held = [(2, depth, 2, r, item) for item in columns]
    last = lambda i: jnp.minimum(i, tiles - 1)
    later = lambda i: jnp.clip(i - 2 * tiles, 0, tiles - 1)
    c = lambda: lax.rem(lax.axis_index("wide"), 2)
    return pl.pallas_call(
        functools.partial(middle_kernel, depth, cuts),
        grid=(3 * tiles + 4,),
        out_shape=[
            low(2 * half, part),
            jax.ShapeDtypeStruct((half, width), WIDE),
            jax.ShapeDtypeStruct((4, width), WIDE),
            low(3, 2 * half, 128),
        ]
        + [low(*item) for item in held],
        in_specs=[
            once((2, 3, half, 128)),
            pl.BlockSpec((2, tile, part), lambda i: (0, c() * tiles + last(i), 0)),
            once(gains.shape),
            ANY,
            ANY,
            ANY,
        ],
        out_specs=[
            ANY,
            pl.BlockSpec((tile, width), lambda i: (later(i), 0)),
            pl.BlockSpec((4, width), lambda i: (0, 0)),
            ANY,
            ANY,
            ANY,
        ],
        scratch_shapes=[
            pltpu.VMEM(m_full.shape, LOW),
            pltpu.VMEM((2, width, columns[0]), LOW),
            pltpu.VMEM((half, hidden), LOW),
            pltpu.VMEM((half, hidden), LOW),
            pltpu.VMEM((half, width), LOW),
            pltpu.VMEM((half, width), LOW),
            pltpu.VMEM((half, width), LOW),
            pltpu.VMEM((2, 3, half, 128), LOW),
            pltpu.VMEM((half, width), WIDE),
            pltpu.VMEM((half, width), WIDE),
            pltpu.VMEM((half, 2), WIDE),
            pltpu.VMEM((2, half, part), LOW),
            pltpu.VMEM((2, half, part), LOW),
        ]
        + [pltpu.VMEM((2, depth, 2, 2, r, item), LOW) for item in columns]
        + [pltpu.VMEM(item, LOW) for item in held]
        + [
            pltpu.VMEM((depth, r, item), LOW)
            for whole, cut in zip(columns, cuts)
            for item in (cut, whole - cut)
        ]
        + [
            pltpu.SemaphoreType.DMA((9,)),
            pltpu.SemaphoreType.DMA((15 + 6 * depth,)),
            pltpu.SemaphoreType.DMA((15 + 6 * depth,)),
            pltpu.SemaphoreType.DMA((3 * depth,)),
        ],
        compiler_params=pltpu.CompilerParams(
            collective_id=1, has_side_effects=True, vmem_limit_bytes=62 * MEGA
        ),
        name="middle",
    )(context, rows, gains, cot, m_full, o_full)


def backward_kernel(depth, cuts, meta, base, jump, soft, grads, context, inverse, q_ref, k_ref, v_ref,
                    rows, kept, q_full, o_in, m_in, t_in, dx_out, o_out, m_out,
                    i_out, q_out, k_out, v_out, t_out, *scratch):
    ones, keys_sum, values_sum, made, weight, q_part, dx_own, dx_give, dx_other = scratch[:9]
    bufs = [scratch[9 + 7 * k : 16 + 7 * k] for k in range(6)]
    piece, send, recv, local, extra_send, extra_recv = scratch[51:]
    step = pl.program_id(0)
    p = step // SPAN
    i = step % SPAN
    length = q_ref.shape[1]
    scale = HEAD_DIM ** (-0.5)
    lane = lanes(BLOCK)
    here = pl.ds(i * BLOCK, BLOCK)
    n = Links(depth)
    r = o_in.shape[-2]
    half, width = kept.shape
    part = width // 2
    kinds = ("later", "later", "swap", "swap", "swap", "join")
    parts = (o_in, m_in) + tuple(q_part.at[k] for k in range(3)) + (t_in,)

    def put_pair(p, total):
        for k, item in enumerate((q_out, k_out, v_out)):
            item[:, p * 128 : (p + 1) * 128] = total[:, k * 128 : (k + 1) * 128]

    def put_whole(target, total):
        target[...] = total

    def put_inner(total):
        m_out[...] = total[:, 0:part]
        i_out[...] = total[:, part:]

    outs = [functools.partial(put_whole, o_out), put_inner]
    outs += [functools.partial(put_pair, k) for k in range(3)]
    outs += [functools.partial(put_whole, t_out)]
    every = [
        Scatter(n, kind, item, cut, buf, out, send, recv, k, local.at[k])
        for k, (kind, item, cut, buf, out) in enumerate(zip(kinds, parts, cuts, bufs, outs))
    ]
    outer, inner, pair0, pair1, pair2, small = every
    dx_over = HandOver(n, dx_own, dx_out, extra_send, extra_recv, 0, local.at[6])
    dx_swap = lambda: remote(dx_give, dx_other, extra_send.at[3], extra_recv.at[3], n.sibling)

    @pl.when(step == 0)
    def _():
        ones[...] = (lanes(length) < 2).astype(WIDE).astype(LOW)
        for item in weight_loads(q_full, n.c, weight, piece):
            item.start()
        n.meet()
        small.begin()
        small.first()
        outer.begin()
        inner.begin()
        for item in weight_loads(q_full, n.c, weight, piece):
            item.wait()

    hooks = {
        1: [small.second],
        3: [outer.third, pair0.first],
        5: [inner.third, small.third],
        6: [outer.fourth, pair0.second, pair1.first],
        7: [pair0.third, pair1.second],
        8: [pair1.third, inner.fourth, small.fourth],
    }
    for at, actions in hooks.items():

        @pl.when(step == at)
        def _():
            for action in actions:
                action()

    grad = grads[p, here].astype(WIDE)
    turned = grad * inverse[p, here]
    both = turned * context[p, here].astype(WIDE)
    turned_low = turned.astype(LOW)
    queries = q_ref[p, here]
    keys = k_ref[p]
    values = jnp.concatenate([v_ref[p], ones[...]], axis=1)
    turned_flip = jnp.transpose(turned).astype(LOW)
    queries_flip = jnp.transpose(queries.astype(WIDE)).astype(LOW)
    found = []
    for head in range(2):
        chosen = (lane // HEAD_DIM) == head
        centre = -jnp.sum(jnp.where(chosen, both, 0.0), axis=1, keepdims=True)
        coarse = centre.astype(LOW).astype(WIDE)
        fine = jnp.where(lane == 0, coarse, jnp.where(lane == 1, centre - coarse, 0.0))
        ours = jnp.concatenate(
            [jnp.where(chosen, turned_low, 0).astype(LOW), fine.astype(LOW)], axis=1
        )
        raised = soft[0, head]
        scores = (contract(ours, values, 1, 1) * raised.astype(WIDE)).astype(LOW)
        found.append(contract(scores, keys, 1, 0))
        mine = slice(head * HEAD_DIM, (head + 1) * HEAD_DIM)
        values_add = contract(turned_flip[mine], raised, 1, 0)
        keys_add = contract(queries_flip[mine], scores, 1, 0)

        @pl.when(i == 0)
        def _():
            values_sum[mine] = values_add
            keys_sum[mine] = keys_add

        @pl.when(i > 0)
        def _():
            values_sum[mine] += values_add
            keys_sum[mine] += keys_add

    cosine, sine, low = turn_parts(meta, base, jump, i)
    grad_queries = jnp.where(lane < HEAD_DIM, found[0], found[1]) * scale
    made[p, here, 0:128] = turn(grad_queries, cosine, -sine, low).astype(LOW)

    @pl.when(i == SPAN - 1)
    def _():
        grad_keys = jnp.transpose(keys_sum[...])
        grad_values = jnp.transpose(values_sum[...])
        for b in range(SPAN):
            there = slice(b * BLOCK, (b + 1) * BLOCK)
            cosine, sine, low = turn_parts(meta, base, jump, b)
            made[p, there, 128:256] = turn(grad_keys[there], cosine, -sine, low).astype(LOW)
        made[p, :, 256:384] = grad_values.astype(LOW)
        for h in range(2):
            found = contract(rows[h], made[p], 0, 0).astype(LOW)
            for k in range(part // r):
                w = h * (part // r) + k
                q_part[p, w // 4, (w // 2) % 2, w % 2] = found[k * r : (k + 1) * r]

    for k in range(3):

        @pl.when(step == k * SPAN + SPAN - 1)
        def _():
            every[2 + k].begin()

    @pl.when(step == 3 * SPAN - 1)
    def _():
        for own in (False, True):
            there = pl.ds((n.c if own else 1 - n.c) * half, half)
            gained = kept[...] if own else jnp.zeros(kept.shape, WIDE)
            for k in range(3):
                gained = gained + contract(
                    made[k, there], weight[:, k * 384 : k * 384 + 384], 1, 1
                )
            target = dx_own if own else dx_give
            for h in range(2):
                target[h] = gained[:, h * part : (h + 1) * part].astype(LOW)
            if own:
                pair2.second()
            else:
                dx_swap().start()
                pair2.first()
        dx_swap().wait_recv()
        for h in range(2):
            dx_own[h] = plus(dx_own[h], dx_other[h])
        dx_over.begin()
        pair2.third()
        pair0.fourth()
        pair1.fourth()
        pair2.fourth()
        for item in every:
            item.close()
        dx_swap().wait_send()
        dx_over.finish()


def backward_call(depth, cuts, meta, base, jump, soft, grads, context, inverse, q, k, v, rows, kept,
                  q_full, o_held, m_held, t_part):
    length = q.shape[1]
    half, width = kept.shape
    part = width // 2
    r = o_held.shape[-2]
    trio = once((3, length, 128))
    low = lambda *shape: jax.ShapeDtypeStruct(shape, LOW)
    widths = (o_held.shape[-1], m_held.shape[-1])
    shape = lambda *item: jax.ShapeDtypeStruct(item, WIDE)
    outs = [shape(r, widths[0]), shape(r, part), shape(r, widths[1] - part)]
    outs += [shape(r, part)] * 3 + [shape(*t_part.shape[-2:])]
    scratch = [
        pltpu.VMEM((length, 128), LOW),
        pltpu.VMEM((128, length), WIDE),
        pltpu.VMEM((128, length), WIDE),
        pltpu.VMEM((3, length, 384), LOW),
        pltpu.VMEM((width, 3 * 384), LOW),
        pltpu.VMEM((3, depth, 2, 2, r, 384), LOW),
        pltpu.VMEM((2, half, part), LOW),
        pltpu.VMEM((2, half, part), LOW),
        pltpu.VMEM((2, half, part), LOW),
    ]
    for at, columns in enumerate(widths + (384,) * 3):
        scratch += scatter_scratch(depth, r, columns, cuts[at], "later" if at < 2 else "swap")
    scratch += scatter_scratch(depth, t_part.shape[-2], t_part.shape[-1], cuts[5], "join", WIDE)
    marks = pltpu.SemaphoreType.DMA((6, scatter_marks(depth)))
    return pl.pallas_call(
        functools.partial(backward_kernel, depth, cuts),
        grid=(3 * SPAN,),
        out_shape=[low(2 * half, part)] + outs,
        in_specs=[
            pl.BlockSpec(memory_space=pltpu.SMEM),
            once(base.shape),
            once(jump.shape),
            pl.BlockSpec((1, 2, BLOCK, length), lambda s: (s, 0, 0, 0)),
            trio,
            trio,
            trio,
            trio,
            trio,
            trio,
            once(rows.shape),
            once(kept.shape),
        ]
        + [ANY] * 4,
        out_specs=[ANY] + [once(item.shape) for item in outs],
        scratch_shapes=scratch
        + [
            pltpu.SemaphoreType.DMA((4 * depth,)),
            marks,
            marks,
            pltpu.SemaphoreType.DMA((8,)),
            pltpu.SemaphoreType.DMA((7,)),
            pltpu.SemaphoreType.DMA((7,)),
        ],
        compiler_params=pltpu.CompilerParams(
            collective_id=2, has_side_effects=True, vmem_limit_bytes=63 * MEGA
        ),
        name="attend_back",
    )(meta, base, jump, soft, grads, context, inverse, q, k, v, rows, kept, q_full, o_held, m_held, t_part)


def owned(
    inputs,
    block_segment,
    query_weight,
    key_weight,
    value_weight,
    output_weight,
    inner_weight,
    outer_weight,
    first_gain,
    first_bias,
    second_gain,
    second_bias,
    output_cotangent,
):
    wide = lax.axis_size("wide")
    depth = wide // 4
    r = query_weight.shape[0]
    part = query_weight.shape[1]
    length = inputs.shape[0]
    half = length // 2
    x, w, c, _, _ = place()
    pairs = part // 128
    meta = jnp.pad(block_segment[None], ((0, 0), (0, 128 - SPAN)))
    hidden = inner_weight.shape[1]
    widths = [3 * part, part + hidden, hidden]
    cuts = [(item // 256) * 128 for item in widths]
    cuts[0] = 128
    gains = [first_gain, first_bias, second_gain, second_bias]
    weights = [query_weight, key_weight, value_weight, output_weight.T, inner_weight, outer_weight.T]
    base, jump = angle_tables()
    meta, gains, rows, q_full, m_full, o_full, pairs_context, q, k, v, soft, inverse, context = (
        forward_call(depth, cuts, meta, gains, inputs, weights, base, jump)
    )
    layer_output, kept, sums, grads, o_held, m_held = middle_call(
        depth,
        [cuts[2], cuts[1]],
        pairs_context,
        rows,
        output_cotangent,
        m_full.reshape(2, 2 * part, widths[1]),
        o_full,
        gains,
    )
    few = 2 * part // (2 * wide)
    spots = jnp.moveaxis(sums.reshape(2, 2, 2, wide, few), (2, 3), (0, 1))
    spots = jnp.pad(jnp.moveaxis(spots, 2, 3), ((0, 0), (0, 0), (0, 6), (0, 0), (0, 128 - few)))
    spots = spots.reshape(2, depth, 2, 2, 8, 256)
    input_gradient, o_sum, m_sum, i_sum, q_sum, k_sum, v_sum, found = backward_call(
        depth,
        [(item // 256) * 128 for item in (widths[2], widths[1])] + [128] * 4,
        meta,
        base,
        jump,
        soft,
        grads,
        context,
        inverse,
        q,
        k,
        v,
        rows,
        kept,
        q_full,
        o_held,
        m_held,
        spots,
    )
    return (
        layer_output,
        input_gradient,
        q_sum,
        k_sum,
        v_sum,
        m_sum.T,
        i_sum,
        o_sum.T,
        found[0, 0:few],
        found[1, 0:few],
        found[0, 128 : 128 + few],
        found[1, 128 : 128 + few],
    )


def program(*arrays):
    rows = arrays[2].shape[0]
    whole = rows % 16 == 0 and lax.axis_size("narrow") == 2 and lax.axis_size("wide") % 4 == 0
    return owned(*arrays) if whole else shards(*arrays)


def solution(mesh):
    placed = (
        P("wide", "narrow"),
        P("wide"),
        P("wide", "narrow"),
        P("wide", "narrow"),
        P("wide", "narrow"),
        P("narrow", "wide"),
        P("wide", "narrow"),
        P("narrow", "wide"),
        P("narrow"),
        P("narrow"),
        P("narrow"),
        P("narrow"),
        P("wide", "narrow"),
    )
    return jax.shard_map(
        program,
        mesh=mesh,
        in_specs=placed,
        out_specs=(
            P("wide", "narrow"),
            P("wide", "narrow"),
            P("wide", "narrow"),
            P("wide", "narrow"),
            P("wide", "narrow"),
            P("narrow", "wide"),
            P("wide", "narrow"),
            P("narrow", "wide"),
            P(("narrow", "wide")),
            P(("narrow", "wide")),
            P(("narrow", "wide")),
            P(("narrow", "wide")),
        ),
        check_vma=False,
    )
```

```python
import functools

import jax
import jax.numpy as jnp
import numpy as np
from jax import lax
from jax.experimental import pallas as pl
from jax.experimental.pallas import tpu as pltpu
from jax.sharding import PartitionSpec as P

HEAD_DIM = 64
BLOCK = 512
SPAN = 3


EPSILON = 1e-06
NEGATIVE = -1e30
THETA = 10000.0
ROOT_HALF = 0.7071067811865476
INVERSE_ROOT = 0.3989422804014327


def product(left, right):
    return jnp.dot(left, right, preferred_element_type=jnp.float32)


def left_transposed(left, right):
    return lax.dot_general(
        left, right, (((0,), (0,)), ((), ())), preferred_element_type=jnp.float32
    )


def right_transposed(left, right):
    return lax.dot_general(
        left, right, (((1,), (1,)), ((), ())), preferred_element_type=jnp.float32
    )


def whole_features(values):
    return lax.all_gather(values, "narrow", axis=1, tiled=True)


def feature_sums(values):
    return lax.psum_scatter(
        values.astype(jnp.bfloat16), "narrow", scatter_dimension=1, tiled=True
    ).astype(jnp.float32)


def moments(first_sum, second_sum):
    return lax.psum((first_sum, second_sum), "narrow")


def gelu_value(values):
    return 0.5 * values * (1.0 + lax.erf(values * ROOT_HALF))


def gelu_slope(values):
    return (
        0.5 * (1.0 + lax.erf(values * ROOT_HALF))
        + values * jnp.exp(-0.5 * values * values) * INVERSE_ROOT
    )


def rotate(values, cosine, sine):
    half = values.shape[-1] // 2
    first = values[..., :half]
    second = values[..., half:]
    return jnp.concatenate(
        [first * cosine - second * sine, second * cosine + first * sine], axis=-1
    )


def rotate_back(values, cosine, sine):
    half = values.shape[-1] // 2
    first = values[..., :half]
    second = values[..., half:]
    return jnp.concatenate(
        [first * cosine + second * sine, second * cosine - first * sine], axis=-1
    )


def tables(block_segment):
    segment = block_segment.reshape(-1, SPAN)
    earlier = jnp.sum((segment[:, None, :] < segment[:, :, None]).astype(jnp.int32), axis=2)
    offsets = (jnp.arange(SPAN, dtype=jnp.int32)[None, :] - earlier) * BLOCK
    positions = (
        (offsets[:, :, None] + jnp.arange(BLOCK, dtype=jnp.int32)[None, None, :])
        .reshape(-1)
        .astype(jnp.float32)
    )
    half = HEAD_DIM // 2
    rates = THETA ** (-jnp.arange(half, dtype=jnp.float32) / half)
    angle = positions[:, None] * rates[None, :]
    labels = jnp.repeat(segment, BLOCK, axis=1)
    return (jnp.cos(angle)[:, None, :], jnp.sin(angle)[:, None, :], labels)


def normalize(summed, gain, bias, width):
    total, squares = moments(jnp.sum(summed, axis=1), jnp.sum(summed * summed, axis=1))
    mean = total / width
    reciprocal = lax.rsqrt(squares / width - mean * mean + EPSILON)
    normed = (summed - mean[:, None]) * reciprocal[:, None]
    return (normed * gain + bias, normed, reciprocal)


def normalize_back(grad, normed, reciprocal, gain, width):
    scaled = grad * gain
    total, cross = moments(jnp.sum(scaled, axis=1), jnp.sum(scaled * normed, axis=1))
    return reciprocal[:, None] * (scaled - total[:, None] / width - normed * cross[:, None] / width)


def block_scores(block_queries, group_keys, block_labels, group_labels, factor):
    scores = (
        jnp.einsum("qhd,khd->hqk", block_queries, group_keys, preferred_element_type=jnp.float32)
        * factor
    )
    same = block_labels[:, None] == group_labels[None, :]
    return jnp.where(same[None], scores, NEGATIVE)


def attention_forward(queries, keys, values, labels, factor):
    groups, length = labels.shape
    shape = (groups, length) + queries.shape[1:]

    def one_group(items):
        group_queries, group_keys, group_values, group_labels = items
        contexts = []
        totals = []
        for index in range(length // BLOCK):
            low_end = index * BLOCK
            high_end = low_end + BLOCK
            scores = block_scores(
                group_queries[low_end:high_end],
                group_keys,
                group_labels[low_end:high_end],
                group_labels,
                factor,
            )
            top = jnp.max(scores, axis=2, keepdims=True)
            raised = jnp.exp(scores - top)
            summed = jnp.sum(raised, axis=2, keepdims=True)
            soft = (raised / summed).astype(jnp.bfloat16)
            contexts.append(
                jnp.einsum("hqk,khd->qhd", soft, group_values, preferred_element_type=jnp.float32)
            )
            totals.append((top + jnp.log(summed))[..., 0])
        return (jnp.concatenate(contexts, axis=0), jnp.concatenate(totals, axis=1))

    contexts, totals = lax.map(
        one_group, (queries.reshape(shape), keys.reshape(shape), values.reshape(shape), labels)
    )
    return (contexts.reshape(queries.shape), totals)


def attention_backward(queries, keys, values, totals, grad_context, labels, factor):
    groups, length = labels.shape
    shape = (groups, length) + queries.shape[1:]

    def one_group(items):
        group_queries, group_keys, group_values, group_totals, group_grads, group_labels = items
        keys_grad = jnp.zeros(group_keys.shape, jnp.float32)
        values_grad = jnp.zeros(group_values.shape, jnp.float32)
        pieces = []
        for index in range(length // BLOCK):
            low_end = index * BLOCK
            high_end = low_end + BLOCK
            block_queries = group_queries[low_end:high_end]
            block_grads = group_grads[low_end:high_end]
            scores = block_scores(
                block_queries, group_keys, group_labels[low_end:high_end], group_labels, factor
            )
            soft = jnp.exp(scores - group_totals[:, low_end:high_end, None])
            inner = jnp.einsum(
                "qhd,khd->hqk", block_grads, group_values, preferred_element_type=jnp.float32
            )
            centre = jnp.sum(soft * inner, axis=2, keepdims=True)
            scores_grad = (soft * (inner - centre)).astype(jnp.bfloat16)
            pieces.append(
                jnp.einsum(
                    "hqk,khd->qhd", scores_grad, group_keys, preferred_element_type=jnp.float32
                )
                * factor
            )
            keys_grad = (
                keys_grad
                + jnp.einsum(
                    "hqk,qhd->khd", scores_grad, block_queries, preferred_element_type=jnp.float32
                )
                * factor
            )
            values_grad = values_grad + jnp.einsum(
                "hqk,qhd->khd",
                soft.astype(jnp.bfloat16),
                block_grads,
                preferred_element_type=jnp.float32,
            )
        return (jnp.concatenate(pieces, axis=0), keys_grad, values_grad)

    queries_grad, keys_grad, values_grad = lax.map(
        one_group,
        (
            queries.reshape(shape),
            keys.reshape(shape),
            values.reshape(shape),
            totals,
            grad_context.reshape(shape),
            labels,
        ),
    )
    return (
        queries_grad.reshape(queries.shape),
        keys_grad.reshape(queries.shape),
        values_grad.reshape(queries.shape),
    )


def shards(
    inputs,
    block_segment,
    query_weight,
    key_weight,
    value_weight,
    output_weight,
    inner_weight,
    outer_weight,
    first_gain,
    first_bias,
    second_gain,
    second_bias,
    output_cotangent,
):
    width = first_gain.shape[0] * lax.axis_size("narrow")
    tokens = inputs.shape[0]
    factor = HEAD_DIM ** (-0.5)
    cosine, sine, labels = tables(block_segment)
    full_inputs = whole_features(inputs)
    query_full, key_full, value_full, inner_full = (
        lax.all_gather(query_weight, "wide", axis=0, tiled=True),
        lax.all_gather(key_weight, "wide", axis=0, tiled=True),
        lax.all_gather(value_weight, "wide", axis=0, tiled=True),
        lax.all_gather(inner_weight, "wide", axis=0, tiled=True),
    )
    output_full, outer_full = (
        lax.all_gather(output_weight, "wide", axis=1, tiled=True),
        lax.all_gather(outer_weight, "wide", axis=1, tiled=True),
    )
    head_shape = (tokens, query_weight.shape[1] // HEAD_DIM, HEAD_DIM)
    queries = rotate(product(full_inputs, query_full).reshape(head_shape), cosine, sine).astype(
        jnp.bfloat16
    )
    keys = rotate(product(full_inputs, key_full).reshape(head_shape), cosine, sine).astype(
        jnp.bfloat16
    )
    values = product(full_inputs, value_full).astype(jnp.bfloat16).reshape(head_shape)
    context, totals = attention_forward(queries, keys, values, labels, factor)
    context_low = context.reshape(tokens, -1).astype(jnp.bfloat16)
    attended = feature_sums(product(context_low, output_full))
    first, first_normed, first_scale = normalize(
        inputs.astype(jnp.float32) + attended, first_gain, first_bias, width
    )
    first_low = first.astype(jnp.bfloat16)
    feed_rows = whole_features(first_low)
    inner = product(feed_rows, inner_full)
    activated = gelu_value(inner).astype(jnp.bfloat16)
    mixed = feature_sums(product(activated, outer_full))
    second, second_normed, second_scale = normalize(first + mixed, second_gain, second_bias, width)
    layer_output = second.astype(jnp.bfloat16)
    cotangent = output_cotangent.astype(jnp.float32)
    second_gain_grad = jnp.sum(cotangent * second_normed, axis=0)
    second_bias_grad = jnp.sum(cotangent, axis=0)
    grad_second = normalize_back(cotangent, second_normed, second_scale, second_gain, width)
    grad_mixed = grad_second.astype(jnp.bfloat16)
    grad_rows = whole_features(grad_mixed)
    grad_activated = right_transposed(grad_rows, outer_full)
    outer_grad = left_transposed(activated, grad_rows)
    grad_inner = (grad_activated * gelu_slope(inner)).astype(jnp.bfloat16)
    inner_grad = left_transposed(feed_rows, grad_inner)
    grad_first = grad_second + feature_sums(right_transposed(grad_inner, inner_full))
    first_gain_grad = jnp.sum(grad_first * first_normed, axis=0)
    first_bias_grad = jnp.sum(grad_first, axis=0)
    grad_first_sum = normalize_back(grad_first, first_normed, first_scale, first_gain, width)
    attended_rows = whole_features(grad_first_sum.astype(jnp.bfloat16))
    output_grad = left_transposed(context_low, attended_rows)
    grad_context = right_transposed(attended_rows, output_full).astype(jnp.bfloat16)
    queries_grad, keys_grad, values_grad = attention_backward(
        queries, keys, values, totals, grad_context.reshape(head_shape), labels, factor
    )
    queries_grad = rotate_back(queries_grad, cosine, sine).reshape(tokens, -1).astype(jnp.bfloat16)
    keys_grad = rotate_back(keys_grad, cosine, sine).reshape(tokens, -1).astype(jnp.bfloat16)
    values_grad = values_grad.reshape(tokens, -1).astype(jnp.bfloat16)
    query_grad = left_transposed(full_inputs, queries_grad)
    key_grad = left_transposed(full_inputs, keys_grad)
    value_grad = left_transposed(full_inputs, values_grad)
    spread = (
        right_transposed(queries_grad, query_full)
        + right_transposed(keys_grad, key_full)
        + right_transposed(values_grad, value_full)
    )
    input_gradient = (grad_first_sum + feature_sums(spread)).astype(jnp.bfloat16)
    (
        query_total,
        key_total,
        value_total,
        inner_total,
        first_gain_total,
        first_bias_total,
        second_gain_total,
        second_bias_total,
    ) = (
        lax.psum_scatter(query_grad, "wide", scatter_dimension=0, tiled=True),
        lax.psum_scatter(key_grad, "wide", scatter_dimension=0, tiled=True),
        lax.psum_scatter(value_grad, "wide", scatter_dimension=0, tiled=True),
        lax.psum_scatter(inner_grad, "wide", scatter_dimension=0, tiled=True),
        lax.psum_scatter(first_gain_grad, "wide", scatter_dimension=0, tiled=True),
        lax.psum_scatter(first_bias_grad, "wide", scatter_dimension=0, tiled=True),
        lax.psum_scatter(second_gain_grad, "wide", scatter_dimension=0, tiled=True),
        lax.psum_scatter(second_bias_grad, "wide", scatter_dimension=0, tiled=True),
    )
    output_total, outer_total = (
        lax.psum_scatter(output_grad, "wide", scatter_dimension=1, tiled=True),
        lax.psum_scatter(outer_grad, "wide", scatter_dimension=1, tiled=True),
    )
    return (
        layer_output,
        input_gradient,
        query_total,
        key_total,
        value_total,
        output_total,
        inner_total,
        outer_total,
        first_gain_total,
        first_bias_total,
        second_gain_total,
        second_bias_total,
    )


LOW = jnp.bfloat16
WIDE = jnp.float32
MESH = pl.DeviceIdType.MESH
MEGA = 1 << 20
ANY = pl.BlockSpec(memory_space=pl.ANY)


def contract(left, right, left_dim, right_dim):
    return lax.dot_general(
        left, right, (((left_dim,), (right_dim,)), ((), ())), preferred_element_type=WIDE
    )


def place():
    x = lax.axis_index("narrow")
    w = lax.axis_index("wide")
    c = lax.rem(w, 2)
    y = lax.rem(lax.div(w, 2), 2)
    q = lax.div(w, 4)
    return x, w, c, y, q


class Links:
    def __init__(self, depth):
        self.depth = depth
        self.x, self.w, self.c, self.y, self.q = place()
        self.across = (1 - self.x, self.w)
        self.beside = (self.x, self.w + 2 - 4 * self.y)
        self.sibling = (self.x, self.w + 1 - 2 * self.c)
        self.corner = (1 - self.x, self.w + 1 - 2 * self.c)

    def far(self, step):
        return (self.x, lax.rem(self.w + 4 * step, 4 * self.depth))

    def row(self, step):
        return lax.rem(self.q + self.depth - step, self.depth)

    def meet(self, pair_only=False):
        barrier = pltpu.get_barrier_semaphore()
        others = [self.sibling, self.across, self.corner]
        if not pair_only:
            others += [self.beside]
            others += [self.far(step) for step in range(1, self.depth)]
        for other in others:
            pl.semaphore_signal(barrier, 1, device_id=other, device_id_type=MESH)
        pl.semaphore_wait(barrier, len(others))


def remote(source, target, send, recv, device):
    return pltpu.make_async_remote_copy(
        src_ref=source,
        dst_ref=target,
        send_sem=send,
        recv_sem=recv,
        device_id=device,
        device_id_type=MESH,
    )


def gather_marks(depth):
    return 5 * depth + 2


class Gather:
    def __init__(self, links, own, full, cut, whole, send, recv, index, local):
        self.links, self.own, self.full, self.cut = links, own, full, cut
        self.whole, self.local = whole, local
        self.send = lambda k: send.at[index, k]
        self.recv = lambda k: recv.at[index, k]
        self.width = own.shape[-1]

    def slot(self, h, q, y):
        return self.full.at[h, q, y, self.links.c]

    def low(self, ref):
        return ref.at[:, pl.ds(0, self.cut)]

    def high(self, ref):
        return ref.at[:, pl.ds(self.cut, self.width - self.cut)]

    def copy(self, kind, step=0):
        n, d = self.links, self.links.depth
        mine = self.slot(n.x, n.q, n.y)
        column = self.slot(n.x, n.row(step), n.y)
        first = self.own if step == 0 else column
        if kind == "far":
            return self.move(self.own, mine, step - 1, n.far(step))
        if kind == "across":
            return self.move(first, column, d + step, n.across)
        if kind == "beside":
            return self.move(first, column, 2 * d + step, n.beside)
        if kind == "high":
            part = self.high(self.slot(1 - n.x, n.row(step), n.y))
            return self.move(part, part, 3 * d + step, n.beside)
        if kind == "low":
            part = self.low(self.slot(n.x, n.row(step), 1 - n.y))
            return self.move(part, part, 4 * d + step, n.across)
        part = self.full.at[step if self.whole else 1 - n.c, :, :, n.c]
        return self.move(part, part, 5 * d + step, n.sibling)

    def move(self, source, target, mark, device):
        return remote(source, target, self.send(mark), self.recv(mark), device)

    def arrived(self, target, mark):
        self.move(target, target, mark, self.links.sibling).wait_recv()

    def keep(self):
        n = self.links
        return pltpu.make_async_copy(self.own, self.slot(n.x, n.q, n.y), self.local)

    def begin(self):
        self.begin_far()
        self.begin_near()

    def begin_far(self):
        for step in range(1, self.links.depth):
            self.copy("far", step).start()

    def begin_near(self):
        self.keep().start()
        self.copy("across").start()
        self.copy("beside").start()

    def second(self, step):
        n = self.links
        self.arrived(self.slot(n.x, n.row(step), n.y), step - 1)
        self.copy("across", step).start()
        self.copy("beside", step).start()

    def third(self, step):
        n, d = self.links, self.links.depth
        self.arrived(self.slot(1 - n.x, n.row(step), n.y), d + step)
        self.copy("high", step).start()
        self.arrived(self.slot(n.x, n.row(step), 1 - n.y), 2 * d + step)
        self.copy("low", step).start()

    def fourth(self):
        n, d = self.links, self.links.depth
        for step in range(d):
            got = self.slot(1 - n.x, n.row(step), 1 - n.y)
            self.arrived(self.high(got), 3 * d + step)
            self.arrived(self.low(got), 4 * d + step)
        self.keep().wait()
        for h in range(2 if self.whole else 1):
            self.copy("sibling", h).start()

    def finish(self):
        n, d = self.links, self.links.depth
        for h in range(2 if self.whole else 1):
            self.arrived(self.full.at[h if self.whole else n.c, :, :, 1 - n.c], 5 * d + h)

    def halfway(self):
        n, d = self.links, self.links.depth
        self.keep().wait()
        for step in range(d):
            self.arrived(self.slot(1 - n.x, n.row(step), n.y), d + step)
            self.arrived(self.slot(n.x, n.row(step), 1 - n.y), 2 * d + step)
            if step:
                self.copy("far", step).wait_send()
            for kind in ("across", "beside"):
                self.copy(kind, step).wait_send()

    def close(self):
        d = self.links.depth
        for step in range(d):
            if step:
                self.copy("far", step).wait_send()
            for kind in ("across", "beside", "high", "low"):
                self.copy(kind, step).wait_send()
        for h in range(2 if self.whole else 1):
            self.copy("sibling", h).wait_send()


class Finish:
    def __init__(self, links, full, flat, cut, send, recv, base, local):
        self.links, self.full, self.flat, self.cut, self.local = links, full, flat, cut, local
        self.send = lambda k: send.at[base + k]
        self.recv = lambda k: recv.at[base + k]
        self.r, self.width = full.shape[-2:]

    def slot(self, h, q, y, c):
        w = (q * 2 + y) * 2 + c
        return self.flat.at[h, pl.ds(pl.multiple_of(w * self.r, self.r), self.r)]

    def low(self, ref):
        return ref.at[:, pl.ds(0, self.cut)]

    def high(self, ref):
        return ref.at[:, pl.ds(self.cut, self.width - self.cut)]

    def hop(self, kind, step):
        n, d = self.links, self.links.depth
        q = n.row(step)
        h, y, part, mark, device = {
            "high": (1 - n.x, n.y, self.high, step, n.beside),
            "low": (n.x, 1 - n.y, self.low, d + step, n.across),
        }[kind]
        source, target = part(self.full.at[h, q, y, n.c]), part(self.slot(h, q, y, n.c))
        return remote(source, target, self.send(mark), self.recv(mark), device)

    def spread(self, h, q, y):
        n, d = self.links, self.links.depth
        mark = 2 * d + (h * d + q) * 2 + y
        part = self.slot(h, q, y, n.c)
        return remote(part, part, self.send(mark), self.recv(mark), n.sibling)

    def loads(self):
        n, d = self.links, self.links.depth
        return [
            pltpu.make_async_copy(
                self.full.at[h, q, y, n.c], self.slot(h, q, y, n.c), self.local.at[k * d + q]
            )
            for k, (h, y) in enumerate(((n.x, n.y), (1 - n.x, n.y), (n.x, 1 - n.y)))
            for q in range(d)
        ]

    def everywhere(self, act):
        for h in range(2):
            for q in range(self.links.depth):
                for y in range(2):
                    act(self.spread(h, q, y))

    def begin(self):
        for step in range(self.links.depth):
            self.hop("high", step).start()
            self.hop("low", step).start()
        for item in self.loads():
            item.start()

    def fourth(self):
        n, d = self.links, self.links.depth
        for item in self.loads():
            item.wait()
        for step in range(d):
            got = self.slot(1 - n.x, n.row(step), 1 - n.y, n.c)
            for part, mark in ((self.high(got), step), (self.low(got), d + step)):
                remote(part, part, self.send(mark), self.recv(mark), n.sibling).wait_recv()
        self.everywhere(lambda item: item.start())

    def finish(self):
        n = self.links
        for h in range(2):
            for q in range(n.depth):
                for y in range(2):
                    mark = 2 * n.depth + (h * n.depth + q) * 2 + y
                    got = self.slot(h, q, y, 1 - n.c)
                    remote(got, got, self.send(mark), self.recv(mark), n.sibling).wait_recv()

    def close(self):
        for step in range(self.links.depth):
            self.hop("high", step).wait_send()
            self.hop("low", step).wait_send()
        self.everywhere(lambda item: item.wait_send())


class Share:
    def __init__(self, links, in_ref, rows, note_in, note, gain_in, gain, send, recv, local):
        n = self.links = links
        self.home = n.x == n.c
        s, r = (lambda k: send.at[k]), (lambda k: recv.at[k])
        near, far = rows.at[n.x], rows.at[1 - n.x]
        self.rows_across = lambda: remote(in_ref, near, s(0), r(0), n.across)
        self.rows_beside = lambda: remote(in_ref, near, s(1), r(1), n.sibling)
        self.rows_further = lambda: remote(far, far, s(2), r(2), n.sibling)
        self.note = lambda: remote(note_in, note, s(3), r(3), n.sibling)
        self.gain = lambda: remote(gain_in, gain.at[n.x], s(4), r(4), n.across)
        self.gain_keep = lambda: pltpu.make_async_copy(gain_in, gain.at[n.x], local.at[0])
        self.rows_keep = lambda: pltpu.make_async_copy(in_ref, near, local.at[1])
        self.note_keep = lambda: pltpu.make_async_copy(note_in, note, local.at[2])

    def begin(self):
        @pl.when(self.home)
        def _():
            self.note().start()
            self.rows_beside().start()
            self.rows_keep().start()
            self.note_keep().start()

        @pl.when(jnp.logical_not(self.home))
        def _():
            self.rows_across().start()

    def further(self):
        self.gain().start()
        self.gain_keep().start()

        @pl.when(self.home)
        def _():
            self.rows_across().wait_recv()
            self.rows_further().start()
            self.rows_keep().wait()
            self.note_keep().wait()

        @pl.when(jnp.logical_not(self.home))
        def _():
            self.note().wait_recv()
            self.rows_beside().wait_recv()
            self.rows_further().wait_recv()

        self.gain_keep().wait()

    def finish(self):
        self.gain().wait()

        @pl.when(self.home)
        def _():
            self.note().wait_send()
            self.rows_beside().wait_send()
            self.rows_further().wait_send()

        @pl.when(jnp.logical_not(self.home))
        def _():
            self.rows_across().wait_send()


class Pull:
    def __init__(self, links, source, target, send, recv, base):
        n = self.links = links
        half = source.shape[0] // 2
        self.home = n.x == n.c
        s, r = (lambda k: send.at[base + k]), (lambda k: recv.at[base + k])
        mine, theirs = source.at[pl.ds(n.c * half, half)], source.at[pl.ds((1 - n.c) * half, half)]
        near = target.at[n.x]
        self.beside = lambda: remote(theirs, near, s(0), r(0), n.sibling)
        self.across = lambda: remote(mine, near, s(1), r(1), n.across)
        self.corner = lambda: remote(theirs, near, s(2), r(2), n.corner)

    def begin(self):
        @pl.when(self.home)
        def _():
            self.beside().start()

        @pl.when(jnp.logical_not(self.home))
        def _():
            self.across().start()
            self.corner().start()

    def finish(self):
        @pl.when(self.home)
        def _():
            self.beside().wait_send()
            self.across().wait_recv()

        @pl.when(jnp.logical_not(self.home))
        def _():
            self.across().wait_send()
            self.corner().wait_send()
            self.beside().wait_recv()
            self.corner().wait_recv()


def plus(left, right):
    return (left.astype(WIDE) + right.astype(WIDE)).astype(left.dtype)


def scatter_marks(depth):
    return depth + 5


class Scatter:
    def __init__(self, links, kind, part, cut, bufs, out, send, recv, index, local):
        self.links, self.kind, self.part, self.cut, self.out = links, kind, part, cut, out
        self.held, self.other, self.x1, self.y1, self.x2, self.y2, self.z = bufs
        self.send = lambda k: send.at[index, k]
        self.recv = lambda k: recv.at[index, k]
        self.local = local
        self.rest = self.held.shape[-1] - cut

    def low(self, ref):
        return ref.at[:, :, pl.ds(0, self.cut)]

    def high(self, ref):
        return ref.at[:, :, pl.ds(self.cut, self.rest)]

    def move(self, source, target, mark, device):
        return remote(source, target, self.send(mark), self.recv(mark), device)

    def copy(self, kind, step=0):
        n = self.links
        if kind == "sibling" and self.kind == "join":
            return self.move(self.part.at[:, :, :, 1 - n.c], self.other, 0, n.sibling)
        if kind == "sibling":
            return self.move(self.part.at[:, :, 1 - n.c], self.held.at[n.c], 0, n.sibling)
        if kind == "x1":
            return self.move(self.low(self.held.at[1 - n.x, :, 1 - n.y]), self.x1, 1, n.across)
        if kind == "y1":
            return self.move(self.high(self.held.at[1 - n.x, :, 1 - n.y]), self.y1, 2, n.beside)
        if kind == "y2":
            return self.move(self.held.at[n.x, :, 1 - n.y], self.y2, 3, n.beside)
        if kind == "x2":
            return self.move(self.held.at[1 - n.x, :, n.y], self.x2, 4, n.across)
        q = lax.rem(n.q + step, n.depth)
        return self.move(self.mine(q), self.z.at[step - 1], 4 + step, n.far(step))

    def mine(self, q):
        n = self.links
        return self.held.at[q] if self.kind == "last" else self.held.at[n.x, q, n.y]

    def keep(self):
        n = self.links
        if self.kind in ("held", "last"):
            return pltpu.make_async_copy(self.part, self.held, self.local)
        if self.kind == "join":
            return pltpu.make_async_copy(self.part.at[:, :, :, n.c], self.held, self.local)
        return pltpu.make_async_copy(self.part.at[:, :, n.c], self.held.at[n.c], self.local)

    def arrived(self, target, mark):
        self.move(target, target, mark, self.links.sibling).wait_recv()

    def begin(self):
        self.keep().start()
        if self.kind in ("join", "swap"):
            self.copy("sibling").start()

    def first(self):
        n = self.links
        self.keep().wait()
        if self.kind == "join":
            self.arrived(self.other, 0)
            self.held[...] = plus(self.held[...], self.other[...])
        if self.kind == "swap":
            self.arrived(self.held.at[1 - n.c], 0)
        self.copy("x1").start()
        self.copy("y1").start()

    def second(self):
        n = self.links
        low, high = pl.ds(0, self.cut), pl.ds(self.cut, self.rest)
        self.arrived(self.x1, 1)
        for q in range(n.depth):
            self.held[n.x, q, 1 - n.y, :, low] = plus(
                self.held[n.x, q, 1 - n.y, :, low], self.x1[q]
            )
        self.copy("y2").start()
        self.arrived(self.y1, 2)
        for q in range(n.depth):
            self.held[1 - n.x, q, n.y, :, high] = plus(
                self.held[1 - n.x, q, n.y, :, high], self.y1[q]
            )
        self.copy("x2").start()

    def third(self):
        n = self.links
        if self.kind == "last":
            self.keep().wait()
        else:
            self.arrived(self.y2, 3)
            self.arrived(self.x2, 4)
        for step in range(1, n.depth):
            q = lax.rem(n.q + step, n.depth)
            if self.kind != "last":
                mine = self.mine(q)
                mine[...] = plus(plus(mine[...], self.x2[q]), self.y2[q])
            self.copy("z", step).start()

    def fourth(self):
        n = self.links
        total = self.mine(n.q)[...].astype(WIDE)
        if self.kind != "last":
            total = total + self.x2[n.q].astype(WIDE) + self.y2[n.q].astype(WIDE)
        for step in range(1, n.depth):
            self.arrived(self.z.at[step - 1], 4 + step)
            total = total + self.z[step - 1].astype(WIDE)
        self.out(total)

    def close(self):
        hops = ("x1", "y1", "x2", "y2")
        hops = {"last": (), "held": hops}.get(self.kind, ("sibling",) + hops)
        for kind in hops:
            self.copy(kind).wait_send()
        for step in range(1, self.links.depth):
            self.copy("z", step).wait_send()


def scatter_scratch(depth, r, columns, cut, kind="swap", of=LOW):
    small = (8, 128)
    later = kind == "last"
    return [
        pltpu.VMEM((depth, r, columns) if later else (2, depth, 2, r, columns), of),
        pltpu.VMEM((2, depth, 2, r, columns) if kind == "join" else small, of),
        pltpu.VMEM(small if later else (depth, r, cut), of),
        pltpu.VMEM(small if later else (depth, r, columns - cut), of),
        pltpu.VMEM(small if later else (depth, r, columns), of),
        pltpu.VMEM(small if later else (depth, r, columns), of),
        pltpu.VMEM((depth - 1, r, columns), of),
    ]


class HandOver:
    def __init__(self, links, source, target, send, recv, base, local, bounce=None):
        self.links, self.source, self.target, self.local = links, source, target, local
        self.bounce = bounce
        self.send = lambda k: send.at[base + k]
        self.recv = lambda k: recv.at[base + k]
        self.half = source.shape[1]

    def rows(self, c):
        return self.target.at[pl.ds(c * self.half, self.half)]

    def copies(self):
        n = self.links
        near, far = self.source.at[n.x], self.source.at[1 - n.x]
        mine = self.rows(n.c)
        return (
            pltpu.make_async_copy(near if self.bounce is None else self.bounce, mine, self.local),
            remote(far, mine, self.send(0), self.recv(0), n.across),
            remote(near, mine, self.send(1), self.recv(1), n.sibling),
            remote(far, mine, self.send(2), self.recv(2), n.corner),
        )

    def begin(self):
        n = self.links
        keep, across, sibling, corner = self.copies()

        @pl.when(n.x == n.c)
        def _():
            keep.start()
            across.start()

        @pl.when(n.x != n.c)
        def _():
            sibling.start()
            corner.start()

    def finish(self):
        n = self.links
        keep, across, sibling, corner = self.copies()
        mine, theirs = self.rows(n.c), self.rows(1 - n.c)

        @pl.when(n.x == n.c)
        def _():
            keep.wait()
            across.wait_send()
            remote(theirs, theirs, self.send(1), self.recv(1), n.sibling).wait_recv()

        @pl.when(n.x != n.c)
        def _():
            sibling.wait_send()
            corner.wait_send()
            remote(mine, mine, self.send(0), self.recv(0), n.across).wait_recv()
            remote(theirs, theirs, self.send(2), self.recv(2), n.corner).wait_recv()


def angle_tables():
    rates = THETA ** (-np.arange(HEAD_DIM // 2) / (HEAD_DIM // 2))
    rates = np.tile(rates, 4)[None]
    base = np.arange(BLOCK)[:, None] * rates
    jump = np.arange(SPAN)[:, None] * BLOCK * rates
    base = np.concatenate([np.cos(base), np.sin(base)], axis=0)
    jump = np.concatenate([np.cos(jump), np.sin(jump), np.zeros((2, 128))], axis=0)
    return jnp.asarray(base, WIDE), jnp.asarray(jump, WIDE)


def lanes(rows):
    return lax.broadcasted_iota(jnp.int32, (rows, 128), 1)


def turn_parts(meta, base, jump, block):
    segment = meta[0, block]
    earlier = [(meta[0, other] < segment).astype(jnp.int32) for other in range(SPAN)]
    offset = block - sum(earlier)
    far_cos = jump[pl.ds(offset, 1), :]
    far_sin = jump[pl.ds(SPAN + offset, 1), :]
    near_cos, near_sin = base[0:BLOCK], base[BLOCK : 2 * BLOCK]
    cosine = near_cos * far_cos - near_sin * far_sin
    sine = near_sin * far_cos + near_cos * far_sin
    low = (lanes(BLOCK) % HEAD_DIM) < HEAD_DIM // 2
    return cosine, jnp.where(low, -sine, sine), low


def turn(values, cosine, sine, low):
    swapped = jnp.where(low, pltpu.roll(values, 96, 1), pltpu.roll(values, 32, 1))
    return values * cosine + swapped * sine


def weight_loads(full, h, flat, marks):
    depth, r = full.shape[1], full.shape[4]
    return [
        pltpu.make_async_copy(
            full.at[h, q, y, c], flat.at[pl.ds(k * r, r)], marks.at[k]
        )
        for k, (q, y, c) in enumerate(
            (q, y, c) for q in range(depth) for y in range(2) for c in range(2)
        )
    ]


def forward_kernel(depth, cuts, note_in, in_ref, cot_in, gain1, gain2, gain3, gain4, query, key, value, output,
                   inner, o_own, base, jump,
                   note, gain, cot, rows, q_full, m_full, o_full, all_context, q_out, k_out, v_out,
                   p_ref, r_ref, c_out, q_ref, k_ref, v_ref, c_ref, marks, meta, held, weight, gain_in, q_own, m_own, piece, send, recv, local, extra_send,
                   extra_recv, context_send, context_recv):
    step = pl.program_id(0)
    scale = HEAD_DIM ** (-0.5)
    n = Links(depth)
    half = in_ref.shape[0] // 2
    gathers = [
        Gather(n, own, full, cut, whole, send, recv, k, local.at[k])
        for k, (own, full, cut, whole) in enumerate(
            zip((q_own, m_own, o_own), (q_full, m_full, o_full), cuts, (False, True, True))
        )
    ]
    share = Share(
        n, in_ref, held, note_in, note, gain_in, gain, extra_send, extra_recv, local.at[pl.ds(3, 3)]
    )
    rows_keep = lambda: pltpu.make_async_copy(held, rows, local.at[7])
    pull = Pull(n, cot_in, cot, extra_send, extra_recv, 5)

    def context_copy(p):
        there = c_ref.at[p, pl.ds((1 - n.c) * half, half)]
        return remote(there, all_context.at[n.c, p], context_send.at[p], context_recv.at[p], n.sibling)

    def context_keep(p):
        here = c_ref.at[p, pl.ds(n.c * half, half)]
        return pltpu.make_async_copy(here, all_context.at[n.c, p], local.at[10 + p])

    @pl.when(step == 0)
    def _():
        for k, item in enumerate((gain1, gain2, gain3, gain4)):
            gain_in[k : k + 1] = item[...].reshape(1, -1)
            gain_in[4 + k : 5 + k] = item[...].reshape(1, -1)
        for p in range(3):
            for k, item in enumerate((query, key, value)):
                column = p * 384 + k * 128
                q_own[:, column : column + 128] = item[:, p * 128 : (p + 1) * 128]
        m_own[:, 0 : output.shape[1]] = output[...]
        m_own[:, output.shape[1] :] = inner[...]
        n.meet()
        gathers[0].begin()
        share.begin()
        gathers[1].begin_far()
        gathers[2].begin_far()
        for k in range(1, depth):
            gathers[0].second(k)
        for k in range(depth):
            gathers[0].third(k)
        gathers[1].begin_near()
        gathers[2].begin_near()
        share.further()
        rows_keep().start()
        loads = [pltpu.make_async_copy(note, meta, local.at[8])]
        loads[0].start()
        gathers[0].fourth()
        gathers[0].finish()
        loads += weight_loads(q_full, n.c, weight, piece)
        for item in loads[1:]:
            item.start()
        for item in loads:
            item.wait()

    flush = lambda: [
        pltpu.make_async_copy(source, target, local.at[13 + at])
        for at, (source, target) in enumerate(
            ((q_ref, q_out), (k_ref, k_out), (v_ref, v_out), (c_ref, c_out))
        )
    ]

    def flush_early():
        for item in flush()[:3]:
            item.start()

    hooks = {
        4: [flush_early],
        1: [functools.partial(gathers[1].second, k) for k in range(1, depth)],
        3: [functools.partial(gathers[2].second, k) for k in range(1, depth)],
        7: [functools.partial(gathers[1].third, k) for k in range(depth)] + [pull.begin],
        11: [gathers[1].fourth],
    }
    for at, actions in hooks.items():

        @pl.when(step == at)
        def _():
            for action in actions:
                action()

    @pl.when(step < SPAN)
    def _():
        here = pl.ds(step * BLOCK, BLOCK)
        cosine, sine, low = turn_parts(meta, base, jump, step)
        values = jnp.concatenate([held[0, here], held[1, here]], axis=1)

        for p in range(3):
            made = contract(values, weight[:, p * 384 : p * 384 + 384], 1, 0)
            q_ref[p, here] = (turn(made[:, 0:128], cosine, sine, low) * scale).astype(LOW)
            k_ref[p, here] = turn(made[:, 128:256], cosine, sine, low).astype(LOW)
            v_ref[p, here] = made[:, 256:384].astype(LOW)
        marks[here] = (lanes(BLOCK) == meta[0, step]).astype(WIDE).astype(LOW)

    @pl.when(step >= SPAN)
    def _():
        turn_number = step - SPAN
        p = turn_number // SPAN
        i = turn_number % SPAN
        here = pl.ds(i * BLOCK, BLOCK)
        lane = lanes(BLOCK)
        queries = q_ref[p, here]
        values = v_ref[p]
        keys = jnp.concatenate([k_ref[p], marks[...]], axis=1)
        barred = jnp.where((lane < SPAN) & (lane != meta[0, i]), NEGATIVE, 0.0).astype(LOW)
        outs = []
        scales = []
        for head in range(2):
            chosen = (lane // HEAD_DIM) == head
            ours = jnp.concatenate([jnp.where(chosen, queries, 0).astype(LOW), barred], axis=1)
            scores = contract(ours, keys, 1, 1)
            top = jnp.max(scores, axis=1, keepdims=True)
            raised = jnp.exp(scores - top)
            inverse = 1.0 / jnp.sum(raised, axis=1, keepdims=True)
            soft = raised.astype(LOW)
            p_ref[0, head] = soft
            outs.append(contract(soft, values, 1, 0))
            scales.append(inverse)
        inverse = jnp.where(lane < HEAD_DIM, scales[0], scales[1])
        r_ref[0, here] = inverse
        c_ref[p, here] = (jnp.where(lane < HEAD_DIM, outs[0], outs[1]) * inverse).astype(LOW)

    for p in range(3):

        @pl.when(step == 2 * SPAN - 1 + p * SPAN)
        def _():
            context_copy(p).start()
            context_keep(p).start()

    @pl.when(step == 4 * SPAN - 1)
    def _():
        flush()[3].start()
        gathers[1].finish()
        gathers[2].halfway()
        gathers[0].close()
        gathers[1].close()
        share.finish()
        pull.finish()
        rows_keep().wait()
        for p in range(3):
            context_copy(p).wait()
            context_keep(p).wait()
        for item in flush():
            item.wait()


def forward_call(depth, cuts, note, gains, rows, cot, weights, base, jump):
    length, part = rows.shape
    half = length // 2
    r, hidden = weights[-1].shape
    columns = (3 * part, part + hidden, hidden)
    low = lambda *shape: jax.ShapeDtypeStruct(shape, LOW)
    full = [low(2, depth, 2, 2, r, item) for item in columns]
    trio = low(3, length, 128)
    vmem = pl.BlockSpec(memory_space=pltpu.VMEM)
    marks = pltpu.SemaphoreType.DMA((3, gather_marks(depth)))
    return pl.pallas_call(
        functools.partial(forward_kernel, depth, cuts),
        grid=(SPAN + 3 * SPAN,),
        out_shape=[
            jax.ShapeDtypeStruct(note.shape, note.dtype),
            jax.ShapeDtypeStruct((2, 8, part), WIDE),
            low(2, half, part),
            low(2, length, part),
        ]
        + full
        + [
            low(2, 3, half, 128),
            trio,
            trio,
            trio,
            low(SPAN * 3, 2, BLOCK, length),
            jax.ShapeDtypeStruct((3, length, 128), WIDE),
            trio,
        ],
        in_specs=[ANY] * 3 + [once(item.shape) for item in (*gains, *weights, base, jump)],
        out_specs=[ANY] * 8
        + [ANY] * 3
        + [
            pl.BlockSpec((1, 2, BLOCK, length), lambda s: (jnp.maximum(s - SPAN, 0), 0, 0, 0)),
            pl.BlockSpec((1, length, 128), lambda s: (jnp.maximum(s - SPAN, 0) // SPAN, 0, 0)),
            ANY,
        ],
        scratch_shapes=[pltpu.VMEM((3, length, 128), LOW)] * 4
        + [
            pltpu.VMEM((length, 128), LOW),
            pltpu.SMEM(note.shape, note.dtype),
            pltpu.VMEM((2, length, part), LOW),
            pltpu.VMEM((4 * depth * r, columns[0]), LOW),
            pltpu.VMEM((8, part), WIDE),
            pltpu.VMEM((r, columns[0]), LOW),
            pltpu.VMEM((r, columns[1]), LOW),
            pltpu.SemaphoreType.DMA((4 * depth,)),
            marks,
            marks,
            pltpu.SemaphoreType.DMA((17,)),
            pltpu.SemaphoreType.DMA((8,)),
            pltpu.SemaphoreType.DMA((8,)),
            pltpu.SemaphoreType.DMA((3,)),
            pltpu.SemaphoreType.DMA((3,)),
        ],
        compiler_params=pltpu.CompilerParams(
            collective_id=0, has_side_effects=True, vmem_limit_bytes=60 * MEGA
        ),
        name="attend",
    )(note, rows, cot, *gains, *weights, base, jump)


def norm_of(summed):
    mean = jnp.mean(summed, axis=1, keepdims=True)
    centred = summed - mean
    variance = jnp.mean(centred * centred, axis=1, keepdims=True)
    scale = lax.rsqrt(variance + EPSILON)
    return centred * scale, scale


def norm_back(scaled, normed, scale):
    total = jnp.mean(scaled, axis=1, keepdims=True)
    cross = jnp.mean(scaled * normed, axis=1, keepdims=True)
    return scale * (scaled - total - normed * cross)


HIDDEN = 512


def middle_kernel(depth, cuts, context, rows, gains, cot_in, cot_got, m_full, o_full, lo_out, gfs_ref, sums, grads,
                  o_held, m_held, m_mat, o_mat, act, gi, fl, gm, ga, gc, n1, n2, scales, cot, lo,
                  o_part, m_part, o_other, m_other, ox, oy, ox2, oy2, local, send, recv, load):
    step = pl.program_id(0)
    tile, part = rows.shape[1:]
    half = fl.shape[0]
    tiles = half // tile
    r = o_part.shape[-2]
    pieces = o_mat.shape[2] // HIDDEN
    width = pieces * HIDDEN
    n = Links(depth)
    early = step < 2 * tiles
    turn_of = jnp.where(early, lax.rem(step, tiles), jnp.clip(step - 2 * tiles - 2, 0, tiles - 1))
    here = pl.ds(pl.multiple_of(turn_of * tile, tile), tile)
    cot_raw = lambda: pltpu.make_async_copy(
        cot_in.at[pl.ds(n.c * half, half)], cot.at[n.x], local.at[7]
    )
    cot_near = lambda: pltpu.make_async_copy(cot_got.at[n.x], cot.at[n.x], local.at[7])
    cot_far = lambda: pltpu.make_async_copy(cot_got.at[1 - n.x], cot.at[1 - n.x], local.at[5])
    lo_copy = lambda: pltpu.make_async_copy(lo, lo_out, local.at[8])
    finish = Finish(n, o_full, o_mat, cuts[0], send, recv, 15, load)
    m_load = lambda: pltpu.make_async_copy(m_full, m_mat, local.at[0])

    def grads_keep():
        own = grads.at[:, pl.ds(n.c * half, half)]
        return pltpu.make_async_copy(gc.at[n.c], own, local.at[2])

    def grads_copy():
        own = grads.at[:, pl.ds(n.c * half, half)]
        return remote(gc.at[1 - n.c], own, send.at[4], recv.at[4], n.sibling)

    order = ((0, 1 - n.x), (0, n.x), (1, 1 - n.x), (1, n.x))
    chunks = ((o_part, o_other, ox, oy, o_held), (m_part, m_other, None, None, m_held))

    def part_copy(k):
        chunk, h = order[k]
        source, target = chunks[chunk][:2]
        return remote(
            source.at[h, :, :, 1 - n.c], target.at[h], send.at[k], recv.at[k], n.sibling
        )

    def join(k):
        chunk, h = order[k]
        source, target = chunks[chunk][:2]
        part_copy(k).wait_recv()
        for q in range(depth):
            for y in range(2):
                target[h, q, y] = plus(source[h, q, y, n.c], target[h, q, y])

    def hop(chunk, across):
        target, x1, y1 = chunks[chunk][1:4]
        corner = target.at[1 - n.x, :, 1 - n.y]
        mark = 11 + 2 * chunk + across
        if across:
            part = corner.at[:, :, pl.ds(0, x1.shape[-1])]
            return remote(part, x1, send.at[mark], recv.at[mark], n.across)
        part = corner.at[:, :, pl.ds(x1.shape[-1], y1.shape[-1])]
        return remote(part, y1, send.at[mark], recv.at[mark], n.beside)

    def land(chunk):
        target, x1, y1, held = chunks[chunk][1:5]
        low, high = pl.ds(0, x1.shape[-1]), pl.ds(x1.shape[-1], y1.shape[-1])
        hop(chunk, True).wait_recv()
        hop(chunk, False).wait_recv()
        for q in range(depth):
            target[n.x, q, 1 - n.y, :, low] = plus(target[n.x, q, 1 - n.y, :, low], x1[q])
            target[1 - n.x, q, n.y, :, high] = plus(target[1 - n.x, q, n.y, :, high], y1[q])

    def hop2(across):
        mark = 13 + across
        if across:
            part = o_other.at[1 - n.x, :, n.y]
            return remote(part, ox2, send.at[mark], recv.at[mark], n.across)
        part = o_other.at[n.x, :, 1 - n.y]
        return remote(part, oy2, send.at[mark], recv.at[mark], n.beside)

    def land2():
        hop2(True).wait_recv()
        hop2(False).wait_recv()
        for q in range(depth):
            ox2[q] = plus(plus(o_other[n.x, q, n.y], ox2[q]), oy2[q])

    def held_copy(chunk):
        source, target = ((ox2, o_held), (m_other, m_held))[chunk]
        return pltpu.make_async_copy(source, target, local.at[3 + chunk])

    @pl.when(step == 0)
    def _():
        m_load().start()
        n.meet()
        finish.begin()
        cot_far().start()

        @pl.when(n.x == n.c)
        def _():
            cot_raw().start()

        @pl.when(n.x != n.c)
        def _():
            cot_near().start()

        m_load().wait()

    @pl.when(step < tiles)
    def _():
        whole = jnp.concatenate([gains[0], gains[1]], axis=1)
        gain1, bias1, gain2, bias2 = (whole[k : k + 1, :] for k in range(4))
        summed = jnp.concatenate([rows[0], rows[1]], axis=1).astype(WIDE)
        for h in range(2):
            seen = jnp.concatenate([context[h, p, here] for p in range(3)], axis=1)
            summed = summed + contract(seen, m_mat[h, :, 0:part], 1, 1)
        normed1, scale1 = norm_of(summed)
        n1[here] = normed1
        scales[here, 0:1] = scale1
        first = normed1 * gain1 + bias1
        first_low = first.astype(LOW)
        fl[here] = first_low
        for h in range(2):
            for j in range(pieces):
                lo_end = part + j * HIDDEN
                there = slice(h * width + j * HIDDEN, h * width + (j + 1) * HIDDEN)
                inner = contract(first_low, m_mat[h, :, lo_end : lo_end + HIDDEN], 1, 0)
                share = 0.5 * (1.0 + lax.erf(inner * ROOT_HALF))
                slope = share + inner * jnp.exp(-0.5 * inner * inner) * INVERSE_ROOT
                gi[here, there] = slope.astype(LOW)
                act[here, there] = (inner * share).astype(LOW)

    @pl.when(step == tiles)
    def _():
        finish.fourth()
        cot_far().wait()
        cot_near().wait()
        finish.finish()

    @pl.when((step >= tiles) & (step < 2 * tiles))
    def _():
        whole = jnp.concatenate([gains[0], gains[1]], axis=1)
        gain1, bias1, gain2, bias2 = (whole[k : k + 1, :] for k in range(4))
        mixed = n1[here] * gain1 + bias1
        for h in range(2):
            mixed = mixed + contract(act[here, h * width : (h + 1) * width], o_mat[h], 1, 1)
        normed2, scale2 = norm_of(mixed)
        result = (normed2 * gain2 + bias2).astype(LOW)
        for h in range(2):
            lo[h, here] = result[:, h * part : (h + 1) * part]
        cotangent = jnp.concatenate([cot[0, here], cot[1, here]], axis=1).astype(WIDE)
        second_gain = jnp.sum(cotangent * normed2, axis=0, keepdims=True)
        second_bias = jnp.sum(cotangent, axis=0, keepdims=True)
        grad_second = norm_back(cotangent * gain2, normed2, scale2)
        grad_mixed = grad_second.astype(LOW)
        gm[here] = grad_mixed
        n2[here] = grad_second
        found = jnp.concatenate([second_gain, second_bias], axis=0)

        @pl.when(step == tiles)
        def _():
            sums[2:4] = found

        @pl.when(step > tiles)
        def _():
            sums[2:4] += found

    @pl.when((step >= 2 * tiles + 2) & (step < 3 * tiles + 2))
    def _():
        whole = jnp.concatenate([gains[0], gains[1]], axis=1)
        gain1 = whole[0:1, :]
        normed1, scale1 = n1[here], scales[here, 0:1]
        grad_mixed = gm[here]
        for h in range(2):
            for j in range(pieces):
                there = slice(h * width + j * HIDDEN, h * width + (j + 1) * HIDDEN)
                raised = contract(grad_mixed, o_mat[h, :, j * HIDDEN : (j + 1) * HIDDEN], 1, 0)
                gi[here, there] = (raised * gi[here, there].astype(WIDE)).astype(LOW)
        grad_first = n2[here]
        for h in range(2):
            grad_first = grad_first + contract(
                gi[here, h * width : (h + 1) * width], m_mat[h, :, part : part + width], 1, 1
            )
        first_gain = jnp.sum(grad_first * normed1, axis=0, keepdims=True)
        first_bias = jnp.sum(grad_first, axis=0, keepdims=True)
        grad_sum = norm_back(grad_first * gain1, normed1, scale1)
        gfs_ref[...] = grad_sum
        grad_attended = grad_sum.astype(LOW)
        ga[here] = grad_attended
        for h in range(2):
            made = contract(grad_attended, m_mat[h, :, 0:part], 1, 0).astype(LOW)
            for p in range(3):
                gc[h, p, here] = made[:, p * 128 : (p + 1) * 128]
        found = jnp.concatenate([first_gain, first_bias], axis=0)

        @pl.when(step == 2 * tiles + 2)
        def _():
            sums[0:2] = found

        @pl.when(step > 2 * tiles + 2)
        def _():
            sums[0:2] += found

    @pl.when(step == 2 * tiles + 3)
    def _():
        join(1)
        land(0)
        hop2(True).start()
        hop2(False).start()
        lo_copy().start()

    @pl.when(step == 3 * tiles + 1)
    def _():
        grads_keep().start()
        grads_copy().start()

    def put(target, h, row, column, values):
        shards = values.shape[0] // r
        for k in range(shards):
            w = row // r + k
            target[h, w // 4, (w // 2) % 2, w % 2, :, column : column + values.shape[1]] = values[
                k * r : (k + 1) * r
            ]

    for k in range(4):

        @pl.when(step == (2 * tiles + k if k < 2 else 3 * tiles + k))
        def _():
            chunk, h = order[k]
            target = chunks[chunk][0]
            for row in range(0, 2 * part, part):
                for j in range(pieces):
                    start = pl.multiple_of(h * width + j * HIDDEN, HIDDEN)
                    there = pl.ds(start, HIDDEN)
                    if chunk == 0:
                        made = contract(gm[:, row : row + part], act[:, there], 0, 0)
                        put(target, h, row, j * HIDDEN, made.astype(LOW))
                    else:
                        made = contract(fl[:, row : row + part], gi[:, there], 0, 0)
                        put(target, h, row, part + j * HIDDEN, made.astype(LOW))
                if chunk == 1:
                    seen = jnp.concatenate([context[h, p] for p in range(3)], axis=1)
                    made = contract(ga[:, row : row + part], seen, 0, 0)
                    put(target, h, row, 0, made.astype(LOW))
            part_copy(k).start()
            if k == 1:
                join(0)
                hop(0, True).start()
                hop(0, False).start()
            if k == 3:
                join(2)
                join(3)
                held_copy(1).start()
                land2()
                held_copy(0).start()
                grads_keep().wait()
                grads_copy().wait()
                for item in range(4):
                    part_copy(item).wait_send()
                hop(0, True).wait_send()
                hop(0, False).wait_send()
                hop2(True).wait_send()
                hop2(False).wait_send()
                held_copy(0).wait()
                held_copy(1).wait()
                lo_copy().wait()
                finish.close()


def once(shape):
    zeros = (0,) * len(shape)
    return pl.BlockSpec(shape, lambda *_: zeros, pipeline_mode=pl.Buffered(1))


def middle_call(depth, cuts, context, rows, cot_in, cot, m_full, o_full, gains):
    tile = 256
    half, part = cot.shape[1:]
    tiles = half // tile
    width = 2 * part
    hidden = 2 * o_full.shape[-1]
    r = width // (4 * depth)
    columns = (o_full.shape[-1], m_full.shape[2])
    low = lambda *shape: jax.ShapeDtypeStruct(shape, LOW)
    held = [(2, depth, 2, r, item) for item in columns]
    last = lambda i: jnp.minimum(i, tiles - 1)
    later = lambda i: jnp.clip(i - 2 * tiles - 2, 0, tiles - 1)
    c = lambda: lax.rem(lax.axis_index("wide"), 2)
    return pl.pallas_call(
        functools.partial(middle_kernel, depth, cuts),
        grid=(3 * tiles + 4,),
        out_shape=[
            low(2, half, part),
            jax.ShapeDtypeStruct((half, width), WIDE),
            jax.ShapeDtypeStruct((4, width), WIDE),
            low(3, 2 * half, 128),
        ]
        + [low(depth, r, columns[0]), low(*held[1])],
        in_specs=[
            once((2, 3, half, 128)),
            pl.BlockSpec((2, tile, part), lambda i: (0, c() * tiles + last(i), 0)),
            once(gains.shape),
            ANY,
            ANY,
            ANY,
            ANY,
        ],
        out_specs=[
            ANY,
            pl.BlockSpec((tile, width), lambda i: (later(i), 0)),
            pl.BlockSpec((4, width), lambda i: (0, 0)),
            ANY,
            ANY,
            ANY,
        ],
        scratch_shapes=[
            pltpu.VMEM(m_full.shape, LOW),
            pltpu.VMEM((2, width, columns[0]), LOW),
            pltpu.VMEM((half, hidden), LOW),
            pltpu.VMEM((half, hidden), LOW),
            pltpu.VMEM((half, width), LOW),
            pltpu.VMEM((half, width), LOW),
            pltpu.VMEM((half, width), LOW),
            pltpu.VMEM((2, 3, half, 128), LOW),
            pltpu.VMEM((half, width), WIDE),
            pltpu.VMEM((half, width), WIDE),
            pltpu.VMEM((half, 2), WIDE),
            pltpu.VMEM((2, half, part), LOW),
            pltpu.VMEM((2, half, part), LOW),
        ]
        + [pltpu.VMEM((2, depth, 2, 2, r, item), LOW) for item in columns]
        + [pltpu.VMEM(item, LOW) for item in held]
        + [
            pltpu.VMEM((depth, r, item), LOW)
            for item in (cuts[0], columns[0] - cuts[0], columns[0], columns[0])
        ]
        + [
            pltpu.SemaphoreType.DMA((9,)),
            pltpu.SemaphoreType.DMA((15 + 6 * depth,)),
            pltpu.SemaphoreType.DMA((15 + 6 * depth,)),
            pltpu.SemaphoreType.DMA((3 * depth,)),
        ],
        compiler_params=pltpu.CompilerParams(
            collective_id=1, has_side_effects=True, vmem_limit_bytes=62 * MEGA
        ),
        name="middle",
    )(context, rows, gains, cot_in, cot, m_full, o_full)


def backward_kernel(depth, cuts, meta, base, jump, soft, grads, context, inverse, q_ref, k_ref, v_ref,
                    rows_in, kept_in, q_full, lo_in, o_in, m_in, t_in, lo_out, dx_out, o_out, m_out,
                    i_out, q_out, k_out, v_out, t_out, *scratch):
    ones, keys_sum, values_sum, made, weight, q_part, dx_own, dx_give, dx_other = scratch[:9]
    rows, kept, bounce = scratch[-3:]
    bufs = [scratch[9 + 7 * k : 16 + 7 * k] for k in range(6)]
    piece, send, recv, local, extra_send, extra_recv = scratch[51:-3]
    step = pl.program_id(0)
    p = step // SPAN
    i = step % SPAN
    length = q_ref.shape[1]
    scale = HEAD_DIM ** (-0.5)
    lane = lanes(BLOCK)
    here = pl.ds(i * BLOCK, BLOCK)
    n = Links(depth)
    r = o_in.shape[-2]
    half, width = kept.shape
    part = width // 2
    kinds = ("last", "held", "swap", "swap", "swap", "join")
    parts = (o_in, m_in) + tuple(q_part.at[k] for k in range(3)) + (t_in,)

    def put_pair(p, total):
        for k, item in enumerate((q_out, k_out, v_out)):
            item[:, p * 128 : (p + 1) * 128] = total[:, k * 128 : (k + 1) * 128]

    def put_whole(target, total):
        target[...] = total

    def put_inner(total):
        m_out[...] = total[:, 0:part]
        i_out[...] = total[:, part:]

    outs = [functools.partial(put_whole, o_out), put_inner]
    outs += [functools.partial(put_pair, k) for k in range(3)]
    outs += [functools.partial(put_whole, t_out)]
    every = [
        Scatter(n, kind, item, cut, buf, out, send, recv, k, local.at[k])
        for k, (kind, item, cut, buf, out) in enumerate(zip(kinds, parts, cuts, bufs, outs))
    ]
    outer, inner, pair0, pair1, pair2, small = every
    dx_over = HandOver(n, dx_own, dx_out, extra_send, extra_recv, 0, local.at[6])
    rows_load = lambda: pltpu.make_async_copy(rows_in, rows, local.at[7])
    kept_load = lambda: pltpu.make_async_copy(kept_in, kept, local.at[8])
    lo_load = lambda: pltpu.make_async_copy(lo_in.at[n.x], bounce, local.at[9])
    lo_over = HandOver(n, lo_in, lo_out, extra_send, extra_recv, 4, local.at[10], bounce)
    dx_swap = lambda: remote(dx_give, dx_other, extra_send.at[3], extra_recv.at[3], n.sibling)

    @pl.when(step == 0)
    def _():
        ones[...] = (lanes(length) < 2).astype(WIDE).astype(LOW)
        for item in weight_loads(q_full, n.c, weight, piece):
            item.start()
        inner.begin()
        outer.begin()
        rows_load().start()
        kept_load().start()
        lo_load().start()
        n.meet()
        small.begin()
        small.first()
        inner.first()
        outer.third()
        for item in weight_loads(q_full, n.c, weight, piece):
            item.wait()


    def lo_begin():
        lo_load().wait()
        lo_over.begin()

    hooks = {1: [small.second], 2: [lambda: rows_load().wait(), lo_begin], 3: [inner.second], 4: [outer.fourth, pair0.first], 6: [small.third, pair1.first], 8: [inner.third, pair0.second, pair0.third, pair1.second]}
    for at, actions in hooks.items():

        @pl.when(step == at)
        def _():
            for action in actions:
                action()

    grad = grads[0, here].astype(WIDE)
    turned = grad * inverse[0, here]
    both = turned * context[0, here].astype(WIDE)
    turned_low = turned.astype(LOW)
    queries = q_ref[0, here]
    keys = k_ref[0]
    values = jnp.concatenate([v_ref[0], ones[...]], axis=1)
    turned_flip = jnp.transpose(turned).astype(LOW)
    queries_flip = jnp.transpose(queries.astype(WIDE)).astype(LOW)
    found = []
    for head in range(2):
        chosen = (lane // HEAD_DIM) == head
        centre = -jnp.sum(jnp.where(chosen, both, 0.0), axis=1, keepdims=True)
        coarse = centre.astype(LOW).astype(WIDE)
        fine = jnp.where(lane == 0, coarse, jnp.where(lane == 1, centre - coarse, 0.0))
        ours = jnp.concatenate(
            [jnp.where(chosen, turned_low, 0).astype(LOW), fine.astype(LOW)], axis=1
        )
        raised = soft[0, head]
        scores = (contract(ours, values, 1, 1) * raised.astype(WIDE)).astype(LOW)
        found.append(contract(scores, keys, 1, 0))
        mine = slice(head * HEAD_DIM, (head + 1) * HEAD_DIM)
        values_add = contract(turned_flip[mine], raised, 1, 0)
        keys_add = contract(queries_flip[mine], scores, 1, 0)

        @pl.when(i == 0)
        def _():
            values_sum[mine] = values_add
            keys_sum[mine] = keys_add

        @pl.when(i > 0)
        def _():
            values_sum[mine] += values_add
            keys_sum[mine] += keys_add

    cosine, sine, low = turn_parts(meta, base, jump, i)
    grad_queries = jnp.where(lane < HEAD_DIM, found[0], found[1]) * scale
    made[p, here, 0:128] = turn(grad_queries, cosine, -sine, low).astype(LOW)

    @pl.when(i == SPAN - 1)
    def _():
        grad_keys = jnp.transpose(keys_sum[...])
        grad_values = jnp.transpose(values_sum[...])
        for b in range(SPAN):
            there = slice(b * BLOCK, (b + 1) * BLOCK)
            cosine, sine, low = turn_parts(meta, base, jump, b)
            made[p, there, 128:256] = turn(grad_keys[there], cosine, -sine, low).astype(LOW)
        made[p, :, 256:384] = grad_values.astype(LOW)
        for h in range(2):
            found = contract(rows[h], made[p], 0, 0).astype(LOW)
            for k in range(part // r):
                w = h * (part // r) + k
                q_part[p, w // 4, (w // 2) % 2, w % 2] = found[k * r : (k + 1) * r]

    for k in range(3):

        @pl.when(step == k * SPAN + SPAN - 1)
        def _():
            every[2 + k].begin()

    @pl.when(step == 3 * SPAN - 1)
    def _():
        kept_load().wait()
        for own in (False, True):
            there = pl.ds((n.c if own else 1 - n.c) * half, half)
            gained = kept[...] if own else jnp.zeros(kept.shape, WIDE)
            for k in range(3):
                gained = gained + contract(
                    made[k, there], weight[:, k * 384 : k * 384 + 384], 1, 1
                )
            target = dx_own if own else dx_give
            for h in range(2):
                target[h] = gained[:, h * part : (h + 1) * part].astype(LOW)
            if own:
                pair2.second()
            else:
                dx_swap().start()
                pair2.first()
        dx_swap().wait_recv()
        for h in range(2):
            dx_own[h] = plus(dx_own[h], dx_other[h])
        dx_over.begin()
        pair1.third()
        pair2.third()
        small.fourth()
        inner.fourth()
        pair0.fourth()
        pair1.fourth()
        pair2.fourth()
        for item in every:
            item.close()
        dx_swap().wait_send()
        lo_over.finish()
        dx_over.finish()


def backward_call(depth, cuts, meta, base, jump, soft, grads, context, inverse, q, k, v, rows, kept,
                  q_full, lo, o_held, m_held, t_part):
    length = q.shape[1]
    half, width = kept.shape
    part = width // 2
    r = o_held.shape[-2]
    trio = pl.BlockSpec((1, length, 128), lambda s: (s // SPAN, 0, 0))
    low = lambda *shape: jax.ShapeDtypeStruct(shape, LOW)
    widths = (o_held.shape[-1], m_held.shape[-1])
    shape = lambda *item: jax.ShapeDtypeStruct(item, WIDE)
    outs = [shape(r, widths[0]), shape(r, part), shape(r, widths[1] - part)]
    outs += [shape(r, part)] * 3 + [shape(*t_part.shape[-2:])]
    scratch = [
        pltpu.VMEM((length, 128), LOW),
        pltpu.VMEM((128, length), WIDE),
        pltpu.VMEM((128, length), WIDE),
        pltpu.VMEM((3, length, 384), LOW),
        pltpu.VMEM((width, 3 * 384), LOW),
        pltpu.VMEM((3, depth, 2, 2, r, 384), LOW),
        pltpu.VMEM((2, half, part), LOW),
        pltpu.VMEM((2, half, part), LOW),
        pltpu.VMEM((2, half, part), LOW),
    ]
    for at, columns in enumerate(widths + (384,) * 3):
        scratch += scatter_scratch(depth, r, columns, cuts[at], ("last", "held", "swap")[min(at, 2)])
    scratch += scatter_scratch(depth, t_part.shape[-2], t_part.shape[-1], cuts[5], "join", WIDE)
    marks = pltpu.SemaphoreType.DMA((6, scatter_marks(depth)))
    return pl.pallas_call(
        functools.partial(backward_kernel, depth, cuts),
        grid=(3 * SPAN,),
        out_shape=[low(2 * half, part)] * 2 + outs,
        in_specs=[
            pl.BlockSpec(memory_space=pltpu.SMEM),
            once(base.shape),
            once(jump.shape),
            pl.BlockSpec((1, 2, BLOCK, length), lambda s: (s, 0, 0, 0)),
            trio,
            trio,
            trio,
            trio,
            trio,
            trio,
        ]
        + [ANY] * 7,
        out_specs=[ANY] * 2 + [once(item.shape) for item in outs],
        scratch_shapes=scratch
        + [
            pltpu.SemaphoreType.DMA((4 * depth,)),
            marks,
            marks,
            pltpu.SemaphoreType.DMA((11,)),
            pltpu.SemaphoreType.DMA((7,)),
            pltpu.SemaphoreType.DMA((7,)),
            pltpu.VMEM(rows.shape, LOW),
            pltpu.VMEM(kept.shape, WIDE),
            pltpu.VMEM((half, part), LOW),
        ],
        compiler_params=pltpu.CompilerParams(
            collective_id=2, has_side_effects=True, vmem_limit_bytes=63 * MEGA
        ),
        name="attend_back",
    )(meta, base, jump, soft, grads, context, inverse, q, k, v, rows, kept, q_full, lo, o_held, m_held, t_part)


def owned(
    inputs,
    block_segment,
    query_weight,
    key_weight,
    value_weight,
    output_weight,
    inner_weight,
    outer_weight,
    first_gain,
    first_bias,
    second_gain,
    second_bias,
    output_cotangent,
):
    wide = lax.axis_size("wide")
    depth = wide // 4
    r = query_weight.shape[0]
    part = query_weight.shape[1]
    length = inputs.shape[0]
    half = length // 2
    x, w, c, _, _ = place()
    pairs = part // 128
    meta = jnp.pad(block_segment[None], ((0, 0), (0, 128 - SPAN)))
    hidden = inner_weight.shape[1]
    widths = [3 * part, part + hidden, hidden]
    cuts = [(item // 384) * 128 for item in widths]
    cuts[0] = 128
    gains = [first_gain, first_bias, second_gain, second_bias]
    weights = [query_weight, key_weight, value_weight, output_weight.T, inner_weight, outer_weight.T]
    base, jump = angle_tables()
    found = forward_call(
        depth, cuts, meta, gains, inputs, output_cotangent, weights, base, jump
    )
    meta, gains, cot, rows, q_full, m_full, o_full, pairs_context, q, k, v, soft, inverse, context = found
    lo, kept, sums, grads, o_held, m_held = middle_call(
        depth,
        [cuts[2], cuts[1]],
        pairs_context,
        rows,
        output_cotangent,
        cot,
        m_full.reshape(2, 2 * part, widths[1]),
        o_full,
        gains,
    )
    few = 2 * part // (2 * wide)
    spots = jnp.moveaxis(sums.reshape(2, 2, 2, wide, few), (2, 3), (0, 1))
    spots = jnp.pad(jnp.moveaxis(spots, 2, 3), ((0, 0), (0, 0), (0, 6), (0, 0), (0, 128 - few)))
    spots = spots.reshape(2, depth, 2, 2, 8, 256)
    layer_output, input_gradient, o_sum, m_sum, i_sum, q_sum, k_sum, v_sum, found = backward_call(
        depth,
        [(item // 512) * 128 for item in (widths[2], widths[1])] + [128] * 4,
        meta,
        base,
        jump,
        soft,
        grads,
        context,
        inverse,
        q,
        k,
        v,
        rows,
        kept,
        q_full,
        lo,
        o_held,
        m_held,
        spots,
    )
    return (
        layer_output,
        input_gradient,
        q_sum,
        k_sum,
        v_sum,
        m_sum.T,
        i_sum,
        o_sum.T,
        found[0, 0:few],
        found[1, 0:few],
        found[0, 128 : 128 + few],
        found[1, 128 : 128 + few],
    )


def program(*arrays):
    rows = arrays[2].shape[0]
    whole = rows % 16 == 0 and lax.axis_size("narrow") == 2 and lax.axis_size("wide") % 4 == 0
    return owned(*arrays) if whole else shards(*arrays)


def solution(mesh):
    placed = (
        P("wide", "narrow"),
        P("wide"),
        P("wide", "narrow"),
        P("wide", "narrow"),
        P("wide", "narrow"),
        P("narrow", "wide"),
        P("wide", "narrow"),
        P("narrow", "wide"),
        P("narrow"),
        P("narrow"),
        P("narrow"),
        P("narrow"),
        P("wide", "narrow"),
    )
    return jax.shard_map(
        program,
        mesh=mesh,
        in_specs=placed,
        out_specs=(
            P("wide", "narrow"),
            P("wide", "narrow"),
            P("wide", "narrow"),
            P("wide", "narrow"),
            P("wide", "narrow"),
            P("narrow", "wide"),
            P("wide", "narrow"),
            P("narrow", "wide"),
            P(("narrow", "wide")),
            P(("narrow", "wide")),
            P(("narrow", "wide")),
            P(("narrow", "wide")),
        ),
        check_vma=False,
    )
```

```python
import functools

import jax
import jax.numpy as jnp
import numpy as np
from jax import lax
from jax.experimental import pallas as pl
from jax.experimental.pallas import tpu as pltpu
from jax.sharding import PartitionSpec as P

HEAD_DIM = 64
BLOCK = 512
SPAN = 3


EPSILON = 1e-06
NEGATIVE = -1e30
THETA = 10000.0
ROOT_HALF = 0.7071067811865476
INVERSE_ROOT = 0.3989422804014327


def product(left, right):
    return jnp.dot(left, right, preferred_element_type=jnp.float32)


def left_transposed(left, right):
    return lax.dot_general(
        left, right, (((0,), (0,)), ((), ())), preferred_element_type=jnp.float32
    )


def right_transposed(left, right):
    return lax.dot_general(
        left, right, (((1,), (1,)), ((), ())), preferred_element_type=jnp.float32
    )


def whole_features(values):
    return lax.all_gather(values, "narrow", axis=1, tiled=True)


def feature_sums(values):
    return lax.psum_scatter(
        values.astype(jnp.bfloat16), "narrow", scatter_dimension=1, tiled=True
    ).astype(jnp.float32)


def moments(first_sum, second_sum):
    return lax.psum((first_sum, second_sum), "narrow")


def gelu_value(values):
    return 0.5 * values * (1.0 + lax.erf(values * ROOT_HALF))


def gelu_slope(values):
    return (
        0.5 * (1.0 + lax.erf(values * ROOT_HALF))
        + values * jnp.exp(-0.5 * values * values) * INVERSE_ROOT
    )


def rotate(values, cosine, sine):
    half = values.shape[-1] // 2
    first = values[..., :half]
    second = values[..., half:]
    return jnp.concatenate(
        [first * cosine - second * sine, second * cosine + first * sine], axis=-1
    )


def rotate_back(values, cosine, sine):
    half = values.shape[-1] // 2
    first = values[..., :half]
    second = values[..., half:]
    return jnp.concatenate(
        [first * cosine + second * sine, second * cosine - first * sine], axis=-1
    )


def tables(block_segment):
    segment = block_segment.reshape(-1, SPAN)
    earlier = jnp.sum((segment[:, None, :] < segment[:, :, None]).astype(jnp.int32), axis=2)
    offsets = (jnp.arange(SPAN, dtype=jnp.int32)[None, :] - earlier) * BLOCK
    positions = (
        (offsets[:, :, None] + jnp.arange(BLOCK, dtype=jnp.int32)[None, None, :])
        .reshape(-1)
        .astype(jnp.float32)
    )
    half = HEAD_DIM // 2
    rates = THETA ** (-jnp.arange(half, dtype=jnp.float32) / half)
    angle = positions[:, None] * rates[None, :]
    labels = jnp.repeat(segment, BLOCK, axis=1)
    return (jnp.cos(angle)[:, None, :], jnp.sin(angle)[:, None, :], labels)


def normalize(summed, gain, bias, width):
    total, squares = moments(jnp.sum(summed, axis=1), jnp.sum(summed * summed, axis=1))
    mean = total / width
    reciprocal = lax.rsqrt(squares / width - mean * mean + EPSILON)
    normed = (summed - mean[:, None]) * reciprocal[:, None]
    return (normed * gain + bias, normed, reciprocal)


def normalize_back(grad, normed, reciprocal, gain, width):
    scaled = grad * gain
    total, cross = moments(jnp.sum(scaled, axis=1), jnp.sum(scaled * normed, axis=1))
    return reciprocal[:, None] * (scaled - total[:, None] / width - normed * cross[:, None] / width)


def block_scores(block_queries, group_keys, block_labels, group_labels, factor):
    scores = (
        jnp.einsum("qhd,khd->hqk", block_queries, group_keys, preferred_element_type=jnp.float32)
        * factor
    )
    same = block_labels[:, None] == group_labels[None, :]
    return jnp.where(same[None], scores, NEGATIVE)


def attention_forward(queries, keys, values, labels, factor):
    groups, length = labels.shape
    shape = (groups, length) + queries.shape[1:]

    def one_group(items):
        group_queries, group_keys, group_values, group_labels = items
        contexts = []
        totals = []
        for index in range(length // BLOCK):
            low_end = index * BLOCK
            high_end = low_end + BLOCK
            scores = block_scores(
                group_queries[low_end:high_end],
                group_keys,
                group_labels[low_end:high_end],
                group_labels,
                factor,
            )
            top = jnp.max(scores, axis=2, keepdims=True)
            raised = jnp.exp(scores - top)
            summed = jnp.sum(raised, axis=2, keepdims=True)
            soft = (raised / summed).astype(jnp.bfloat16)
            contexts.append(
                jnp.einsum("hqk,khd->qhd", soft, group_values, preferred_element_type=jnp.float32)
            )
            totals.append((top + jnp.log(summed))[..., 0])
        return (jnp.concatenate(contexts, axis=0), jnp.concatenate(totals, axis=1))

    contexts, totals = lax.map(
        one_group, (queries.reshape(shape), keys.reshape(shape), values.reshape(shape), labels)
    )
    return (contexts.reshape(queries.shape), totals)


def attention_backward(queries, keys, values, totals, grad_context, labels, factor):
    groups, length = labels.shape
    shape = (groups, length) + queries.shape[1:]

    def one_group(items):
        group_queries, group_keys, group_values, group_totals, group_grads, group_labels = items
        keys_grad = jnp.zeros(group_keys.shape, jnp.float32)
        values_grad = jnp.zeros(group_values.shape, jnp.float32)
        pieces = []
        for index in range(length // BLOCK):
            low_end = index * BLOCK
            high_end = low_end + BLOCK
            block_queries = group_queries[low_end:high_end]
            block_grads = group_grads[low_end:high_end]
            scores = block_scores(
                block_queries, group_keys, group_labels[low_end:high_end], group_labels, factor
            )
            soft = jnp.exp(scores - group_totals[:, low_end:high_end, None])
            inner = jnp.einsum(
                "qhd,khd->hqk", block_grads, group_values, preferred_element_type=jnp.float32
            )
            centre = jnp.sum(soft * inner, axis=2, keepdims=True)
            scores_grad = (soft * (inner - centre)).astype(jnp.bfloat16)
            pieces.append(
                jnp.einsum(
                    "hqk,khd->qhd", scores_grad, group_keys, preferred_element_type=jnp.float32
                )
                * factor
            )
            keys_grad = (
                keys_grad
                + jnp.einsum(
                    "hqk,qhd->khd", scores_grad, block_queries, preferred_element_type=jnp.float32
                )
                * factor
            )
            values_grad = values_grad + jnp.einsum(
                "hqk,qhd->khd",
                soft.astype(jnp.bfloat16),
                block_grads,
                preferred_element_type=jnp.float32,
            )
        return (jnp.concatenate(pieces, axis=0), keys_grad, values_grad)

    queries_grad, keys_grad, values_grad = lax.map(
        one_group,
        (
            queries.reshape(shape),
            keys.reshape(shape),
            values.reshape(shape),
            totals,
            grad_context.reshape(shape),
            labels,
        ),
    )
    return (
        queries_grad.reshape(queries.shape),
        keys_grad.reshape(queries.shape),
        values_grad.reshape(queries.shape),
    )


def shards(
    inputs,
    block_segment,
    query_weight,
    key_weight,
    value_weight,
    output_weight,
    inner_weight,
    outer_weight,
    first_gain,
    first_bias,
    second_gain,
    second_bias,
    output_cotangent,
):
    width = first_gain.shape[0] * lax.axis_size("narrow")
    tokens = inputs.shape[0]
    factor = HEAD_DIM ** (-0.5)
    cosine, sine, labels = tables(block_segment)
    full_inputs = whole_features(inputs)
    query_full, key_full, value_full, inner_full = (
        lax.all_gather(query_weight, "wide", axis=0, tiled=True),
        lax.all_gather(key_weight, "wide", axis=0, tiled=True),
        lax.all_gather(value_weight, "wide", axis=0, tiled=True),
        lax.all_gather(inner_weight, "wide", axis=0, tiled=True),
    )
    output_full, outer_full = (
        lax.all_gather(output_weight, "wide", axis=1, tiled=True),
        lax.all_gather(outer_weight, "wide", axis=1, tiled=True),
    )
    head_shape = (tokens, query_weight.shape[1] // HEAD_DIM, HEAD_DIM)
    queries = rotate(product(full_inputs, query_full).reshape(head_shape), cosine, sine).astype(
        jnp.bfloat16
    )
    keys = rotate(product(full_inputs, key_full).reshape(head_shape), cosine, sine).astype(
        jnp.bfloat16
    )
    values = product(full_inputs, value_full).astype(jnp.bfloat16).reshape(head_shape)
    context, totals = attention_forward(queries, keys, values, labels, factor)
    context_low = context.reshape(tokens, -1).astype(jnp.bfloat16)
    attended = feature_sums(product(context_low, output_full))
    first, first_normed, first_scale = normalize(
        inputs.astype(jnp.float32) + attended, first_gain, first_bias, width
    )
    first_low = first.astype(jnp.bfloat16)
    feed_rows = whole_features(first_low)
    inner = product(feed_rows, inner_full)
    activated = gelu_value(inner).astype(jnp.bfloat16)
    mixed = feature_sums(product(activated, outer_full))
    second, second_normed, second_scale = normalize(first + mixed, second_gain, second_bias, width)
    layer_output = second.astype(jnp.bfloat16)
    cotangent = output_cotangent.astype(jnp.float32)
    second_gain_grad = jnp.sum(cotangent * second_normed, axis=0)
    second_bias_grad = jnp.sum(cotangent, axis=0)
    grad_second = normalize_back(cotangent, second_normed, second_scale, second_gain, width)
    grad_mixed = grad_second.astype(jnp.bfloat16)
    grad_rows = whole_features(grad_mixed)
    grad_activated = right_transposed(grad_rows, outer_full)
    outer_grad = left_transposed(activated, grad_rows)
    grad_inner = (grad_activated * gelu_slope(inner)).astype(jnp.bfloat16)
    inner_grad = left_transposed(feed_rows, grad_inner)
    grad_first = grad_second + feature_sums(right_transposed(grad_inner, inner_full))
    first_gain_grad = jnp.sum(grad_first * first_normed, axis=0)
    first_bias_grad = jnp.sum(grad_first, axis=0)
    grad_first_sum = normalize_back(grad_first, first_normed, first_scale, first_gain, width)
    attended_rows = whole_features(grad_first_sum.astype(jnp.bfloat16))
    output_grad = left_transposed(context_low, attended_rows)
    grad_context = right_transposed(attended_rows, output_full).astype(jnp.bfloat16)
    queries_grad, keys_grad, values_grad = attention_backward(
        queries, keys, values, totals, grad_context.reshape(head_shape), labels, factor
    )
    queries_grad = rotate_back(queries_grad, cosine, sine).reshape(tokens, -1).astype(jnp.bfloat16)
    keys_grad = rotate_back(keys_grad, cosine, sine).reshape(tokens, -1).astype(jnp.bfloat16)
    values_grad = values_grad.reshape(tokens, -1).astype(jnp.bfloat16)
    query_grad = left_transposed(full_inputs, queries_grad)
    key_grad = left_transposed(full_inputs, keys_grad)
    value_grad = left_transposed(full_inputs, values_grad)
    spread = (
        right_transposed(queries_grad, query_full)
        + right_transposed(keys_grad, key_full)
        + right_transposed(values_grad, value_full)
    )
    input_gradient = (grad_first_sum + feature_sums(spread)).astype(jnp.bfloat16)
    (
        query_total,
        key_total,
        value_total,
        inner_total,
        first_gain_total,
        first_bias_total,
        second_gain_total,
        second_bias_total,
    ) = (
        lax.psum_scatter(query_grad, "wide", scatter_dimension=0, tiled=True),
        lax.psum_scatter(key_grad, "wide", scatter_dimension=0, tiled=True),
        lax.psum_scatter(value_grad, "wide", scatter_dimension=0, tiled=True),
        lax.psum_scatter(inner_grad, "wide", scatter_dimension=0, tiled=True),
        lax.psum_scatter(first_gain_grad, "wide", scatter_dimension=0, tiled=True),
        lax.psum_scatter(first_bias_grad, "wide", scatter_dimension=0, tiled=True),
        lax.psum_scatter(second_gain_grad, "wide", scatter_dimension=0, tiled=True),
        lax.psum_scatter(second_bias_grad, "wide", scatter_dimension=0, tiled=True),
    )
    output_total, outer_total = (
        lax.psum_scatter(output_grad, "wide", scatter_dimension=1, tiled=True),
        lax.psum_scatter(outer_grad, "wide", scatter_dimension=1, tiled=True),
    )
    return (
        layer_output,
        input_gradient,
        query_total,
        key_total,
        value_total,
        output_total,
        inner_total,
        outer_total,
        first_gain_total,
        first_bias_total,
        second_gain_total,
        second_bias_total,
    )


LOW = jnp.bfloat16
WIDE = jnp.float32
MESH = pl.DeviceIdType.MESH
MEGA = 1 << 20
ANY = pl.BlockSpec(memory_space=pl.ANY)


def contract(left, right, left_dim, right_dim):
    return lax.dot_general(
        left, right, (((left_dim,), (right_dim,)), ((), ())), preferred_element_type=WIDE
    )


def place():
    x = lax.axis_index("narrow")
    w = lax.axis_index("wide")
    c = lax.rem(w, 2)
    y = lax.rem(lax.div(w, 2), 2)
    q = lax.div(w, 4)
    return x, w, c, y, q


class Links:
    def __init__(self, depth):
        self.depth = depth
        self.x, self.w, self.c, self.y, self.q = place()
        self.across = (1 - self.x, self.w)
        self.beside = (self.x, self.w + 2 - 4 * self.y)
        self.sibling = (self.x, self.w + 1 - 2 * self.c)
        self.corner = (1 - self.x, self.w + 1 - 2 * self.c)

    def far(self, step):
        return (self.x, lax.rem(self.w + 4 * step, 4 * self.depth))

    def row(self, step):
        return lax.rem(self.q + self.depth - step, self.depth)

    def meet(self, pair_only=False):
        barrier = pltpu.get_barrier_semaphore()
        others = [self.sibling, self.across, self.corner]
        if not pair_only:
            others += [self.beside]
            others += [self.far(step) for step in range(1, self.depth)]
        for other in others:
            pl.semaphore_signal(barrier, 1, device_id=other, device_id_type=MESH)
        pl.semaphore_wait(barrier, len(others))


def remote(source, target, send, recv, device):
    return pltpu.make_async_remote_copy(
        src_ref=source,
        dst_ref=target,
        send_sem=send,
        recv_sem=recv,
        device_id=device,
        device_id_type=MESH,
    )


def gather_marks(depth):
    return 5 * depth + 2


class Gather:
    def __init__(self, links, own, full, cut, whole, send, recv, index, local):
        self.links, self.own, self.full, self.cut = links, own, full, cut
        self.whole, self.local = whole, local
        self.send = lambda k: send.at[index, k]
        self.recv = lambda k: recv.at[index, k]
        self.width = own.shape[-1]

    def slot(self, h, q, y):
        return self.full.at[h, q, y, self.links.c]

    def low(self, ref):
        return ref.at[:, pl.ds(0, self.cut)]

    def high(self, ref):
        return ref.at[:, pl.ds(self.cut, self.width - self.cut)]

    def copy(self, kind, step=0):
        n, d = self.links, self.links.depth
        mine = self.slot(n.x, n.q, n.y)
        column = self.slot(n.x, n.row(step), n.y)
        first = self.own if step == 0 else column
        if kind == "far":
            return self.move(self.own, mine, step - 1, n.far(step))
        if kind == "across":
            return self.move(first, column, d + step, n.across)
        if kind == "beside":
            return self.move(first, column, 2 * d + step, n.beside)
        if kind == "high":
            part = self.high(self.slot(1 - n.x, n.row(step), n.y))
            return self.move(part, part, 3 * d + step, n.beside)
        if kind == "low":
            part = self.low(self.slot(n.x, n.row(step), 1 - n.y))
            return self.move(part, part, 4 * d + step, n.across)
        part = self.full.at[step if self.whole else 1 - n.c, :, :, n.c]
        return self.move(part, part, 5 * d + step, n.sibling)

    def move(self, source, target, mark, device):
        return remote(source, target, self.send(mark), self.recv(mark), device)

    def arrived(self, target, mark):
        self.move(target, target, mark, self.links.sibling).wait_recv()

    def keep(self):
        n = self.links
        return pltpu.make_async_copy(self.own, self.slot(n.x, n.q, n.y), self.local)

    def begin(self):
        self.begin_far()
        self.begin_near()

    def begin_far(self):
        for step in range(1, self.links.depth):
            self.copy("far", step).start()

    def begin_near(self):
        self.keep().start()
        self.copy("across").start()
        self.copy("beside").start()

    def second(self, step):
        n = self.links
        self.arrived(self.slot(n.x, n.row(step), n.y), step - 1)
        self.copy("across", step).start()
        self.copy("beside", step).start()

    def third(self, step):
        n, d = self.links, self.links.depth
        self.arrived(self.slot(1 - n.x, n.row(step), n.y), d + step)
        self.copy("high", step).start()
        self.arrived(self.slot(n.x, n.row(step), 1 - n.y), 2 * d + step)
        self.copy("low", step).start()

    def fourth(self):
        n, d = self.links, self.links.depth
        for step in range(d):
            got = self.slot(1 - n.x, n.row(step), 1 - n.y)
            self.arrived(self.high(got), 3 * d + step)
            self.arrived(self.low(got), 4 * d + step)
        self.keep().wait()
        for h in range(2 if self.whole else 1):
            self.copy("sibling", h).start()

    def finish(self):
        n, d = self.links, self.links.depth
        for h in range(2 if self.whole else 1):
            self.arrived(self.full.at[h if self.whole else n.c, :, :, 1 - n.c], 5 * d + h)

    def halfway(self):
        n, d = self.links, self.links.depth
        self.keep().wait()
        for step in range(d):
            self.arrived(self.slot(1 - n.x, n.row(step), n.y), d + step)
            self.arrived(self.slot(n.x, n.row(step), 1 - n.y), 2 * d + step)
            if step:
                self.copy("far", step).wait_send()
            for kind in ("across", "beside"):
                self.copy(kind, step).wait_send()

    def close(self):
        d = self.links.depth
        for step in range(d):
            if step:
                self.copy("far", step).wait_send()
            for kind in ("across", "beside", "high", "low"):
                self.copy(kind, step).wait_send()
        for h in range(2 if self.whole else 1):
            self.copy("sibling", h).wait_send()


class Finish:
    def __init__(self, links, full, flat, cut, send, recv, base, local):
        self.links, self.full, self.flat, self.cut, self.local = links, full, flat, cut, local
        self.send = lambda k: send.at[base + k]
        self.recv = lambda k: recv.at[base + k]
        self.r, self.width = full.shape[-2:]

    def slot(self, h, q, y, c):
        w = (q * 2 + y) * 2 + c
        return self.flat.at[h, pl.ds(pl.multiple_of(w * self.r, self.r), self.r)]

    def low(self, ref):
        return ref.at[:, pl.ds(0, self.cut)]

    def high(self, ref):
        return ref.at[:, pl.ds(self.cut, self.width - self.cut)]

    def hop(self, kind, step):
        n, d = self.links, self.links.depth
        q = n.row(step)
        h, y, part, mark, device = {
            "high": (1 - n.x, n.y, self.high, step, n.beside),
            "low": (n.x, 1 - n.y, self.low, d + step, n.across),
        }[kind]
        source, target = part(self.full.at[h, q, y, n.c]), part(self.slot(h, q, y, n.c))
        return remote(source, target, self.send(mark), self.recv(mark), device)

    def spread(self, h, q, y):
        n, d = self.links, self.links.depth
        mark = 2 * d + (h * d + q) * 2 + y
        part = self.slot(h, q, y, n.c)
        return remote(part, part, self.send(mark), self.recv(mark), n.sibling)

    def loads(self):
        n, d = self.links, self.links.depth
        return [
            pltpu.make_async_copy(
                self.full.at[h, q, y, n.c], self.slot(h, q, y, n.c), self.local.at[k * d + q]
            )
            for k, (h, y) in enumerate(((n.x, n.y), (1 - n.x, n.y), (n.x, 1 - n.y)))
            for q in range(d)
        ]

    def everywhere(self, act):
        for h in range(2):
            for q in range(self.links.depth):
                for y in range(2):
                    act(self.spread(h, q, y))

    def begin(self):
        for step in range(self.links.depth):
            self.hop("high", step).start()
            self.hop("low", step).start()
        for item in self.loads():
            item.start()

    def fourth(self):
        n, d = self.links, self.links.depth
        for item in self.loads():
            item.wait()
        for step in range(d):
            got = self.slot(1 - n.x, n.row(step), 1 - n.y, n.c)
            for part, mark in ((self.high(got), step), (self.low(got), d + step)):
                remote(part, part, self.send(mark), self.recv(mark), n.sibling).wait_recv()
        self.everywhere(lambda item: item.start())

    def finish(self):
        n = self.links
        for h in range(2):
            for q in range(n.depth):
                for y in range(2):
                    mark = 2 * n.depth + (h * n.depth + q) * 2 + y
                    got = self.slot(h, q, y, 1 - n.c)
                    remote(got, got, self.send(mark), self.recv(mark), n.sibling).wait_recv()

    def close(self):
        for step in range(self.links.depth):
            self.hop("high", step).wait_send()
            self.hop("low", step).wait_send()
        self.everywhere(lambda item: item.wait_send())


class Share:
    def __init__(self, links, in_ref, rows, note_in, note, gain_in, gain, send, recv, local):
        n = self.links = links
        self.home = n.x == n.c
        s, r = (lambda k: send.at[k]), (lambda k: recv.at[k])
        near, far = rows.at[n.x], rows.at[1 - n.x]
        self.rows_across = lambda: remote(in_ref, near, s(0), r(0), n.across)
        self.rows_beside = lambda: remote(in_ref, near, s(1), r(1), n.sibling)
        self.rows_further = lambda: remote(far, far, s(2), r(2), n.sibling)
        self.note = lambda: remote(note_in, note, s(3), r(3), n.sibling)
        self.gain = lambda: remote(gain_in, gain.at[n.x], s(4), r(4), n.across)
        self.gain_keep = lambda: pltpu.make_async_copy(gain_in, gain.at[n.x], local.at[0])
        self.rows_keep = lambda: pltpu.make_async_copy(in_ref, near, local.at[1])
        self.note_keep = lambda: pltpu.make_async_copy(note_in, note, local.at[2])

    def begin(self):
        @pl.when(self.home)
        def _():
            self.note().start()
            self.rows_beside().start()
            self.rows_keep().start()
            self.note_keep().start()

        @pl.when(jnp.logical_not(self.home))
        def _():
            self.rows_across().start()

    def further(self):
        self.gain().start()
        self.gain_keep().start()

        @pl.when(self.home)
        def _():
            self.rows_across().wait_recv()
            self.rows_further().start()
            self.rows_keep().wait()
            self.note_keep().wait()

        @pl.when(jnp.logical_not(self.home))
        def _():
            self.note().wait_recv()
            self.rows_beside().wait_recv()
            self.rows_further().wait_recv()

        self.gain_keep().wait()

    def finish(self):
        self.gain().wait()

        @pl.when(self.home)
        def _():
            self.note().wait_send()
            self.rows_beside().wait_send()
            self.rows_further().wait_send()

        @pl.when(jnp.logical_not(self.home))
        def _():
            self.rows_across().wait_send()


class Pull:
    def __init__(self, links, source, target, send, recv, base):
        n = self.links = links
        half = source.shape[0] // 2
        self.home = n.x == n.c
        s, r = (lambda k: send.at[base + k]), (lambda k: recv.at[base + k])
        mine, theirs = source.at[pl.ds(n.c * half, half)], source.at[pl.ds((1 - n.c) * half, half)]
        near = target.at[n.x]
        self.beside = lambda: remote(theirs, near, s(0), r(0), n.sibling)
        self.across = lambda: remote(mine, near, s(1), r(1), n.across)
        self.corner = lambda: remote(theirs, near, s(2), r(2), n.corner)

    def begin(self):
        @pl.when(self.home)
        def _():
            self.beside().start()

        @pl.when(jnp.logical_not(self.home))
        def _():
            self.across().start()
            self.corner().start()

    def finish(self):
        @pl.when(self.home)
        def _():
            self.beside().wait_send()
            self.across().wait_recv()

        @pl.when(jnp.logical_not(self.home))
        def _():
            self.across().wait_send()
            self.corner().wait_send()
            self.beside().wait_recv()
            self.corner().wait_recv()


def plus(left, right):
    return (left.astype(WIDE) + right.astype(WIDE)).astype(left.dtype)


def scatter_marks(depth):
    return depth + 5


class Scatter:
    def __init__(self, links, kind, part, cut, bufs, out, send, recv, index, local):
        self.links, self.kind, self.part, self.cut, self.out = links, kind, part, cut, out
        self.held, self.other, self.x1, self.y1, self.x2, self.y2, self.z = bufs
        self.send = lambda k: send.at[index, k]
        self.recv = lambda k: recv.at[index, k]
        self.local = local
        self.rest = self.held.shape[-1] - cut

    def low(self, ref):
        return ref.at[:, :, pl.ds(0, self.cut)]

    def high(self, ref):
        return ref.at[:, :, pl.ds(self.cut, self.rest)]

    def move(self, source, target, mark, device):
        return remote(source, target, self.send(mark), self.recv(mark), device)

    def copy(self, kind, step=0):
        n = self.links
        if kind == "sibling" and self.kind == "join":
            return self.move(self.part.at[:, :, :, 1 - n.c], self.other, 0, n.sibling)
        if kind == "sibling":
            return self.move(self.part.at[:, :, 1 - n.c], self.held.at[n.c], 0, n.sibling)
        if kind == "x1":
            return self.move(self.low(self.held.at[1 - n.x, :, 1 - n.y]), self.x1, 1, n.across)
        if kind == "y1":
            return self.move(self.high(self.held.at[1 - n.x, :, 1 - n.y]), self.y1, 2, n.beside)
        if kind == "y2":
            return self.move(self.held.at[n.x, :, 1 - n.y], self.y2, 3, n.beside)
        if kind == "x2":
            return self.move(self.held.at[1 - n.x, :, n.y], self.x2, 4, n.across)
        q = lax.rem(n.q + step, n.depth)
        return self.move(self.mine(q), self.z.at[step - 1], 4 + step, n.far(step))

    def mine(self, q):
        n = self.links
        return self.held.at[q] if self.kind == "last" else self.held.at[n.x, q, n.y]

    def keep(self):
        n = self.links
        if self.kind in ("held", "last"):
            return pltpu.make_async_copy(self.part, self.held, self.local)
        if self.kind == "join":
            return pltpu.make_async_copy(self.part.at[:, :, :, n.c], self.held, self.local)
        return pltpu.make_async_copy(self.part.at[:, :, n.c], self.held.at[n.c], self.local)

    def arrived(self, target, mark):
        self.move(target, target, mark, self.links.sibling).wait_recv()

    def begin(self):
        self.keep().start()
        if self.kind in ("join", "swap"):
            self.copy("sibling").start()

    def first(self):
        n = self.links
        self.keep().wait()
        if self.kind == "join":
            self.arrived(self.other, 0)
            self.held[...] = plus(self.held[...], self.other[...])
        if self.kind == "swap":
            self.arrived(self.held.at[1 - n.c], 0)
        self.copy("x1").start()
        self.copy("y1").start()

    def second(self):
        n = self.links
        low, high = pl.ds(0, self.cut), pl.ds(self.cut, self.rest)
        self.arrived(self.x1, 1)
        for q in range(n.depth):
            self.held[n.x, q, 1 - n.y, :, low] = plus(
                self.held[n.x, q, 1 - n.y, :, low], self.x1[q]
            )
        self.copy("y2").start()
        self.arrived(self.y1, 2)
        for q in range(n.depth):
            self.held[1 - n.x, q, n.y, :, high] = plus(
                self.held[1 - n.x, q, n.y, :, high], self.y1[q]
            )
        self.copy("x2").start()

    def third(self):
        n = self.links
        if self.kind == "last":
            self.keep().wait()
        else:
            self.arrived(self.y2, 3)
            self.arrived(self.x2, 4)
        for step in range(1, n.depth):
            q = lax.rem(n.q + step, n.depth)
            if self.kind != "last":
                mine = self.mine(q)
                mine[...] = plus(plus(mine[...], self.x2[q]), self.y2[q])
            self.copy("z", step).start()

    def fourth(self):
        n = self.links
        total = self.mine(n.q)[...].astype(WIDE)
        if self.kind != "last":
            total = total + self.x2[n.q].astype(WIDE) + self.y2[n.q].astype(WIDE)
        for step in range(1, n.depth):
            self.arrived(self.z.at[step - 1], 4 + step)
            total = total + self.z[step - 1].astype(WIDE)
        self.out(total)

    def close(self):
        hops = ("x1", "y1", "x2", "y2")
        hops = {"last": (), "held": hops}.get(self.kind, ("sibling",) + hops)
        for kind in hops:
            self.copy(kind).wait_send()
        for step in range(1, self.links.depth):
            self.copy("z", step).wait_send()


def scatter_scratch(depth, r, columns, cut, kind="swap", of=LOW):
    small = (8, 128)
    later = kind == "last"
    return [
        pltpu.VMEM((depth, r, columns) if later else (2, depth, 2, r, columns), of),
        pltpu.VMEM((2, depth, 2, r, columns) if kind == "join" else small, of),
        pltpu.VMEM(small if later else (depth, r, cut), of),
        pltpu.VMEM(small if later else (depth, r, columns - cut), of),
        pltpu.VMEM(small if later else (depth, r, columns), of),
        pltpu.VMEM(small if later else (depth, r, columns), of),
        pltpu.VMEM((depth - 1, r, columns), of),
    ]


class HandOver:
    def __init__(self, links, source, target, send, recv, base, local, bounce=None):
        self.links, self.source, self.target, self.local = links, source, target, local
        self.bounce = bounce
        self.send = lambda k: send.at[base + k]
        self.recv = lambda k: recv.at[base + k]
        self.half = source.shape[1]

    def rows(self, c):
        return self.target.at[pl.ds(c * self.half, self.half)]

    def copies(self):
        n = self.links
        near, far = self.source.at[n.x], self.source.at[1 - n.x]
        mine = self.rows(n.c)
        return (
            pltpu.make_async_copy(near if self.bounce is None else self.bounce, mine, self.local),
            remote(far, mine, self.send(0), self.recv(0), n.across),
            remote(near, mine, self.send(1), self.recv(1), n.sibling),
            remote(far, mine, self.send(2), self.recv(2), n.corner),
        )

    def begin(self):
        n = self.links
        keep, across, sibling, corner = self.copies()

        @pl.when(n.x == n.c)
        def _():
            keep.start()
            across.start()

        @pl.when(n.x != n.c)
        def _():
            sibling.start()
            corner.start()

    def finish(self):
        n = self.links
        keep, across, sibling, corner = self.copies()
        mine, theirs = self.rows(n.c), self.rows(1 - n.c)

        @pl.when(n.x == n.c)
        def _():
            keep.wait()
            across.wait_send()
            remote(theirs, theirs, self.send(1), self.recv(1), n.sibling).wait_recv()

        @pl.when(n.x != n.c)
        def _():
            sibling.wait_send()
            corner.wait_send()
            remote(mine, mine, self.send(0), self.recv(0), n.across).wait_recv()
            remote(theirs, theirs, self.send(2), self.recv(2), n.corner).wait_recv()


def angle_tables():
    rates = THETA ** (-np.arange(HEAD_DIM // 2) / (HEAD_DIM // 2))
    rates = np.tile(rates, 4)[None]
    base = np.arange(BLOCK)[:, None] * rates
    jump = np.arange(SPAN)[:, None] * BLOCK * rates
    base = np.concatenate([np.cos(base), np.sin(base)], axis=0)
    jump = np.concatenate([np.cos(jump), np.sin(jump), np.zeros((2, 128))], axis=0)
    return jnp.asarray(base, WIDE), jnp.asarray(jump, WIDE)


def lanes(rows):
    return lax.broadcasted_iota(jnp.int32, (rows, 128), 1)


def turn_parts(meta, base, jump, block):
    segment = meta[0, block]
    earlier = [(meta[0, other] < segment).astype(jnp.int32) for other in range(SPAN)]
    offset = block - sum(earlier)
    far_cos = jump[pl.ds(offset, 1), :]
    far_sin = jump[pl.ds(SPAN + offset, 1), :]
    near_cos, near_sin = base[0:BLOCK], base[BLOCK : 2 * BLOCK]
    cosine = near_cos * far_cos - near_sin * far_sin
    sine = near_sin * far_cos + near_cos * far_sin
    low = (lanes(BLOCK) % HEAD_DIM) < HEAD_DIM // 2
    return cosine, jnp.where(low, -sine, sine), low


def turn(values, cosine, sine, low):
    swapped = jnp.where(low, pltpu.roll(values, 96, 1), pltpu.roll(values, 32, 1))
    return values * cosine + swapped * sine


def weight_loads(full, h, flat, marks):
    depth, r = full.shape[1], full.shape[4]
    return [
        pltpu.make_async_copy(
            full.at[h, q, y, c], flat.at[pl.ds(k * r, r)], marks.at[k]
        )
        for k, (q, y, c) in enumerate(
            (q, y, c) for q in range(depth) for y in range(2) for c in range(2)
        )
    ]


def forward_kernel(depth, cuts, note_in, in_ref, cot_in, gain1, gain2, gain3, gain4, query, key, value, output,
                   inner, o_own, base, jump,
                   note, gain, cot, rows, q_full, m_full, o_full, all_context, q_out, k_out, v_out,
                   p_ref, r_ref, c_out, q_ref, k_ref, v_ref, c_ref, marks, meta, held, weight, gain_in, q_own, m_own, piece, send, recv, local, extra_send,
                   extra_recv, context_send, context_recv):
    step = pl.program_id(0)
    scale = HEAD_DIM ** (-0.5)
    n = Links(depth)
    half = in_ref.shape[0] // 2
    gathers = [
        Gather(n, own, full, cut, whole, send, recv, k, local.at[k])
        for k, (own, full, cut, whole) in enumerate(
            zip((q_own, m_own, o_own), (q_full, m_full, o_full), cuts, (False, True, True))
        )
    ]
    share = Share(
        n, in_ref, held, note_in, note, gain_in, gain, extra_send, extra_recv, local.at[pl.ds(3, 3)]
    )
    rows_keep = lambda: pltpu.make_async_copy(held, rows, local.at[7])
    pull = Pull(n, cot_in, cot, extra_send, extra_recv, 5)

    def context_copy(p):
        there = c_ref.at[p, pl.ds((1 - n.c) * half, half)]
        return remote(there, all_context.at[n.c, p], context_send.at[p], context_recv.at[p], n.sibling)

    def context_keep(p):
        here = c_ref.at[p, pl.ds(n.c * half, half)]
        return pltpu.make_async_copy(here, all_context.at[n.c, p], local.at[10 + p])

    @pl.when(step == 0)
    def _():
        for k, item in enumerate((gain1, gain2, gain3, gain4)):
            gain_in[k : k + 1] = item[...].reshape(1, -1)
            gain_in[4 + k : 5 + k] = item[...].reshape(1, -1)
        for p in range(3):
            for k, item in enumerate((query, key, value)):
                column = p * 384 + k * 128
                q_own[:, column : column + 128] = item[:, p * 128 : (p + 1) * 128]
        m_own[:, 0 : output.shape[1]] = output[...]
        m_own[:, output.shape[1] :] = inner[...]
        n.meet()
        gathers[0].begin()
        share.begin()
        gathers[1].begin_far()
        gathers[2].begin_far()
        for k in range(1, depth):
            gathers[0].second(k)
        for k in range(depth):
            gathers[0].third(k)
        gathers[1].begin_near()
        gathers[2].begin_near()
        share.further()
        rows_keep().start()
        loads = [pltpu.make_async_copy(note, meta, local.at[8])]
        loads[0].start()
        gathers[0].fourth()
        gathers[0].finish()
        loads += weight_loads(q_full, n.c, weight, piece)
        for item in loads[1:]:
            item.start()
        for item in loads:
            item.wait()

    flush = lambda: [
        pltpu.make_async_copy(source, target, local.at[13 + at])
        for at, (source, target) in enumerate(
            ((q_ref, q_out), (k_ref, k_out), (v_ref, v_out), (c_ref, c_out))
        )
    ]

    def flush_early():
        for item in flush()[:3]:
            item.start()

    hooks = {
        4: [flush_early],
        1: [functools.partial(gathers[1].second, k) for k in range(1, depth)],
        3: [functools.partial(gathers[2].second, k) for k in range(1, depth)],
        7: [functools.partial(gathers[1].third, k) for k in range(depth)] + [pull.begin],
        11: [gathers[1].fourth],
    }
    for at, actions in hooks.items():

        @pl.when(step == at)
        def _():
            for action in actions:
                action()

    @pl.when(step < SPAN)
    def _():
        here = pl.ds(step * BLOCK, BLOCK)
        cosine, sine, low = turn_parts(meta, base, jump, step)
        values = jnp.concatenate([held[0, here], held[1, here]], axis=1)

        for p in range(3):
            made = contract(values, weight[:, p * 384 : p * 384 + 384], 1, 0)
            q_ref[p, here] = (turn(made[:, 0:128], cosine, sine, low) * scale).astype(LOW)
            k_ref[p, here] = turn(made[:, 128:256], cosine, sine, low).astype(LOW)
            v_ref[p, here] = made[:, 256:384].astype(LOW)
        marks[here] = (lanes(BLOCK) == meta[0, step]).astype(WIDE).astype(LOW)

    @pl.when(step >= SPAN)
    def _():
        turn_number = step - SPAN
        p = turn_number // SPAN
        i = turn_number % SPAN
        here = pl.ds(i * BLOCK, BLOCK)
        lane = lanes(BLOCK)
        queries = q_ref[p, here]
        values = v_ref[p]
        keys = jnp.concatenate([k_ref[p], marks[...]], axis=1)
        barred = jnp.where((lane < SPAN) & (lane != meta[0, i]), NEGATIVE, 0.0).astype(LOW)
        outs = []
        scales = []
        for head in range(2):
            chosen = (lane // HEAD_DIM) == head
            ours = jnp.concatenate([jnp.where(chosen, queries, 0).astype(LOW), barred], axis=1)
            scores = contract(ours, keys, 1, 1)
            top = jnp.max(scores, axis=1, keepdims=True)
            raised = jnp.exp(scores - top)
            inverse = 1.0 / jnp.sum(raised, axis=1, keepdims=True)
            soft = raised.astype(LOW)
            p_ref[0, head] = soft
            outs.append(contract(soft, values, 1, 0))
            scales.append(inverse)
        inverse = jnp.where(lane < HEAD_DIM, scales[0], scales[1])
        r_ref[0, here] = inverse
        c_ref[p, here] = (jnp.where(lane < HEAD_DIM, outs[0], outs[1]) * inverse).astype(LOW)

    for p in range(3):

        @pl.when(step == 2 * SPAN - 1 + p * SPAN)
        def _():
            context_copy(p).start()
            context_keep(p).start()

    @pl.when(step == 4 * SPAN - 1)
    def _():
        flush()[3].start()
        gathers[1].finish()
        gathers[2].halfway()
        gathers[0].close()
        gathers[1].close()
        share.finish()
        pull.finish()
        rows_keep().wait()
        for p in range(3):
            context_copy(p).wait()
            context_keep(p).wait()
        for item in flush():
            item.wait()


def forward_call(depth, cuts, note, gains, rows, cot, weights, base, jump):
    length, part = rows.shape
    half = length // 2
    r, hidden = weights[-1].shape
    columns = (3 * part, part + hidden, hidden)
    low = lambda *shape: jax.ShapeDtypeStruct(shape, LOW)
    full = [low(2, depth, 2, 2, r, item) for item in columns]
    trio = low(3, length, 128)
    vmem = pl.BlockSpec(memory_space=pltpu.VMEM)
    marks = pltpu.SemaphoreType.DMA((3, gather_marks(depth)))
    return pl.pallas_call(
        functools.partial(forward_kernel, depth, cuts),
        grid=(SPAN + 3 * SPAN,),
        out_shape=[
            jax.ShapeDtypeStruct(note.shape, note.dtype),
            jax.ShapeDtypeStruct((2, 8, part), WIDE),
            low(2, half, part),
            low(2, length, part),
        ]
        + full
        + [
            low(2, 3, half, 128),
            trio,
            trio,
            trio,
            low(SPAN * 3, 2, BLOCK, length),
            jax.ShapeDtypeStruct((3, length, 128), WIDE),
            trio,
        ],
        in_specs=[ANY] * 3 + [once(item.shape) for item in (*gains, *weights, base, jump)],
        out_specs=[ANY] * 8
        + [ANY] * 3
        + [
            pl.BlockSpec((1, 2, BLOCK, length), lambda s: (jnp.maximum(s - SPAN, 0), 0, 0, 0)),
            pl.BlockSpec((1, length, 128), lambda s: (jnp.maximum(s - SPAN, 0) // SPAN, 0, 0)),
            ANY,
        ],
        scratch_shapes=[pltpu.VMEM((3, length, 128), LOW)] * 4
        + [
            pltpu.VMEM((length, 128), LOW),
            pltpu.SMEM(note.shape, note.dtype),
            pltpu.VMEM((2, length, part), LOW),
            pltpu.VMEM((4 * depth * r, columns[0]), LOW),
            pltpu.VMEM((8, part), WIDE),
            pltpu.VMEM((r, columns[0]), LOW),
            pltpu.VMEM((r, columns[1]), LOW),
            pltpu.SemaphoreType.DMA((4 * depth,)),
            marks,
            marks,
            pltpu.SemaphoreType.DMA((17,)),
            pltpu.SemaphoreType.DMA((8,)),
            pltpu.SemaphoreType.DMA((8,)),
            pltpu.SemaphoreType.DMA((3,)),
            pltpu.SemaphoreType.DMA((3,)),
        ],
        compiler_params=pltpu.CompilerParams(
            collective_id=0, has_side_effects=True, vmem_limit_bytes=60 * MEGA
        ),
        name="attend",
    )(note, rows, cot, *gains, *weights, base, jump)


def norm_of(summed):
    mean = jnp.mean(summed, axis=1, keepdims=True)
    centred = summed - mean
    variance = jnp.mean(centred * centred, axis=1, keepdims=True)
    scale = lax.rsqrt(variance + EPSILON)
    return centred * scale, scale


def norm_back(scaled, normed, scale):
    total = jnp.mean(scaled, axis=1, keepdims=True)
    cross = jnp.mean(scaled * normed, axis=1, keepdims=True)
    return scale * (scaled - total - normed * cross)


HIDDEN = 512


def middle_kernel(depth, cuts, context, rows, gains, cot_in, cot_got, m_full, o_full, lo_out, gfs_ref, sums, grads,
                  o_held, m_held, m_mat, o_mat, act, gi, fl, gm, ga, gc, n1, n2, scales, cot, lo,
                  o_part, m_part, o_other, m_other, ox, oy, ox2, oy2, local, send, recv, load):
    step = pl.program_id(0)
    tile, part = rows.shape[1:]
    half = fl.shape[0]
    tiles = half // tile
    r = o_part.shape[-2]
    pieces = o_mat.shape[2] // HIDDEN
    width = pieces * HIDDEN
    n = Links(depth)
    early = step < 2 * tiles
    turn_of = jnp.where(early, lax.rem(step, tiles), jnp.clip(step - 2 * tiles - 2, 0, tiles - 1))
    here = pl.ds(pl.multiple_of(turn_of * tile, tile), tile)
    cot_raw = lambda: pltpu.make_async_copy(
        cot_in.at[pl.ds(n.c * half, half)], cot.at[n.x], local.at[7]
    )
    cot_near = lambda: pltpu.make_async_copy(cot_got.at[n.x], cot.at[n.x], local.at[7])
    cot_far = lambda: pltpu.make_async_copy(cot_got.at[1 - n.x], cot.at[1 - n.x], local.at[5])
    lo_copy = lambda: pltpu.make_async_copy(lo, lo_out, local.at[8])
    finish = Finish(n, o_full, o_mat, cuts[0], send, recv, 15, load)
    m_load = lambda: pltpu.make_async_copy(m_full, m_mat, local.at[0])

    def grads_keep():
        own = grads.at[:, pl.ds(n.c * half, half)]
        return pltpu.make_async_copy(gc.at[n.c], own, local.at[2])

    def grads_copy():
        own = grads.at[:, pl.ds(n.c * half, half)]
        return remote(gc.at[1 - n.c], own, send.at[4], recv.at[4], n.sibling)

    order = ((0, 1 - n.x), (0, n.x), (1, 1 - n.x), (1, n.x))
    chunks = ((o_part, o_other, ox, oy, o_held), (m_part, m_other, None, None, m_held))

    def part_copy(k):
        chunk, h = order[k]
        source, target = chunks[chunk][:2]
        return remote(
            source.at[h, :, :, 1 - n.c], target.at[h], send.at[k], recv.at[k], n.sibling
        )

    def join(k):
        chunk, h = order[k]
        source, target = chunks[chunk][:2]
        part_copy(k).wait_recv()
        for q in range(depth):
            for y in range(2):
                target[h, q, y] = plus(source[h, q, y, n.c], target[h, q, y])

    def hop(chunk, across):
        target, x1, y1 = chunks[chunk][1:4]
        corner = target.at[1 - n.x, :, 1 - n.y]
        mark = 11 + 2 * chunk + across
        if across:
            part = corner.at[:, :, pl.ds(0, x1.shape[-1])]
            return remote(part, x1, send.at[mark], recv.at[mark], n.across)
        part = corner.at[:, :, pl.ds(x1.shape[-1], y1.shape[-1])]
        return remote(part, y1, send.at[mark], recv.at[mark], n.beside)

    def land(chunk):
        target, x1, y1, held = chunks[chunk][1:5]
        low, high = pl.ds(0, x1.shape[-1]), pl.ds(x1.shape[-1], y1.shape[-1])
        hop(chunk, True).wait_recv()
        hop(chunk, False).wait_recv()
        for q in range(depth):
            target[n.x, q, 1 - n.y, :, low] = plus(target[n.x, q, 1 - n.y, :, low], x1[q])
            target[1 - n.x, q, n.y, :, high] = plus(target[1 - n.x, q, n.y, :, high], y1[q])

    def hop2(across):
        mark = 13 + across
        if across:
            part = o_other.at[1 - n.x, :, n.y]
            return remote(part, ox2, send.at[mark], recv.at[mark], n.across)
        part = o_other.at[n.x, :, 1 - n.y]
        return remote(part, oy2, send.at[mark], recv.at[mark], n.beside)

    def land2():
        hop2(True).wait_recv()
        hop2(False).wait_recv()
        for q in range(depth):
            ox2[q] = plus(plus(o_other[n.x, q, n.y], ox2[q]), oy2[q])

    def held_copy(chunk):
        source, target = ((ox2, o_held), (m_other, m_held))[chunk]
        return pltpu.make_async_copy(source, target, local.at[3 + chunk])

    @pl.when(step == 0)
    def _():
        m_load().start()
        n.meet()
        finish.begin()
        cot_far().start()

        @pl.when(n.x == n.c)
        def _():
            cot_raw().start()

        @pl.when(n.x != n.c)
        def _():
            cot_near().start()

        m_load().wait()

    @pl.when(step < tiles)
    def _():
        whole = jnp.concatenate([gains[0], gains[1]], axis=1)
        gain1, bias1, gain2, bias2 = (whole[k : k + 1, :] for k in range(4))
        summed = jnp.concatenate([rows[0], rows[1]], axis=1).astype(WIDE)
        for h in range(2):
            seen = jnp.concatenate([context[h, p, here] for p in range(3)], axis=1)
            summed = summed + contract(seen, m_mat[h, :, 0:part], 1, 1)
        normed1, scale1 = norm_of(summed)
        n1[here] = normed1
        scales[here, 0:1] = scale1
        first = normed1 * gain1 + bias1
        first_low = first.astype(LOW)
        fl[here] = first_low
        for h in range(2):
            for j in range(pieces):
                lo_end = part + j * HIDDEN
                there = slice(h * width + j * HIDDEN, h * width + (j + 1) * HIDDEN)
                inner = contract(first_low, m_mat[h, :, lo_end : lo_end + HIDDEN], 1, 0)
                share = 0.5 * (1.0 + lax.erf(inner * ROOT_HALF))
                slope = share + inner * jnp.exp(-0.5 * inner * inner) * INVERSE_ROOT
                gi[here, there] = slope.astype(LOW)
                act[here, there] = (inner * share).astype(LOW)

    @pl.when(step == tiles)
    def _():
        finish.fourth()
        cot_far().wait()
        cot_near().wait()
        finish.finish()

    @pl.when((step >= tiles) & (step < 2 * tiles))
    def _():
        whole = jnp.concatenate([gains[0], gains[1]], axis=1)
        gain1, bias1, gain2, bias2 = (whole[k : k + 1, :] for k in range(4))
        mixed = n1[here] * gain1 + bias1
        for h in range(2):
            mixed = mixed + contract(act[here, h * width : (h + 1) * width], o_mat[h], 1, 1)
        normed2, scale2 = norm_of(mixed)
        result = (normed2 * gain2 + bias2).astype(LOW)
        for h in range(2):
            lo[h, here] = result[:, h * part : (h + 1) * part]
        cotangent = jnp.concatenate([cot[0, here], cot[1, here]], axis=1).astype(WIDE)
        second_gain = jnp.sum(cotangent * normed2, axis=0, keepdims=True)
        second_bias = jnp.sum(cotangent, axis=0, keepdims=True)
        grad_second = norm_back(cotangent * gain2, normed2, scale2)
        grad_mixed = grad_second.astype(LOW)
        gm[here] = grad_mixed
        n2[here] = grad_second
        found = jnp.concatenate([second_gain, second_bias], axis=0)

        @pl.when(step == tiles)
        def _():
            sums[2:4] = found

        @pl.when(step > tiles)
        def _():
            sums[2:4] += found

    @pl.when((step >= 2 * tiles + 2) & (step < 3 * tiles + 2))
    def _():
        whole = jnp.concatenate([gains[0], gains[1]], axis=1)
        gain1 = whole[0:1, :]
        normed1, scale1 = n1[here], scales[here, 0:1]
        grad_mixed = gm[here]
        for h in range(2):
            for j in range(pieces):
                there = slice(h * width + j * HIDDEN, h * width + (j + 1) * HIDDEN)
                raised = contract(grad_mixed, o_mat[h, :, j * HIDDEN : (j + 1) * HIDDEN], 1, 0)
                gi[here, there] = (raised * gi[here, there].astype(WIDE)).astype(LOW)
        grad_first = n2[here]
        for h in range(2):
            grad_first = grad_first + contract(
                gi[here, h * width : (h + 1) * width], m_mat[h, :, part : part + width], 1, 1
            )
        first_gain = jnp.sum(grad_first * normed1, axis=0, keepdims=True)
        first_bias = jnp.sum(grad_first, axis=0, keepdims=True)
        grad_sum = norm_back(grad_first * gain1, normed1, scale1)
        gfs_ref[...] = grad_sum
        grad_attended = grad_sum.astype(LOW)
        ga[here] = grad_attended
        for h in range(2):
            made = contract(grad_attended, m_mat[h, :, 0:part], 1, 0).astype(LOW)
            for p in range(3):
                gc[h, p, here] = made[:, p * 128 : (p + 1) * 128]
        found = jnp.concatenate([first_gain, first_bias], axis=0)

        @pl.when(step == 2 * tiles + 2)
        def _():
            sums[0:2] = found

        @pl.when(step > 2 * tiles + 2)
        def _():
            sums[0:2] += found

    @pl.when(step == 2 * tiles + 3)
    def _():
        join(1)
        land(0)
        hop2(True).start()
        hop2(False).start()
        lo_copy().start()

    @pl.when(step == 3 * tiles + 1)
    def _():
        grads_keep().start()
        grads_copy().start()

    def put(target, h, row, column, values):
        shards = values.shape[0] // r
        for k in range(shards):
            w = row // r + k
            target[h, w // 4, (w // 2) % 2, w % 2, :, column : column + values.shape[1]] = values[
                k * r : (k + 1) * r
            ]

    for k in range(4):

        @pl.when(step == (2 * tiles + k if k < 2 else 3 * tiles + k))
        def _():
            chunk, h = order[k]
            target = chunks[chunk][0]
            for row in range(0, 2 * part, part):
                for j in range(pieces):
                    start = pl.multiple_of(h * width + j * HIDDEN, HIDDEN)
                    there = pl.ds(start, HIDDEN)
                    if chunk == 0:
                        made = contract(gm[:, row : row + part], act[:, there], 0, 0)
                        put(target, h, row, j * HIDDEN, made.astype(LOW))
                    else:
                        made = contract(fl[:, row : row + part], gi[:, there], 0, 0)
                        put(target, h, row, part + j * HIDDEN, made.astype(LOW))
                if chunk == 1:
                    seen = jnp.concatenate([context[h, p] for p in range(3)], axis=1)
                    made = contract(ga[:, row : row + part], seen, 0, 0)
                    put(target, h, row, 0, made.astype(LOW))
            part_copy(k).start()
            if k == 1:
                join(0)
                hop(0, True).start()
                hop(0, False).start()
            if k == 3:
                join(2)
                join(3)
                held_copy(1).start()
                land2()
                held_copy(0).start()
                grads_keep().wait()
                grads_copy().wait()
                for item in range(4):
                    part_copy(item).wait_send()
                hop(0, True).wait_send()
                hop(0, False).wait_send()
                hop2(True).wait_send()
                hop2(False).wait_send()
                held_copy(0).wait()
                held_copy(1).wait()
                lo_copy().wait()
                finish.close()


def once(shape):
    zeros = (0,) * len(shape)
    return pl.BlockSpec(shape, lambda *_: zeros, pipeline_mode=pl.Buffered(1))


def middle_call(depth, cuts, context, rows, cot_in, cot, m_full, o_full, gains):
    tile = 256
    half, part = cot.shape[1:]
    tiles = half // tile
    width = 2 * part
    hidden = 2 * o_full.shape[-1]
    r = width // (4 * depth)
    columns = (o_full.shape[-1], m_full.shape[2])
    low = lambda *shape: jax.ShapeDtypeStruct(shape, LOW)
    held = [(2, depth, 2, r, item) for item in columns]
    last = lambda i: jnp.minimum(i, tiles - 1)
    later = lambda i: jnp.clip(i - 2 * tiles - 2, 0, tiles - 1)
    c = lambda: lax.rem(lax.axis_index("wide"), 2)
    return pl.pallas_call(
        functools.partial(middle_kernel, depth, cuts),
        grid=(3 * tiles + 4,),
        out_shape=[
            low(2, half, part),
            jax.ShapeDtypeStruct((half, width), WIDE),
            jax.ShapeDtypeStruct((4, width), WIDE),
            low(3, 2 * half, 128),
        ]
        + [low(depth, r, columns[0]), low(*held[1])],
        in_specs=[
            once((2, 3, half, 128)),
            pl.BlockSpec((2, tile, part), lambda i: (0, c() * tiles + last(i), 0)),
            once(gains.shape),
            ANY,
            ANY,
            ANY,
            ANY,
        ],
        out_specs=[
            ANY,
            pl.BlockSpec((tile, width), lambda i: (later(i), 0)),
            pl.BlockSpec((4, width), lambda i: (0, 0)),
            ANY,
            ANY,
            ANY,
        ],
        scratch_shapes=[
            pltpu.VMEM(m_full.shape, LOW),
            pltpu.VMEM((2, width, columns[0]), LOW),
            pltpu.VMEM((half, hidden), LOW),
            pltpu.VMEM((half, hidden), LOW),
            pltpu.VMEM((half, width), LOW),
            pltpu.VMEM((half, width), LOW),
            pltpu.VMEM((half, width), LOW),
            pltpu.VMEM((2, 3, half, 128), LOW),
            pltpu.VMEM((half, width), WIDE),
            pltpu.VMEM((half, width), WIDE),
            pltpu.VMEM((half, 2), WIDE),
            pltpu.VMEM((2, half, part), LOW),
            pltpu.VMEM((2, half, part), LOW),
        ]
        + [pltpu.VMEM((2, depth, 2, 2, r, item), LOW) for item in columns]
        + [pltpu.VMEM(item, LOW) for item in held]
        + [
            pltpu.VMEM((depth, r, item), LOW)
            for item in (cuts[0], columns[0] - cuts[0], columns[0], columns[0])
        ]
        + [
            pltpu.SemaphoreType.DMA((9,)),
            pltpu.SemaphoreType.DMA((15 + 6 * depth,)),
            pltpu.SemaphoreType.DMA((15 + 6 * depth,)),
            pltpu.SemaphoreType.DMA((3 * depth,)),
        ],
        compiler_params=pltpu.CompilerParams(
            collective_id=1, has_side_effects=True, vmem_limit_bytes=62 * MEGA
        ),
        name="middle",
    )(context, rows, gains, cot_in, cot, m_full, o_full)


def backward_kernel(depth, cuts, meta, base, jump, soft, grads, context, inverse, q_ref, k_ref, v_ref,
                    rows_in, kept_in, q_full, lo_in, o_in, m_in, t_in, lo_out, dx_out, o_out, m_out,
                    i_out, q_out, k_out, v_out, t_out, *scratch):
    ones, keys_sum, values_sum, made, weight, q_part, dx_own, dx_give, dx_other = scratch[:9]
    rows, kept, bounce = scratch[-3:]
    bufs = [scratch[9 + 7 * k : 16 + 7 * k] for k in range(6)]
    piece, send, recv, local, extra_send, extra_recv = scratch[51:-3]
    step = pl.program_id(0)
    p = step // SPAN
    i = step % SPAN
    length = q_ref.shape[1]
    scale = HEAD_DIM ** (-0.5)
    lane = lanes(BLOCK)
    here = pl.ds(i * BLOCK, BLOCK)
    n = Links(depth)
    r = o_in.shape[-2]
    half, width = kept.shape
    part = width // 2
    kinds = ("last", "held", "swap", "swap", "swap", "join")
    parts = (o_in, m_in) + tuple(q_part.at[k] for k in range(3)) + (t_in,)

    def put_pair(p, total):
        for k, item in enumerate((q_out, k_out, v_out)):
            item[:, p * 128 : (p + 1) * 128] = total[:, k * 128 : (k + 1) * 128]

    def put_whole(target, total):
        target[...] = total

    def put_inner(total):
        m_out[...] = total[:, 0:part]
        i_out[...] = total[:, part:]

    outs = [functools.partial(put_whole, o_out), put_inner]
    outs += [functools.partial(put_pair, k) for k in range(3)]
    outs += [functools.partial(put_whole, t_out)]
    every = [
        Scatter(n, kind, item, cut, buf, out, send, recv, k, local.at[k])
        for k, (kind, item, cut, buf, out) in enumerate(zip(kinds, parts, cuts, bufs, outs))
    ]
    outer, inner, pair0, pair1, pair2, small = every
    dx_over = HandOver(n, dx_own, dx_out, extra_send, extra_recv, 0, local.at[6])
    rows_load = lambda: pltpu.make_async_copy(rows_in, rows, local.at[7])
    kept_load = lambda: pltpu.make_async_copy(kept_in, kept, local.at[8])
    lo_load = lambda: pltpu.make_async_copy(lo_in.at[n.x], bounce, local.at[9])
    lo_over = HandOver(n, lo_in, lo_out, extra_send, extra_recv, 4, local.at[10], bounce)
    dx_swap = lambda: remote(dx_give, dx_other, extra_send.at[3], extra_recv.at[3], n.sibling)

    @pl.when(step == 0)
    def _():
        ones[...] = (lanes(length) < 2).astype(WIDE).astype(LOW)
        for item in weight_loads(q_full, n.c, weight, piece):
            item.start()
        inner.begin()
        outer.begin()
        rows_load().start()
        kept_load().start()
        lo_load().start()
        n.meet()
        small.begin()
        small.first()
        inner.first()
        outer.third()
        for item in weight_loads(q_full, n.c, weight, piece):
            item.wait()


    def lo_begin():
        lo_load().wait()
        lo_over.begin()

    hooks = {1: [small.second], 2: [lambda: rows_load().wait(), lo_begin], 3: [inner.second], 4: [outer.fourth, pair0.first], 6: [small.third, pair1.first], 8: [inner.third, pair0.second, pair0.third, pair1.second]}
    for at, actions in hooks.items():

        @pl.when(step == at)
        def _():
            for action in actions:
                action()

    grad = grads[0, here].astype(WIDE)
    turned = grad * inverse[0, here]
    both = turned * context[0, here].astype(WIDE)
    turned_low = turned.astype(LOW)
    queries = q_ref[0, here]
    keys = k_ref[0]
    values = jnp.concatenate([v_ref[0], ones[...]], axis=1)
    turned_flip = jnp.transpose(turned).astype(LOW)
    queries_flip = jnp.transpose(queries.astype(WIDE)).astype(LOW)
    found = []
    for head in range(2):
        chosen = (lane // HEAD_DIM) == head
        centre = -jnp.sum(jnp.where(chosen, both, 0.0), axis=1, keepdims=True)
        coarse = centre.astype(LOW).astype(WIDE)
        fine = jnp.where(lane == 0, coarse, jnp.where(lane == 1, centre - coarse, 0.0))
        ours = jnp.concatenate(
            [jnp.where(chosen, turned_low, 0).astype(LOW), fine.astype(LOW)], axis=1
        )
        raised = soft[0, head]
        scores = (contract(ours, values, 1, 1) * raised.astype(WIDE)).astype(LOW)
        found.append(contract(scores, keys, 1, 0))
        mine = slice(head * HEAD_DIM, (head + 1) * HEAD_DIM)
        values_add = contract(turned_flip[mine], raised, 1, 0)
        keys_add = contract(queries_flip[mine], scores, 1, 0)

        @pl.when(i == 0)
        def _():
            values_sum[mine] = values_add
            keys_sum[mine] = keys_add

        @pl.when(i > 0)
        def _():
            values_sum[mine] += values_add
            keys_sum[mine] += keys_add

    cosine, sine, low = turn_parts(meta, base, jump, i)
    grad_queries = jnp.where(lane < HEAD_DIM, found[0], found[1]) * scale
    made[p, here, 0:128] = turn(grad_queries, cosine, -sine, low).astype(LOW)

    @pl.when(i == SPAN - 1)
    def _():
        grad_keys = jnp.transpose(keys_sum[...])
        grad_values = jnp.transpose(values_sum[...])
        for b in range(SPAN):
            there = slice(b * BLOCK, (b + 1) * BLOCK)
            cosine, sine, low = turn_parts(meta, base, jump, b)
            made[p, there, 128:256] = turn(grad_keys[there], cosine, -sine, low).astype(LOW)
        made[p, :, 256:384] = grad_values.astype(LOW)
        for h in range(2):
            found = contract(rows[h], made[p], 0, 0).astype(LOW)
            for k in range(part // r):
                w = h * (part // r) + k
                q_part[p, w // 4, (w // 2) % 2, w % 2] = found[k * r : (k + 1) * r]

    for k in range(3):

        @pl.when(step == k * SPAN + SPAN - 1)
        def _():
            every[2 + k].begin()

    @pl.when(step == 3 * SPAN - 1)
    def _():
        kept_load().wait()
        for own in (False, True):
            there = pl.ds((n.c if own else 1 - n.c) * half, half)
            gained = kept[...] if own else jnp.zeros(kept.shape, WIDE)
            for k in range(3):
                gained = gained + contract(
                    made[k, there], weight[:, k * 384 : k * 384 + 384], 1, 1
                )
            target = dx_own if own else dx_give
            for h in range(2):
                target[h] = gained[:, h * part : (h + 1) * part].astype(LOW)
            if own:
                pair2.second()
            else:
                dx_swap().start()
                pair2.first()
        dx_swap().wait_recv()
        for h in range(2):
            dx_own[h] = plus(dx_own[h], dx_other[h])
        dx_over.begin()
        pair1.third()
        pair2.third()
        small.fourth()
        inner.fourth()
        pair0.fourth()
        pair1.fourth()
        pair2.fourth()
        for item in every:
            item.close()
        dx_swap().wait_send()
        lo_over.finish()
        dx_over.finish()


def backward_call(depth, cuts, meta, base, jump, soft, grads, context, inverse, q, k, v, rows, kept,
                  q_full, lo, o_held, m_held, t_part):
    length = q.shape[1]
    half, width = kept.shape
    part = width // 2
    r = o_held.shape[-2]
    trio = pl.BlockSpec((1, length, 128), lambda s: (s // SPAN, 0, 0))
    low = lambda *shape: jax.ShapeDtypeStruct(shape, LOW)
    widths = (o_held.shape[-1], m_held.shape[-1])
    shape = lambda *item: jax.ShapeDtypeStruct(item, WIDE)
    outs = [shape(r, widths[0]), shape(r, part), shape(r, widths[1] - part)]
    outs += [shape(r, part)] * 3 + [shape(*t_part.shape[-2:])]
    scratch = [
        pltpu.VMEM((length, 128), LOW),
        pltpu.VMEM((128, length), WIDE),
        pltpu.VMEM((128, length), WIDE),
        pltpu.VMEM((3, length, 384), LOW),
        pltpu.VMEM((width, 3 * 384), LOW),
        pltpu.VMEM((3, depth, 2, 2, r, 384), LOW),
        pltpu.VMEM((2, half, part), LOW),
        pltpu.VMEM((2, half, part), LOW),
        pltpu.VMEM((2, half, part), LOW),
    ]
    for at, columns in enumerate(widths + (384,) * 3):
        scratch += scatter_scratch(depth, r, columns, cuts[at], ("last", "held", "swap")[min(at, 2)])
    scratch += scatter_scratch(depth, t_part.shape[-2], t_part.shape[-1], cuts[5], "join", WIDE)
    marks = pltpu.SemaphoreType.DMA((6, scatter_marks(depth)))
    return pl.pallas_call(
        functools.partial(backward_kernel, depth, cuts),
        grid=(3 * SPAN,),
        out_shape=[low(2 * half, part)] * 2 + outs,
        in_specs=[
            pl.BlockSpec(memory_space=pltpu.SMEM),
            once(base.shape),
            once(jump.shape),
            pl.BlockSpec((1, 2, BLOCK, length), lambda s: (s, 0, 0, 0)),
            trio,
            trio,
            trio,
            trio,
            trio,
            trio,
        ]
        + [ANY] * 7,
        out_specs=[ANY] * 2 + [once(item.shape) for item in outs],
        scratch_shapes=scratch
        + [
            pltpu.SemaphoreType.DMA((4 * depth,)),
            marks,
            marks,
            pltpu.SemaphoreType.DMA((11,)),
            pltpu.SemaphoreType.DMA((7,)),
            pltpu.SemaphoreType.DMA((7,)),
            pltpu.VMEM(rows.shape, LOW),
            pltpu.VMEM(kept.shape, WIDE),
            pltpu.VMEM((half, part), LOW),
        ],
        compiler_params=pltpu.CompilerParams(
            collective_id=2, has_side_effects=True, vmem_limit_bytes=63 * MEGA
        ),
        name="attend_back",
    )(meta, base, jump, soft, grads, context, inverse, q, k, v, rows, kept, q_full, lo, o_held, m_held, t_part)


def owned(
    inputs,
    block_segment,
    query_weight,
    key_weight,
    value_weight,
    output_weight,
    inner_weight,
    outer_weight,
    first_gain,
    first_bias,
    second_gain,
    second_bias,
    output_cotangent,
):
    wide = lax.axis_size("wide")
    depth = wide // 4
    r = query_weight.shape[0]
    part = query_weight.shape[1]
    length = inputs.shape[0]
    half = length // 2
    x, w, c, _, _ = place()
    pairs = part // 128
    meta = jnp.pad(block_segment[None], ((0, 0), (0, 128 - SPAN)))
    hidden = inner_weight.shape[1]
    widths = [3 * part, part + hidden, hidden]
    cuts = [(item // 384) * 128 for item in widths]
    cuts[0] = 128
    gains = [first_gain, first_bias, second_gain, second_bias]
    weights = [query_weight, key_weight, value_weight, output_weight.T, inner_weight, outer_weight.T]
    base, jump = angle_tables()
    found = forward_call(
        depth, cuts, meta, gains, inputs, output_cotangent, weights, base, jump
    )
    meta, gains, cot, rows, q_full, m_full, o_full, pairs_context, q, k, v, soft, inverse, context = found
    lo, kept, sums, grads, o_held, m_held = middle_call(
        depth,
        [cuts[2], cuts[1]],
        pairs_context,
        rows,
        output_cotangent,
        cot,
        m_full.reshape(2, 2 * part, widths[1]),
        o_full,
        gains,
    )
    few = 2 * part // (2 * wide)
    spots = jnp.moveaxis(sums.reshape(2, 2, 2, wide, few), (2, 3), (0, 1))
    spots = jnp.pad(jnp.moveaxis(spots, 2, 3), ((0, 0), (0, 0), (0, 6), (0, 0), (0, 128 - few)))
    spots = spots.reshape(2, depth, 2, 2, 8, 256)
    layer_output, input_gradient, o_sum, m_sum, i_sum, q_sum, k_sum, v_sum, found = backward_call(
        depth,
        [(item // 384) * 128 for item in (widths[2], widths[1])] + [128] * 4,
        meta,
        base,
        jump,
        soft,
        grads,
        context,
        inverse,
        q,
        k,
        v,
        rows,
        kept,
        q_full,
        lo,
        o_held,
        m_held,
        spots,
    )
    return (
        layer_output,
        input_gradient,
        q_sum,
        k_sum,
        v_sum,
        m_sum.T,
        i_sum,
        o_sum.T,
        found[0, 0:few],
        found[1, 0:few],
        found[0, 128 : 128 + few],
        found[1, 128 : 128 + few],
    )


def program(*arrays):
    rows = arrays[2].shape[0]
    whole = rows % 16 == 0 and lax.axis_size("narrow") == 2 and lax.axis_size("wide") % 4 == 0
    return owned(*arrays) if whole else shards(*arrays)


def solution(mesh):
    placed = (
        P("wide", "narrow"),
        P("wide"),
        P("wide", "narrow"),
        P("wide", "narrow"),
        P("wide", "narrow"),
        P("narrow", "wide"),
        P("wide", "narrow"),
        P("narrow", "wide"),
        P("narrow"),
        P("narrow"),
        P("narrow"),
        P("narrow"),
        P("wide", "narrow"),
    )
    return jax.shard_map(
        program,
        mesh=mesh,
        in_specs=placed,
        out_specs=(
            P("wide", "narrow"),
            P("wide", "narrow"),
            P("wide", "narrow"),
            P("wide", "narrow"),
            P("wide", "narrow"),
            P("narrow", "wide"),
            P("wide", "narrow"),
            P("narrow", "wide"),
            P(("narrow", "wide")),
            P(("narrow", "wide")),
            P(("narrow", "wide")),
            P(("narrow", "wide")),
        ),
        check_vma=False,
    )
```
